32 devices in a mesh: band: 16 (over z, y, core), helper: 2 (over x).
Axes of the slice: x: 2, y: 2, z: 4, core: 2. Of those that a mesh axis runs over, the one named last changes fastest.
Arguments:
- node_latent: bfloat16 [2048, 256], P(('band', 'helper')), may hold values from -6 to 6
- edge_latent: bfloat16 [32768, 256], P(('band', 'helper')), may hold values from -6 to 6
- grad_out_node: bfloat16 [2048, 256], P(('band', 'helper')), may hold values from -6 to 6
- grad_out_edge: bfloat16 [32768, 256], P(('band', 'helper')), may hold values from -6 to 6
- senders: int32 [32768], P(('band', 'helper')), may hold values from 0 to 191
- receivers: int32 [32768], P(('band', 'helper')), may hold values from 0 to 127, as said below
- band_edges: int32 [16], replicated, may hold values from 2 to 16, as said below
- halo_list: int32 [16, 32], P('band'), may hold values from 0 to 127, as said below
- sea_mask: int32 [2048], P(('band', 'helper')), may hold values 0 or 1
- edge_w1: bfloat16 [768, 256], replicated, may hold values from -0.21875 to 0.21875
- edge_b1: float32 [256], replicated, may hold values from -3 to 3
- edge_w2: bfloat16 [256, 256], replicated, may hold values from -0.375 to 0.375
- edge_b2: float32 [256], replicated, may hold values from -3 to 3
- node_w1: bfloat16 [512, 256], replicated, may hold values from -0.25 to 0.25
- node_b1: float32 [256], replicated, may hold values from -3 to 3
- node_w2: bfloat16 [256, 256], replicated, may hold values from -0.375 to 0.375
- node_b2: float32 [256], replicated, may hold values from -3 to 3
Outputs:
- grad_node: float32 [2048, 256], P(('band', 'helper'))
- grad_edge: bfloat16 [32768, 256], P(('band', 'helper'))
- grad_edge_w1: float32 [768, 256], replicated
- grad_edge_b1: float32 [256], replicated
- grad_edge_w2: float32 [256, 256], replicated
- grad_edge_b2: float32 [256], replicated
- grad_node_w1: float32 [512, 256], replicated
- grad_node_b1: float32 [256], replicated
- grad_node_w2: float32 [256, 256], replicated
- grad_node_b2: float32 [256], replicated
The draws below stay inside these ranges and needn't reach their ends.
Inputs may be any that keep to these rules, and one draw needn't show every extreme that they name: In every aligned block of 128 edge rows, all receivers lie in one aligned tile of 64 nodes. `band_edges`: A quarter of the bands, consecutive along the cycle, hold 16 live blocks; every other band holds between 2 and 6. `halo_list`: the 32 entries of a band are distinct.
All inputs are finite; a program needn't handle non-finite values. No bound on the sum of `sea_mask` on one device may be relied on, other than what follows from the above.
Results may differ from the reference program's by a relative error of at most 0.01.
Values may be sent and summed in bfloat16 or wider, within the bound.
No kernel may reach another device: no remote copies, remote signals or barrier semaphores. Data moves between devices by JAX's collectives and lax.ppermute only.
A program may use at most 64 MiB of HBM per device.

```python
import math
import jax
import jax.numpy as jnp
from jax import lax

L = 256
NODE_DEV = 64
EB = 128
RTILE = 64
BLK_DEV = 8
NPB = 128
HALO = 32
NODES = 2048
EDGES = 32768
N_BAND = 16
N_HELPER = 2


def draw_receivers(key, part):
    block_count = EDGES // EB
    tiles = jax.random.randint(jax.random.fold_in(key, 11), (block_count, 1), 0, NPB // RTILE)
    lanes = jax.random.randint(jax.random.fold_in(key, 12), (block_count, EB), 0, RTILE)
    return (tiles * RTILE + lanes).reshape(EDGES).astype(jnp.int32)


def draw_band_edges(key, part):
    capacity = BLK_DEV * N_HELPER
    offset = jax.random.randint(jax.random.fold_in(key, 21), (), 0, N_BAND)
    band_ids = jnp.arange(N_BAND, dtype=jnp.int32)
    coastal = (band_ids - offset) % N_BAND < N_BAND // 4
    others = jax.random.randint(jax.random.fold_in(key, 22), (N_BAND,), capacity // 8, 3 * capacity // 8 + 1)
    return jnp.where(coastal, capacity, others).astype(jnp.int32)


def draw_halo_list(key, part):
    band_keys = jax.random.split(jax.random.fold_in(key, 31), N_BAND)

    def one_band(band_key):
        return jax.random.permutation(band_key, NPB)[:HALO]
    return jax.vmap(one_band)(band_keys).astype(jnp.int32)


def plant(values, stream_key, low, largest):
    longest = values.shape.index(max(values.shape))
    spots = []
    for shift in (0, 1):
        where = [jax.random.randint(jax.random.fold_in(stream_key, axis), (), 0, length) for axis, length in enumerate(values.shape)]
        where[longest] = (where[longest] + shift) % values.shape[longest]
        spots.append(tuple(where))
    return values.at[spots[0]].set(low).at[spots[1]].set(largest)


def level_of(key, dims, shards, smallest, largest):
    gain = 1.0
    for dim, blocks in shards:
        draws = jax.random.uniform(jax.random.fold_in(jax.random.fold_in(key, 6), dim), (blocks,), jnp.float32, smallest / len(shards), largest / len(shards))
        gain = gain * jnp.repeat(jnp.exp(draws), dims[dim] // blocks).reshape((-1,) + (1,) * (len(dims) - 1 - dim))
    return gain


def scatter_about(stream_key, extent, deviation, limit, pieces=(), held_as=jnp.bfloat16):
    loudness = level_of(stream_key, extent, pieces, -0.22, 0.18) if pieces else 1.0
    result = jax.random.normal(stream_key, extent, jnp.float32) * deviation * loudness
    return jnp.minimum(jnp.maximum(result, -limit), limit).astype(held_as)


def setup_inputs(seed: int = 0) -> dict:
    key_list = jax.random.split(jax.random.key(seed), 18)
    return {
        "node_latent": scatter_about(key_list[0], (NODES, L), 1.0, 6.0, ((0, 32),)),
        "edge_latent": scatter_about(key_list[1], (EDGES, L), 1.0, 6.0, ((0, 32),)),
        "grad_out_node": scatter_about(key_list[2], (NODES, L), 1.0, 6.0, ((0, 32),)),
        "grad_out_edge": scatter_about(key_list[3], (EDGES, L), 1.0, 6.0, ((0, 32),)),
        "senders": plant(jax.random.randint(key_list[4], (EDGES,), 0, NPB + 2 * HALO), jax.random.fold_in(key_list[4], 1), 0, (NPB + 2 * HALO) - 1).astype(jnp.int32),
        "receivers": draw_receivers(jax.random.fold_in(key_list[17], 71), 0),
        "band_edges": draw_band_edges(jax.random.fold_in(key_list[17], 71), 0),
        "halo_list": draw_halo_list(jax.random.fold_in(key_list[17], 71), 0),
        "sea_mask": plant((jax.random.randint(key_list[8], (NODES,), 0, 4) < 3).astype(jnp.int32), jax.random.fold_in(key_list[8], 1), 0, 1),
        "edge_w1": scatter_about(key_list[9], (3 * L, L), (3 * L) ** -0.5, 0.21875),
        "edge_b1": scatter_about(key_list[10], (L,), 0.5, 3.0, (), jnp.float32),
        "edge_w2": scatter_about(key_list[11], (L, L), L ** -0.5, 0.375),
        "edge_b2": scatter_about(key_list[12], (L,), 0.5, 3.0, (), jnp.float32),
        "node_w1": scatter_about(key_list[13], (2 * L, L), (2 * L) ** -0.5, 0.25),
        "node_b1": scatter_about(key_list[14], (L,), 0.5, 3.0, (), jnp.float32),
        "node_w2": scatter_about(key_list[15], (L, L), L ** -0.5, 0.375),
        "node_b2": scatter_about(key_list[16], (L,), 0.5, 3.0, (), jnp.float32),
    }


norm_eps = 1e-05

def layer_norm(pre_act):
    row_mean = lax.optimization_barrier(jnp.mean(pre_act, axis=-1, keepdims=True))
    centre = pre_act - row_mean
    inv_dev = lax.rsqrt(lax.optimization_barrier(jnp.mean(centre * centre, axis=-1, keepdims=True)) + norm_eps)
    return (centre * inv_dev, inv_dev)

def norm_back(grad_in, normed, inv_dev):
    return inv_dev * (grad_in - lax.optimization_barrier(jnp.mean(grad_in, axis=-1, keepdims=True)) - normed * lax.optimization_barrier(jnp.mean(grad_in * normed, axis=-1, keepdims=True)))

def silu_slope(pre_act):
    sigmoid_v = jax.nn.sigmoid(pre_act)
    return sigmoid_v * (1.0 + pre_act * (1.0 - sigmoid_v))

def dot_left_t(left_op, right_op):
    return lax.dot_general(left_op, right_op, (((0,), (0,)), ((), ())), preferred_element_type=jnp.float32)

def dot_right_t(left_op, right_op):
    return lax.dot_general(left_op, right_op, (((1,), (1,)), ((), ())), preferred_element_type=jnp.float32)

def mlp_forward(inputs, w_first, b_first, w_second, b_second):
    pre_act = jnp.dot(inputs, w_first, preferred_element_type=jnp.float32) + b_first
    hidden = jax.nn.silu(pre_act).astype(jnp.bfloat16)
    normed, inv_dev = layer_norm(jnp.dot(hidden, w_second, preferred_element_type=jnp.float32) + b_second)
    return (pre_act, hidden, normed, inv_dev)

def mlp_backward(inputs, w_first, w_second, pre_act, hidden, normed, inv_dev, grad_out):
    grad_second = norm_back(grad_out, normed, inv_dev)
    second_b = grad_second.astype(jnp.bfloat16)
    gw_second = dot_left_t(hidden, second_b)
    gb_second = lax.optimization_barrier(jnp.sum(grad_second, axis=0))
    grad_first = dot_right_t(second_b, w_second) * silu_slope(pre_act)
    first_b = grad_first.astype(jnp.bfloat16)
    gw_first = dot_left_t(inputs, first_b)
    gb_first = lax.optimization_barrier(jnp.sum(grad_first, axis=0))
    grad_inputs = dot_right_t(first_b, w_first)
    return (grad_inputs, gw_first, gb_first, gw_second, gb_second)

def reference(node_latent, edge_latent, grad_out_node, grad_out_edge, senders, receivers, band_edges, halo_list, sea_mask, edge_w1, edge_b1, edge_w2, edge_b2, node_w1, node_b1, node_w2, node_b2):
    band_size = NODE_DEV * N_HELPER
    features = L
    per_band = N_HELPER * BLK_DEV * EB
    nodes = node_latent.reshape(N_BAND, band_size, features)

    def pick_rows(band_nodes, halo_ids):
        return band_nodes[halo_ids]
    halo_rows = jax.vmap(pick_rows)(nodes, halo_list)
    lookups = jnp.concatenate([nodes, jnp.roll(halo_rows, 1, axis=0), jnp.roll(halo_rows, -1, axis=0)], axis=1)
    slot_ids = jnp.arange(BLK_DEV, dtype=jnp.int32)[None, :] * N_HELPER + jnp.arange(N_HELPER, dtype=jnp.int32)[:, None]
    alive_mask = (slot_ids[None, :, :] < band_edges[:, None, None]).astype(jnp.float32)
    alive_mask = jnp.broadcast_to(alive_mask[..., None], (N_BAND, N_HELPER, BLK_DEV, EB)).reshape(N_BAND, per_band)

    def one_band(band_item):
        lookup, band_nodes, edge_rows, grad_edges, send_ids, recv_ids, alive, grad_rows, sea_rows = band_item
        inputs = jnp.concatenate([lookup[send_ids], band_nodes[recv_ids], edge_rows], axis=1)
        pre_act, hidden, normed, inv_dev = mlp_forward(inputs, edge_w1, edge_b1, edge_w2, edge_b2)
        message = lax.optimization_barrier(normed.astype(jnp.bfloat16)).astype(jnp.float32) * alive[:, None]
        agg_rows = jax.ops.segment_sum(message, recv_ids, num_segments=band_size)
        node_in = jnp.concatenate([band_nodes, agg_rows.astype(jnp.bfloat16)], axis=1)
        n_pre, n_hidden, n_normed, n_inv = mlp_forward(node_in, node_w1, node_b1, node_w2, node_b2)
        node_seed = sea_rows[:, None].astype(jnp.float32) * grad_rows.astype(jnp.float32)
        node_back = mlp_backward(node_in, node_w1, node_w2, n_pre, n_hidden, n_normed, n_inv, node_seed)
        agg_grad = lax.optimization_barrier(node_back[0][:, features:].astype(jnp.bfloat16))
        msg_grad = (grad_edges.astype(jnp.float32) + agg_grad[recv_ids].astype(jnp.float32)) * alive[:, None]
        edge_back = mlp_backward(inputs, edge_w1, edge_w2, pre_act, hidden, normed, inv_dev, msg_grad)
        grad_inputs = edge_back[0]
        lookup_grad = jnp.zeros((band_size + 2 * HALO, features), jnp.float32)
        lookup_grad = lookup_grad.at[send_ids].add(grad_inputs[:, :features])
        lookup_grad = lookup_grad.at[recv_ids].add(grad_inputs[:, features:2 * features])
        edge_grad = ((grad_edges.astype(jnp.float32) + grad_inputs[:, 2 * features:]) * alive[:, None]).astype(jnp.bfloat16)
        node_grad = grad_rows.astype(jnp.float32) + node_back[0][:, :features]
        return (lookup_grad, edge_grad, node_grad, edge_back[1:], node_back[1:])
    band_items = (lookups, nodes, edge_latent.reshape(N_BAND, per_band, features), grad_out_edge.reshape(N_BAND, per_band, features), senders.reshape(N_BAND, per_band), receivers.reshape(N_BAND, per_band), alive_mask, grad_out_node.reshape(N_BAND, band_size, features), sea_mask.reshape(N_BAND, band_size))
    lookup_grads, edge_grads, node_grads, edge_wgrads, node_wgrads = lax.map(one_band, band_items)
    returned = jnp.roll(lookup_grads[:, band_size:band_size + HALO], -1, axis=0) + jnp.roll(lookup_grads[:, band_size + HALO:], 1, axis=0)
    node_grads = node_grads + lookup_grads[:, :band_size]

    def add_back(band_nodes, halo_ids, extra_rows):
        return band_nodes.at[halo_ids].add(extra_rows)
    node_grads = jax.vmap(add_back)(node_grads, halo_list, returned)
    edge_scale = 1.0 / math.sqrt(EDGES)
    node_scale = 1.0 / math.sqrt(NODES)
    ew = [lax.optimization_barrier(jnp.sum(grad_part, axis=0)) * edge_scale for grad_part in edge_wgrads]
    nw = [lax.optimization_barrier(jnp.sum(grad_part, axis=0)) * node_scale for grad_part in node_wgrads]
    return (node_grads.reshape(NODES, features), edge_grads.reshape(EDGES, features), ew[0], ew[1], ew[2], ew[3], nw[0], nw[1], nw[2], nw[3])
```

```python
import functools
import math

import jax
import jax.numpy as jnp
from jax import lax
from jax.experimental import pallas as pl
from jax.experimental.pallas import tpu as pltpu
from jax.sharding import PartitionSpec as P

EB = 128
LANES = 128
NORM_EPS = 1e-05
BF = jnp.bfloat16
F32 = jnp.float32
AXES = ("band", "helper")
VMEM_LIMIT = 24 * 1024 * 1024


def round_up(size, unit):
    return -(-size // unit) * unit


def dot(left, right):
    return jnp.dot(left, right, preferred_element_type=F32)


def dot_left_t(left, right):
    return lax.dot_general(left, right, (((0,), (0,)), ((), ())), preferred_element_type=F32)


def dot_right_t(left, right):
    return lax.dot_general(left, right, (((1,), (1,)), ((), ())), preferred_element_type=F32)


def normalise(pre):
    centre = pre - jnp.mean(pre, axis=-1, keepdims=True)
    inv = lax.rsqrt(jnp.mean(centre * centre, axis=-1, keepdims=True) + NORM_EPS)
    return centre * inv, inv


def norm_back(grad, normed, inv):
    return inv * (
        grad
        - jnp.mean(grad, axis=-1, keepdims=True)
        - normed * jnp.mean(grad * normed, axis=-1, keepdims=True)
    )


def ids_down_rows(ids_row):
    return jnp.broadcast_to(ids_row, (LANES, LANES)).T


def onehot_rows(ids_cols, width):
    rows = ids_cols[0].shape[0]
    lane = lax.broadcasted_iota(jnp.int32, (rows, LANES), 1)
    tiles = []
    for start in range(0, width, LANES):
        hit = ids_cols[0] == lane + start
        for more in ids_cols[1:]:
            hit = hit | (more == lane + start)
        tiles.append(jnp.where(hit, 1.0, 0.0).astype(BF))
    return jnp.concatenate(tiles, axis=1)


def onehot_cols(ids_rows, height):
    count = ids_rows[0].shape[1]
    down = lax.broadcasted_iota(jnp.int32, (height, count), 0)
    hit = ids_rows[0] == down
    for more in ids_rows[1:]:
        hit = hit | (more == down)
    return jnp.where(hit, 1.0, 0.0).astype(BF)


def call(kernel, out_shape, args, scratch=(), smem=(), flops=0, name=None):
    in_specs = [
        pl.BlockSpec(memory_space=pltpu.SMEM if i in smem else pltpu.VMEM)
        for i in range(len(args))
    ]
    nbytes = sum(a.size * a.dtype.itemsize for a in args)
    nbytes += sum(math.prod(o.shape) * o.dtype.itemsize for o in out_shape)
    return pl.pallas_call(
        kernel,
        out_shape=out_shape,
        in_specs=in_specs,
        out_specs=[pl.BlockSpec(memory_space=pltpu.VMEM)] * len(out_shape),
        scratch_shapes=list(scratch),
        compiler_params=pltpu.CompilerParams(vmem_limit_bytes=VMEM_LIMIT),
        cost_estimate=pl.CostEstimate(flops=flops, bytes_accessed=nbytes, transcendentals=0),
        name=name,
    )(*args)


def sds(rows, cols, dtype):
    return jax.ShapeDtypeStruct((rows, cols), dtype)


class Groups:
    def __init__(self, bands, helpers):
        self.bands = bands
        self.helpers = helpers
        self.core = 2 if bands % 2 == 0 else 1
        rest = bands // self.core
        self.near = 2 if (helpers <= 2 and rest % 2 == 0) else 1
        self.group = self.near * helpers
        far = rest // self.near
        self.far_rounds = []
        stride = self.core * self.near
        while far > 1:
            size = 4 if far % 4 == 0 else 2
            self.far_rounds.append((stride, size))
            stride *= size
            far //= size

    def permute(self, array, move):
        pairs = []
        for band in range(self.bands):
            for helper in range(self.helpers):
                to_band, to_helper = move(band, helper)
                pairs.append((band * self.helpers + helper, to_band * self.helpers + to_helper))
        return lax.ppermute(array, AXES, pairs)

    def core_swap(self, array):
        return self.permute(array, lambda b, h: (b ^ 1, h))

    def helper_swap(self, array, k):
        return self.permute(array, lambda b, h: (b, h ^ k))

    def group_swap(self, array, k):
        near, help_k = divmod(k, self.helpers)
        return self.permute(array, lambda b, h: (b ^ (near * self.core), h ^ help_k))

    def far_swap(self, array, stride, k):
        return self.permute(array, lambda b, h: (b ^ (k * stride), h))

    def ring(self, array, by):
        return self.permute(array, lambda b, h: ((b + by) % self.bands, h))

    def core_id(self):
        return lax.rem(lax.axis_index("band"), self.core)

    def group_id(self):
        near = lax.rem(lax.div(lax.axis_index("band"), self.core), self.near)
        return near * self.helpers + lax.axis_index("helper")


def tree_sum(parts):
    parts = list(parts)
    while len(parts) > 1:
        parts = [parts[i] + parts[i + 1] for i in range(0, len(parts), 2)]
    return parts[0]


def on_device(
    node_latent,
    edge_latent,
    grad_out_node,
    grad_out_edge,
    senders,
    receivers,
    band_edges,
    halo_list,
    sea_mask,
    edge_w1,
    edge_b1,
    edge_w2,
    edge_b2,
    node_w1,
    node_b1,
    node_w2,
    node_b2,
):
    helpers = lax.axis_size("helper")
    bands = lax.axis_size("band")
    groups = Groups(bands, helpers)
    own, feat = node_latent.shape
    band = own * helpers
    halo = halo_list.shape[1]
    edges = edge_latent.shape[0]
    slots = edges // EB
    look = band + 2 * halo
    width = round_up(look + band, LANES)
    chunk = 2 * EB if slots % 2 == 0 else EB
    per_chunk = chunk // EB
    edge_scale = 1.0 / math.sqrt(edges * helpers * bands)
    node_scale = 1.0 / math.sqrt(own * helpers * bands)
    unit = edges * feat * feat * 2

    send_ids = senders.reshape(slots, EB)
    recv_ids = receivers.reshape(slots, EB)

    w1_rows, w2_rows = edge_w1.shape[0], edge_w2.shape[0]
    n1_rows, n2_rows = node_w1.shape[0], node_w2.shape[0]
    at_w2 = w1_rows
    at_n1 = at_w2 + w2_rows
    at_n2 = at_n1 + n1_rows
    at_bias = at_n2 + n2_rows
    pieces = groups.core * groups.group
    piece = round_up(at_bias + 8, 8 * pieces) // pieces
    half = piece * groups.group
    total = half * groups.core

    seed_own = grad_out_node * sea_mask[:, None].astype(BF)
    mine = jnp.concatenate([node_latent, seed_own], axis=0)
    theirs = [groups.helper_swap(mine, k) for k in range(1, helpers)]

    def gather_kernel(halo_ref, *refs):
        parts, (band_ref, seed_ref, out_ref) = refs[:helpers], refs[helpers:]
        me = lax.axis_index("helper")
        for k in range(helpers):
            at = pl.multiple_of((me ^ k) * own, own)
            band_ref[pl.ds(at, own), :] = parts[k][:own, :]
            seed_ref[pl.ds(at, own), :] = parts[k][own:, :]
        pick = onehot_cols([halo_ref[...]], band)
        out_ref[...] = dot_left_t(pick, band_ref[...]).astype(BF)

    band_rows, band_seed, outgoing = call(
        gather_kernel,
        [sds(band, feat, BF), sds(band, feat, BF), sds(halo, feat, BF)],
        [halo_list, mine, *theirs],
        name="band_gather",
    )
    from_prev = groups.ring(outgoing, 1)
    from_next = groups.ring(outgoing, -1)

    def live_of(be_ref, slot):
        count = be_ref[lax.axis_index("band")]
        return slot * helpers + lax.axis_index("helper") < count

    def chunk_live(be_ref, index):
        rows = [
            jnp.broadcast_to(jnp.where(live_of(be_ref, index * per_chunk + j), 1.0, 0.0), (EB, feat))
            for j in range(per_chunk)
        ]
        return jnp.concatenate(rows, axis=0)

    def chunk_ids(ref, index):
        return jnp.concatenate(
            [
                ids_down_rows(ref[pl.ds(index * per_chunk + j, 1), :])
                for j in range(per_chunk)
            ],
            axis=0,
        )

    def chunk_row(ref, index):
        return jnp.concatenate(
            [ref[pl.ds(index * per_chunk + j, 1), :] for j in range(per_chunk)], axis=1
        )

    def forward_kernel(
        be_ref, send_ref, recv_ref, band_ref, prev_ref, next_ref, e_ref, w1_ref, b1_ref,
        w2_ref, b2_ref, hid_ref, slope_ref, norm_ref, inv_ref, agg_ref, table,
    ):
        lookup = jnp.concatenate([band_ref[...], prev_ref[...], next_ref[...]], axis=0)
        proj_s = dot(lookup, w1_ref[:feat, :])
        proj_r = dot(band_ref[...], w1_ref[feat : 2 * feat, :])
        spare = width - look - band
        for at, proj in ((0, proj_s), (look, proj_r)):
            high = proj.astype(BF)
            table[at : at + proj.shape[0], :] = high
            table[width + at : width + at + proj.shape[0], :] = (proj - high.astype(F32)).astype(BF)
        if spare:
            blank = jnp.zeros((spare, feat), BF)
            table[look + band : width, :] = blank
            table[width + look + band :, :] = blank
        table_v = table[...]
        w1e = w1_ref[2 * feat :, :]
        for i in range(edges // chunk):
            rows = pl.ds(i * chunk, chunk)
            pick = onehot_rows([chunk_ids(send_ref, i), chunk_ids(recv_ref, i) + look], width)
            pre = dot(jnp.concatenate([pick, pick], axis=1), table_v)
            pre = pre + dot(e_ref[rows, :], w1e) + b1_ref[...][None, :]
            sig = jax.nn.sigmoid(pre)
            hidden = (pre * sig).astype(BF)
            hid_ref[rows, :] = hidden
            slope_ref[rows, :] = sig * (1.0 + pre * (1.0 - sig))
            normed, inv = normalise(dot(hidden, w2_ref[...]) + b2_ref[...][None, :])
            norm_ref[rows, :] = normed
            inv_ref[rows, :] = inv
            message = (normed * chunk_live(be_ref, i)).astype(BF)
            part = dot(onehot_cols([chunk_row(recv_ref, i)], band), message)
            if i == 0:
                agg_ref[...] = part
            else:
                agg_ref[...] += part

    hidden, slope, normed, inv, agg_part = call(
        forward_kernel,
        [sds(edges, feat, BF), sds(edges, feat, F32), sds(edges, feat, F32), sds(edges, 1, F32),
         sds(band, feat, F32)],
        [band_edges, send_ids, recv_ids, band_rows, from_prev, from_next, edge_latent, edge_w1,
         edge_b1, edge_w2, edge_b2],
        scratch=[pltpu.VMEM((2 * width, feat), BF)],
        smem=(0,),
        flops=6 * unit,
        name="edge_forward",
    )

    agg_parts = [agg_part] + [groups.helper_swap(agg_part, k) for k in range(1, helpers)]

    def backward_kernel(
        be_ref, send_ref, recv_ref, band_ref, prev_ref, next_ref, seed_ref, e_ref, geo_ref,
        hid_ref, slope_ref, norm_ref, inv_ref, w1_ref, w2_ref, nw1_ref, nb1_ref, nw2_ref,
        nb2_ref, *refs,
    ):
        aggs = refs[:helpers]
        edge_ref, keep_ref, give_ref, lg_ref, din_ref, grads, sums = refs[helpers:]
        band_v = band_ref[...]
        agg = tree_sum([a[...] for a in aggs]).astype(BF)
        node_in = jnp.concatenate([band_v, agg], axis=1)
        n_pre = dot(node_in, nw1_ref[...]) + nb1_ref[...][None, :]
        n_sig = jax.nn.sigmoid(n_pre)
        n_hidden = (n_pre * n_sig).astype(BF)
        n_normed, n_inv = normalise(dot(n_hidden, nw2_ref[...]) + nb2_ref[...][None, :])
        n_dz = norm_back(seed_ref[...].astype(F32), n_normed, n_inv)
        n_dzb = n_dz.astype(BF)
        n_dpre = dot_right_t(n_dzb, nw2_ref[...]) * (n_sig * (1.0 + n_pre * (1.0 - n_sig)))
        n_dpreb = n_dpre.astype(BF)
        din_ref[...] = dot_right_t(n_dpreb, nw1_ref[:feat, :])
        agg_grad = dot_right_t(n_dpreb, nw1_ref[feat:, :]).astype(BF)
        share = node_scale / helpers
        grads[at_n1:at_n2, :] = dot_left_t(node_in, n_dpreb) * share
        grads[at_n2:at_bias, :] = dot_left_t(n_hidden, n_dzb) * share
        gb_n1 = jnp.sum(n_dpre, axis=0, keepdims=True) * share
        gb_n2 = jnp.sum(n_dz, axis=0, keepdims=True) * share

        w1e = w1_ref[2 * feat :, :]
        gb_1 = jnp.zeros((1, feat), F32)
        gb_2 = jnp.zeros((1, feat), F32)
        gw_1 = jnp.zeros((feat, feat), F32)
        gw_2 = jnp.zeros((feat, feat), F32)
        for i in range(edges // chunk):
            rows = pl.ds(i * chunk, chunk)
            live = chunk_live(be_ref, i)
            geo = geo_ref[rows, :].astype(F32)
            at_recv = dot(onehot_rows([chunk_ids(recv_ref, i)], round_up(band, LANES)), agg_grad)
            msg_grad = (geo + at_recv) * live
            dz = norm_back(msg_grad, norm_ref[rows, :], inv_ref[rows, :])
            gb_2 = gb_2 + jnp.sum(dz, axis=0, keepdims=True)
            dzb = dz.astype(BF)
            gw_2 = gw_2 + dot_left_t(hid_ref[rows, :], dzb)
            dpre = dot_right_t(dzb, w2_ref[...]) * slope_ref[rows, :]
            gb_1 = gb_1 + jnp.sum(dpre, axis=0, keepdims=True)
            dpreb = dpre.astype(BF)
            gw_1 = gw_1 + dot_left_t(e_ref[rows, :], dpreb)
            edge_ref[rows, :] = ((geo + dot_right_t(dpreb, w1e)) * live).astype(BF)
            place = onehot_cols([chunk_row(send_ref, i), chunk_row(recv_ref, i) + look], look + band)
            part = dot(place, dpreb)
            if i == 0:
                sums[...] = part
            else:
                sums[...] += part
        at_send = sums[:look, :].astype(BF)
        at_recv = sums[look:, :].astype(BF)
        lookup = jnp.concatenate([band_v, prev_ref[...], next_ref[...]], axis=0)
        look_grad = dot_right_t(at_send, w1_ref[:feat, :])
        recv_grad = dot_right_t(at_recv, w1_ref[feat : 2 * feat, :])
        lg_ref[:band, :] = (look_grad[:band, :] + recv_grad).astype(BF)
        lg_ref[band:, :] = look_grad[band:, :].astype(BF)
        grads[:feat, :] = dot_left_t(lookup, at_send) * edge_scale
        grads[feat : 2 * feat, :] = dot_left_t(band_v, at_recv) * edge_scale
        grads[2 * feat : at_w2, :] = gw_1 * edge_scale
        grads[at_w2:at_n1, :] = gw_2 * edge_scale
        bias = jnp.concatenate([gb_1 * edge_scale, gb_2 * edge_scale, gb_n1, gb_n2], axis=0)
        grads[at_bias:, :] = jnp.concatenate(
            [bias, jnp.zeros((total - at_bias - 4, feat), F32)], axis=0
        )
        core = groups.core_id()
        keep_ref[...] = grads[pl.ds(pl.multiple_of(core * half, 8), half), :]
        other = groups.core - 1 - core
        give_ref[...] = grads[pl.ds(pl.multiple_of(other * half, 8), half), :].astype(BF)

    grad_edge, keep, give, look_grad, node_din = call(
        backward_kernel,
        [sds(edges, feat, BF), sds(half, feat, F32), sds(half, feat, BF), sds(look, feat, BF),
         sds(band, feat, F32)],
        [band_edges, send_ids, recv_ids, band_rows, from_prev, from_next, band_seed, edge_latent,
         grad_out_edge, hidden, slope, normed, inv, edge_w1, edge_w2, node_w1, node_b1, node_w2,
         node_b2, *agg_parts],
        scratch=[pltpu.VMEM((total, feat), F32), pltpu.VMEM((look + band, feat), F32)],
        smem=(0,),
        flops=8 * unit,
        name="node_and_edge_backward",
    )

    got = groups.core_swap(give)
    group = groups.group

    def split_kernel(keep_ref, got_ref, lg_ref, own_ref, *refs):
        outs, summed = refs[:-1], refs[-1]
        summed[...] = keep_ref[...] + got_ref[...].astype(F32)
        me = groups.group_id()

        def part(k):
            return summed[pl.ds(pl.multiple_of((me ^ k) * piece, 8), piece), :]

        own_ref[...] = part(0)
        for k in range(1, group):
            if k < helpers:
                outs[k - 1][:look, :] = lg_ref[...]
                outs[k - 1][look:, :] = part(k).astype(BF)
            else:
                outs[k - 1][...] = part(k).astype(BF)

    own_part, *to_group = call(
        split_kernel,
        [sds(piece, feat, F32)]
        + [sds(piece + (look if k < helpers else 0), feat, BF) for k in range(1, group)],
        [keep, got, look_grad],
        scratch=[pltpu.VMEM((half, feat), F32)],
        name="split_for_group",
    )
    from_group = [groups.group_swap(part, k) for k, part in enumerate(to_group, 1)]

    def join_kernel(own_ref, lg_ref, *refs):
        parts, (piece_ref, band_ref, prev_ref, next_ref) = refs[: group - 1], refs[group - 1 :]
        summed = own_ref[...]
        looked = lg_ref[...].astype(F32)
        for k in range(1, group):
            if k < helpers:
                looked = looked + parts[k - 1][:look, :].astype(F32)
                summed = summed + parts[k - 1][look:, :].astype(F32)
            else:
                summed = summed + parts[k - 1][...].astype(F32)
        piece_ref[...] = summed.astype(BF)
        band_ref[...] = looked[:band, :]
        prev_ref[...] = looked[band : band + halo, :].astype(BF)
        next_ref[...] = looked[band + halo :, :].astype(BF)

    piece_sum, band_grad, prev_grad, next_grad = call(
        join_kernel,
        [sds(piece, feat, BF), sds(band, feat, F32), sds(halo, feat, BF), sds(halo, feat, BF)],
        [own_part, look_grad, *from_group],
        name="join_group",
    )

    for stride, size in groups.far_rounds:
        swapped = [piece_sum] + [groups.far_swap(piece_sum, stride, k) for k in range(1, size)]

        def far_kernel(*refs):
            refs[-1][...] = tree_sum([r[...].astype(F32) for r in refs[:-1]]).astype(BF)

        (piece_sum,) = call(far_kernel, [sds(piece, feat, BF)], swapped, name="join_far")
    halo_back = groups.ring(prev_grad, -1)
    halo_forth = groups.ring(next_grad, 1)

    gathered = [piece_sum] + [groups.group_swap(piece_sum, k) for k in range(1, group)]

    def node_kernel(halo_ref, band_ref, din_ref, gon_ref, back_ref, forth_ref, out_ref):
        at = pl.multiple_of(lax.axis_index("helper") * own, own)
        place = onehot_cols([halo_ref[...] - at], own)
        out_ref[...] = (
            band_ref[pl.ds(at, own), :]
            + din_ref[pl.ds(at, own), :]
            + gon_ref[...].astype(F32)
            + dot(place, back_ref[...])
            + dot(place, forth_ref[...])
        )

    (grad_node,) = call(
        node_kernel,
        [sds(own, feat, F32)],
        [halo_list, band_grad, node_din, grad_out_node, halo_back, halo_forth],
        name="node_gradient",
    )

    my_half = jnp.concatenate(gathered, axis=0)
    other_half = groups.core_swap(my_half)

    def final_kernel(my_ref, other_ref, *refs):
        outs, full = refs[:-1], refs[-1]
        core, me = groups.core_id(), groups.group_id()
        for source, which in ((my_ref, core), (other_ref, groups.core - 1 - core)):
            for k in range(group):
                at = pl.multiple_of(which * half + (me ^ k) * piece, 8)
                full[pl.ds(at, piece), :] = source[k * piece : (k + 1) * piece, :].astype(F32)
        w1_out, b1_out, w2_out, b2_out, n1_out, nb1_out, n2_out, nb2_out = outs
        w1_out[...] = full[:at_w2, :]
        w2_out[...] = full[at_w2:at_n1, :]
        n1_out[...] = full[at_n1:at_n2, :]
        n2_out[...] = full[at_n2:at_bias, :]
        for i, out in enumerate((b1_out, b2_out, nb1_out, nb2_out)):
            out[...] = full[at_bias + i, :]

    vec = jax.ShapeDtypeStruct((feat,), F32)
    weight_grads = call(
        final_kernel,
        [sds(w1_rows, feat, F32), vec, sds(w2_rows, feat, F32), vec, sds(n1_rows, feat, F32), vec,
         sds(n2_rows, feat, F32), vec],
        [my_half, other_half],
        scratch=[pltpu.VMEM((total, feat), F32)],
        name="place_weight_gradients",
    )
    return (grad_node, grad_edge, *weight_grads)


def solution(mesh):
    rows = P(AXES, None)
    flat = P(AXES)
    in_specs = (
        rows, rows, rows, rows, flat, flat, P(), P("band", None), flat,
        P(), P(), P(), P(), P(), P(), P(), P(),
    )
    out_specs = (rows, rows) + (P(),) * 8
    return jax.shard_map(
        on_device, mesh=mesh, in_specs=in_specs, out_specs=out_specs, check_vma=False
    )
```

```python
import functools
import math

import jax
import jax.numpy as jnp
from jax import lax
from jax.experimental import pallas as pl
from jax.experimental.pallas import tpu as pltpu
from jax.sharding import PartitionSpec as P

EB = 128
LANES = 128
NORM_EPS = 1e-05
BF = jnp.bfloat16
F32 = jnp.float32
AXES = ("band", "helper")
VMEM_LIMIT = 24 * 1024 * 1024


def round_up(size, unit):
    return -(-size // unit) * unit


def dot(left, right):
    return jnp.dot(left, right, preferred_element_type=F32)


def dot_left_t(left, right):
    return lax.dot_general(left, right, (((0,), (0,)), ((), ())), preferred_element_type=F32)


def dot_right_t(left, right):
    return lax.dot_general(left, right, (((1,), (1,)), ((), ())), preferred_element_type=F32)


def normalise(pre):
    centre = pre - jnp.mean(pre, axis=-1, keepdims=True)
    inv = lax.rsqrt(jnp.mean(centre * centre, axis=-1, keepdims=True) + NORM_EPS)
    return centre * inv, inv


def norm_back(grad, normed, inv):
    return inv * (
        grad
        - jnp.mean(grad, axis=-1, keepdims=True)
        - normed * jnp.mean(grad * normed, axis=-1, keepdims=True)
    )


def ids_down_rows(ids_row):
    return jnp.broadcast_to(ids_row, (LANES, LANES)).T


def onehot_rows(ids_cols, width):
    rows = ids_cols[0].shape[0]
    lane = lax.broadcasted_iota(jnp.int32, (rows, LANES), 1)
    tiles = []
    for start in range(0, width, LANES):
        hit = ids_cols[0] == lane + start
        for more in ids_cols[1:]:
            hit = hit | (more == lane + start)
        tiles.append(jnp.where(hit, 1.0, 0.0).astype(BF))
    return jnp.concatenate(tiles, axis=1)


def onehot_cols(ids_rows, height):
    count = ids_rows[0].shape[1]
    down = lax.broadcasted_iota(jnp.int32, (height, count), 0)
    hit = ids_rows[0] == down
    for more in ids_rows[1:]:
        hit = hit | (more == down)
    return jnp.where(hit, 1.0, 0.0).astype(BF)


def call(kernel, out_shape, args, scratch=(), smem=(), flops=0, name=None):
    in_specs = [
        pl.BlockSpec(memory_space=pltpu.SMEM if i in smem else pltpu.VMEM)
        for i in range(len(args))
    ]
    nbytes = sum(a.size * a.dtype.itemsize for a in args)
    nbytes += sum(math.prod(o.shape) * o.dtype.itemsize for o in out_shape)
    return pl.pallas_call(
        kernel,
        out_shape=out_shape,
        in_specs=in_specs,
        out_specs=[pl.BlockSpec(memory_space=pltpu.VMEM)] * len(out_shape),
        scratch_shapes=list(scratch),
        compiler_params=pltpu.CompilerParams(vmem_limit_bytes=VMEM_LIMIT),
        cost_estimate=pl.CostEstimate(flops=flops, bytes_accessed=nbytes, transcendentals=0),
        name=name,
    )(*args)


def sds(rows, cols, dtype):
    return jax.ShapeDtypeStruct((rows, cols), dtype)


class Groups:
    def __init__(self, bands, helpers):
        self.bands = bands
        self.helpers = helpers
        self.core = 2 if bands % 2 == 0 else 1
        rest = bands // self.core
        self.near = 2 if (helpers <= 2 and rest % 2 == 0) else 1
        self.group = self.near * helpers
        far = rest // self.near
        self.far_rounds = []
        stride = self.core * self.near
        while far > 1:
            size = 4 if far % 4 == 0 else 2
            self.far_rounds.append((stride, size))
            stride *= size
            far //= size

    def permute(self, array, move):
        pairs = []
        for band in range(self.bands):
            for helper in range(self.helpers):
                to_band, to_helper = move(band, helper)
                pairs.append((band * self.helpers + helper, to_band * self.helpers + to_helper))
        return lax.ppermute(array, AXES, pairs)

    def core_swap(self, array):
        return self.permute(array, lambda b, h: (b ^ 1, h))

    def helper_swap(self, array, k):
        return self.permute(array, lambda b, h: (b, h ^ k))

    def group_swap(self, array, k):
        near, help_k = divmod(k, self.helpers)
        return self.permute(array, lambda b, h: (b ^ (near * self.core), h ^ help_k))

    def far_swap(self, array, stride, k):
        return self.permute(array, lambda b, h: (b ^ (k * stride), h))

    def ring(self, array, by):
        return self.permute(array, lambda b, h: ((b + by) % self.bands, h))

    def core_id(self):
        return lax.rem(lax.axis_index("band"), self.core)

    def group_id(self):
        near = lax.rem(lax.div(lax.axis_index("band"), self.core), self.near)
        return near * self.helpers + lax.axis_index("helper")


def tree_sum(parts):
    parts = list(parts)
    while len(parts) > 1:
        parts = [parts[i] + parts[i + 1] for i in range(0, len(parts), 2)]
    return parts[0]


def on_device(
    node_latent,
    edge_latent,
    grad_out_node,
    grad_out_edge,
    senders,
    receivers,
    band_edges,
    halo_list,
    sea_mask,
    edge_w1,
    edge_b1,
    edge_w2,
    edge_b2,
    node_w1,
    node_b1,
    node_w2,
    node_b2,
):
    helpers = lax.axis_size("helper")
    bands = lax.axis_size("band")
    groups = Groups(bands, helpers)
    own, feat = node_latent.shape
    band = own * helpers
    halo = halo_list.shape[1]
    edges = edge_latent.shape[0]
    slots = edges // EB
    look = band + 2 * halo
    width = round_up(look + band, LANES)
    chunk = 2 * EB if slots % 2 == 0 else EB
    per_chunk = chunk // EB
    edge_scale = 1.0 / math.sqrt(edges * helpers * bands)
    node_scale = 1.0 / math.sqrt(own * helpers * bands)
    unit = edges * feat * feat * 2

    send_ids = senders.reshape(slots, EB)
    recv_ids = receivers.reshape(slots, EB)

    group = groups.group
    pieces = groups.core * group
    slices = [edge_w1.shape[0] // pieces, edge_w2.shape[0] // pieces, 8]
    n_slices = [node_w1.shape[0] // pieces, node_w2.shape[0] // pieces]
    e_piece, n_piece = sum(slices), sum(n_slices)
    piece = e_piece + n_piece
    half = piece * group
    starts = [0, slices[0], e_piece, e_piece + n_slices[0]]
    heights = [slices[0], slices[1], n_slices[0], n_slices[1]]
    at_bias = slices[0] + slices[1]

    def chunk_ids(ref, index):
        return jnp.concatenate(
            [
                ids_down_rows(ref[pl.ds(index * per_chunk + j, 1), :])
                for j in range(per_chunk)
            ],
            axis=0,
        )

    def chunk_row(ref, index):
        return jnp.concatenate(
            [ref[pl.ds(index * per_chunk + j, 1), :] for j in range(per_chunk)], axis=1
        )

    def chunk_live(ref, index):
        rows = [
            jnp.broadcast_to(ref[pl.ds(index * per_chunk + j, 1), :], (EB, feat))
            for j in range(per_chunk)
        ]
        return jnp.concatenate(rows, axis=0)

    b_width = round_up(2 * band, LANES)
    h_width = round_up(2 * halo, LANES)
    r_width = round_up(band, LANES)

    theirs = [groups.helper_swap(node_latent, k) for k in range(1, helpers)]

    def gather_kernel(halo_ref, *refs):
        parts, (band_ref, out_ref) = refs[:helpers], refs[helpers:]
        me = lax.axis_index("helper")
        for k in range(helpers):
            at = pl.multiple_of((me ^ k) * own, own)
            band_ref[pl.ds(at, own), :] = parts[k][...]
        pick = onehot_cols([halo_ref[...]], band)
        out_ref[...] = dot_left_t(pick, band_ref[...]).astype(BF)

    band_rows, outgoing = call(
        gather_kernel,
        [sds(band, feat, BF), sds(halo, feat, BF)],
        [halo_list, node_latent, *theirs],
        name="band_gather",
    )
    from_prev = groups.ring(outgoing, 1)
    from_next = groups.ring(outgoing, -1)

    def split_store(table, height, at, proj):
        high = proj.astype(BF)
        table[at : at + proj.shape[0], :] = high
        table[height + at : height + at + proj.shape[0], :] = (proj - high.astype(F32)).astype(BF)

    def local_kernel(
        send_ref, recv_ref, band_ref, e_ref, w1_ref, b1_ref, b2_ref, nb1_ref, nb2_ref, be_ref,
        sea_ref, pre_ref, place_ref, recv_pick_ref, halo_pick_ref, et_ref, bias_ref, live_ref,
        sea_diag_ref, table,
    ):
        for i, ref in enumerate((b1_ref, b2_ref, nb1_ref, nb2_ref)):
            bias_ref[i, :] = ref[...]
        counts = be_ref[...][None, :]
        mine = lax.broadcasted_iota(jnp.int32, counts.shape, 1) == lax.axis_index("band")
        count = jnp.sum(jnp.where(mine, counts, 0), axis=1, keepdims=True)
        slot = lax.broadcasted_iota(jnp.int32, (slots, feat), 0)
        live_ref[...] = jnp.where(
            slot * helpers + lax.axis_index("helper") < count, 1.0, 0.0
        )
        down = lax.broadcasted_iota(jnp.int32, (own, own), 0)
        across = lax.broadcasted_iota(jnp.int32, (own, own), 1)
        sea_diag_ref[...] = jnp.where(
            (down == across) & (sea_ref[...][None, :] != 0), 1.0, 0.0
        ).astype(BF)
        if b_width > 2 * band:
            table[...] = jnp.zeros_like(table)
        for at, rows in ((0, slice(0, feat)), (band, slice(feat, 2 * feat))):
            split_store(table, b_width, at, dot(band_ref[...], w1_ref[rows, :]))
        for i in range(edges // chunk):
            rows = pl.ds(i * chunk, chunk)
            send_cols = chunk_ids(send_ref, i)
            recv_cols = chunk_ids(recv_ref, i)
            halo_pick_ref[rows, :] = onehot_rows([send_cols - band], h_width)
            recv_pick_ref[rows, :] = onehot_rows([recv_cols], r_width)
            place_ref[:, rows] = onehot_cols(
                [chunk_row(send_ref, i), chunk_row(recv_ref, i) + look], look + band
            )
            send_cols = jnp.where(send_cols < band, send_cols, -1)
            pick = onehot_rows([send_cols, recv_cols + band], b_width)
            pre = dot(jnp.concatenate([pick, pick], axis=1), table[...])
            e_rows = e_ref[rows, :]
            pre_ref[rows, :] = pre + dot(e_rows, w1_ref[2 * feat :, :]) + b1_ref[...][None, :]
            et_ref[:, rows] = e_rows.T

    pre_local, place, recv_pick, halo_pick, edge_t, biases, live, sea_diag = call(
        local_kernel,
        [
            sds(edges, feat, F32), sds(look + band, edges, BF), sds(edges, r_width, BF),
            sds(edges, h_width, BF), sds(feat, edges, BF), sds(4, feat, F32),
            sds(slots, feat, F32), sds(own, own, BF),
        ],
        [send_ids, recv_ids, band_rows, edge_latent, edge_w1, edge_b1, edge_b2, node_b1, node_b2,
         band_edges, sea_mask],
        scratch=[pltpu.VMEM((2 * b_width, feat), BF)],
        flops=4 * unit,
        name="edge_local",
    )

    def forward_kernel(
        live_ref, pre_ref, place_ref, halo_pick_ref, prev_ref, next_ref, w1_ref, w2_ref, bias_ref,
        gon_ref, sea_ref, hid_ref, slope_ref, norm_ref, inv_ref, agg, swap_ref, table,
    ):
        if h_width > 2 * halo:
            table[...] = jnp.zeros_like(table)
        halo_rows = jnp.concatenate([prev_ref[...], next_ref[...]], axis=0)
        split_store(table, h_width, 0, dot(halo_rows, w1_ref[...]))
        for i in range(edges // chunk):
            rows = pl.ds(i * chunk, chunk)
            pick = halo_pick_ref[rows, :]
            pre = pre_ref[rows, :] + dot(jnp.concatenate([pick, pick], axis=1), table[...])
            sig = jax.nn.sigmoid(pre)
            hidden = (pre * sig).astype(BF)
            hid_ref[rows, :] = hidden
            slope_ref[rows, :] = sig * (1.0 + pre * (1.0 - sig))
            normed, inv = normalise(dot(hidden, w2_ref[...]) + bias_ref[1:2, :])
            norm_ref[rows, :] = normed
            inv_ref[rows, :] = inv
            message = (normed * chunk_live(live_ref, i)).astype(BF)
            part = dot(place_ref[look:, rows], message)
            if i == 0:
                agg[...] = part
            else:
                agg[...] += part
        swap_ref[:band, :] = agg[...].astype(BF)
        swap_ref[band:, :] = dot(sea_ref[...], gon_ref[...]).astype(BF)

    hidden, slope, normed, inv, agg_own, swap_own = call(
        forward_kernel,
        [sds(edges, feat, BF), sds(edges, feat, F32), sds(edges, feat, F32), sds(edges, 1, F32),
         sds(band, feat, F32), sds(band + own, feat, BF)],
        [live, pre_local, place, halo_pick, from_prev, from_next, edge_w1[:feat], edge_w2,
         biases, grad_out_node, sea_diag],
        scratch=[pltpu.VMEM((2 * h_width, feat), BF)],
        flops=3 * unit,
        name="edge_forward",
    )

    swaps = [swap_own] + [groups.helper_swap(swap_own, k) for k in range(1, helpers)]

    def backward_kernel(
        live_ref, place_ref, recv_pick_ref, band_ref, prev_ref, next_ref, et_ref, geo_ref,
        hid_ref, slope_ref, norm_ref, inv_ref, w1_ref, w2_ref, nw1_ref, nw2_ref, bias_ref,
        agg_ref, *refs,
    ):
        parts = refs[:helpers]
        edge_ref, keep_ref, give_ref, lg_ref, din_ref, grads, sums, seed = refs[helpers:]
        band_v = band_ref[...]
        me = lax.axis_index("helper")
        for k in range(helpers):
            seed[pl.ds(pl.multiple_of((me ^ k) * own, own), own), :] = parts[k][band:, :]
        agg = tree_sum([agg_ref[...]] + [p[:band, :].astype(F32) for p in parts[1:]]).astype(BF)
        node_in = jnp.concatenate([band_v, agg], axis=1)
        n_pre = dot(node_in, nw1_ref[...]) + bias_ref[2:3, :]
        n_sig = jax.nn.sigmoid(n_pre)
        n_hidden = (n_pre * n_sig).astype(BF)
        n_normed, n_inv = normalise(dot(n_hidden, nw2_ref[...]) + bias_ref[3:4, :])
        n_dz = norm_back(seed[...].astype(F32), n_normed, n_inv)
        n_dzb = n_dz.astype(BF)
        n_dpre = dot_right_t(n_dzb, nw2_ref[...]) * (n_sig * (1.0 + n_pre * (1.0 - n_sig)))
        n_dpreb = n_dpre.astype(BF)
        din_ref[...] = dot_right_t(n_dpreb, nw1_ref[:feat, :])
        agg_grad = dot_right_t(n_dpreb, nw1_ref[feat:, :]).astype(BF)

        def put(which, first, value):
            high, row, count = heights[which], 0, value.shape[0]
            while row < count:
                spot, within = divmod(first + row, high)
                take = min(high - within, count - row)
                at = spot * piece + starts[which] + within
                grads[at : at + take, :] = value[row : row + take, :]
                row += take

        put(2, 0, dot_left_t(node_in, n_dpreb) * node_scale)
        put(3, 0, dot_left_t(n_hidden, n_dzb) * node_scale)
        gb_n1 = jnp.sum(n_dpre, axis=0, keepdims=True) * node_scale
        gb_n2 = jnp.sum(n_dz, axis=0, keepdims=True) * node_scale

        w1e = w1_ref[2 * feat :, :]
        gb_1 = jnp.zeros((1, feat), F32)
        gb_2 = jnp.zeros((1, feat), F32)
        gw_1 = jnp.zeros((feat, feat), F32)
        gw_2 = jnp.zeros((feat, feat), F32)
        for i in range(edges // chunk):
            rows = pl.ds(i * chunk, chunk)
            live = chunk_live(live_ref, i)
            geo = geo_ref[rows, :].astype(F32)
            at_recv = dot(recv_pick_ref[rows, :band], agg_grad)
            msg_grad = (geo + at_recv) * live
            dz = norm_back(msg_grad, norm_ref[rows, :], inv_ref[rows, :])
            gb_2 = gb_2 + jnp.sum(dz, axis=0, keepdims=True)
            dzb = dz.astype(BF)
            gw_2 = gw_2 + dot_left_t(hid_ref[rows, :], dzb)
            dpre = dot_right_t(dzb, w2_ref[...]) * slope_ref[rows, :]
            gb_1 = gb_1 + jnp.sum(dpre, axis=0, keepdims=True)
            dpreb = dpre.astype(BF)
            gw_1 = gw_1 + dot(et_ref[:, rows], dpreb)
            edge_ref[rows, :] = ((geo + dot_right_t(dpreb, w1e)) * live).astype(BF)
            part = dot(place_ref[:, rows], dpreb)
            if i == 0:
                sums[...] = part
            else:
                sums[...] += part
        at_send = sums[:look, :].astype(BF)
        at_recv = sums[look:, :].astype(BF)
        lookup = jnp.concatenate([band_v, prev_ref[...], next_ref[...]], axis=0)
        look_grad = dot_right_t(at_send, w1_ref[:feat, :])
        recv_grad = dot_right_t(at_recv, w1_ref[feat : 2 * feat, :])
        lg_ref[:band, :] = (look_grad[:band, :] + recv_grad).astype(BF)
        lg_ref[band:, :] = look_grad[band:, :].astype(BF)
        put(0, 0, dot_left_t(lookup, at_send) * edge_scale)
        put(0, feat, dot_left_t(band_v, at_recv) * edge_scale)
        put(0, 2 * feat, gw_1 * edge_scale)
        put(1, 0, gw_2 * edge_scale)
        share = 1.0 / helpers
        bias = [gb_1 * edge_scale, gb_2 * edge_scale, gb_n1 * share, gb_n2 * share]
        grads[at_bias : at_bias + 8, :] = jnp.concatenate(bias + [jnp.zeros((4, feat), F32)], axis=0)
        for p in range(1, pieces):
            grads[p * piece + at_bias : p * piece + at_bias + 8, :] = jnp.zeros((8, feat), F32)
        core = groups.core_id()
        other = groups.core - 1 - core
        keep_ref[...] = grads[pl.ds(pl.multiple_of(core * half, 8), half), :]
        give_ref[...] = grads[pl.ds(pl.multiple_of(other * half, 8), half), :].astype(BF)

    grad_edge, keep, give, look_grad, node_din = call(
        backward_kernel,
        [sds(edges, feat, BF), sds(half, feat, F32), sds(half, feat, BF), sds(look, feat, BF),
         sds(band, feat, F32)],
        [live, place, recv_pick, band_rows, from_prev, from_next, edge_t, grad_out_edge,
         hidden, slope, normed, inv, edge_w1, edge_w2, node_w1, node_w2, biases, agg_own, *swaps],
        scratch=[pltpu.VMEM((half * groups.core, feat), F32), pltpu.VMEM((look + band, feat), F32),
                 pltpu.VMEM((band, feat), BF)],
        flops=8 * unit,
        name="node_and_edge_backward",
    )

    got = groups.core_swap(give)
    lg_rows = own + 2 * halo

    def swap_rows(k):
        return (lg_rows if k < helpers else 0, e_piece, n_piece if k % helpers == 0 else 0)

    def split_kernel(keep_ref, got_ref, lg_ref, own_ref, *refs):
        outs, summed = refs[:-1], refs[-1]
        summed[...] = keep_ref[...] + got_ref[...].astype(F32)
        me = groups.group_id()
        helper = lax.axis_index("helper")

        def e_part(k):
            return summed[pl.ds(pl.multiple_of((me ^ k) * piece, 8), e_piece), :]

        def n_part(k):
            return summed[pl.ds(pl.multiple_of((me ^ k) * piece + e_piece, 8), n_piece), :]

        own_ref[:e_piece, :] = e_part(0)
        own_ref[e_piece:, :] = n_part(0)
        for k in range(1, group):
            out = outs[k - 1]
            rows = swap_rows(k)
            if rows[0]:
                out[:own, :] = lg_ref[pl.ds(pl.multiple_of((helper ^ k) * own, own), own), :]
                out[own:lg_rows, :] = lg_ref[band:, :]
            out[rows[0] : rows[0] + e_piece, :] = e_part(k).astype(BF)
            if rows[2]:
                out[rows[0] + e_piece :, :] = n_part(k).astype(BF)

    own_part, *to_group = call(
        split_kernel,
        [sds(piece, feat, F32)] + [sds(sum(swap_rows(k)), feat, BF) for k in range(1, group)],
        [keep, got, look_grad],
        scratch=[pltpu.VMEM((half, feat), F32)],
        name="split_for_group",
    )
    from_group = [groups.group_swap(part, k) for k, part in enumerate(to_group, 1)]

    def join_kernel(own_ref, lg_ref, *refs):
        parts, (piece_ref, mine_ref, prev_ref, next_ref) = refs[: group - 1], refs[group - 1 :]
        at = pl.multiple_of(lax.axis_index("helper") * own, own)
        mine = lg_ref[pl.ds(at, own), :].astype(F32)
        halos = lg_ref[band:, :].astype(F32)
        e_sum = own_ref[:e_piece, :]
        n_sum = own_ref[e_piece:, :]
        for k in range(1, group):
            rows = swap_rows(k)
            if rows[0]:
                mine = mine + parts[k - 1][:own, :].astype(F32)
                halos = halos + parts[k - 1][own:lg_rows, :].astype(F32)
            e_sum = e_sum + parts[k - 1][rows[0] : rows[0] + e_piece, :].astype(F32)
            if rows[2]:
                n_sum = n_sum + parts[k - 1][rows[0] + e_piece :, :].astype(F32)
        piece_ref[:e_piece, :] = e_sum.astype(BF)
        piece_ref[e_piece:, :] = n_sum.astype(BF)
        mine_ref[...] = mine
        prev_ref[...] = halos[:halo, :].astype(BF)
        next_ref[...] = halos[halo:, :].astype(BF)

    piece_sum, own_grad, prev_grad, next_grad = call(
        join_kernel,
        [sds(piece, feat, BF), sds(own, feat, F32), sds(halo, feat, BF), sds(halo, feat, BF)],
        [own_part, look_grad, *from_group],
        name="join_group",
    )

    halo_back = groups.ring(prev_grad, -1)
    halo_forth = groups.ring(next_grad, 1)
    halo_sums = None
    for stride, size in groups.far_rounds:
        swapped = [piece_sum] + [groups.far_swap(piece_sum, stride, k) for k in range(1, size)]
        first = halo_sums is None

        def far_kernel(*refs):
            parts, rest = refs[:size], refs[size:]
            rest[-1][...] = tree_sum([r[...].astype(F32) for r in parts]).astype(BF)
            if first:
                halo_ref, back_ref, forth_ref, out_ref, _ = rest
                at = lax.axis_index("helper") * own
                place = onehot_cols([halo_ref[...] - at], own)
                out_ref[...] = dot(place, back_ref[...]) + dot(place, forth_ref[...])

        if first:
            halo_sums, piece_sum = call(
                far_kernel,
                [sds(own, feat, F32), sds(piece, feat, BF)],
                swapped + [halo_list, halo_back, halo_forth],
                name="join_far",
            )
        else:
            (piece_sum,) = call(far_kernel, [sds(piece, feat, BF)], swapped, name="join_far")

    gathered = [piece_sum] + [groups.group_swap(piece_sum, k) for k in range(1, group)]
    vec = jax.ShapeDtypeStruct((feat,), F32)
    out_shape = [
        jax.ShapeDtypeStruct(edge_w1.shape, F32), vec, jax.ShapeDtypeStruct(edge_w2.shape, F32),
        vec, jax.ShapeDtypeStruct(node_w1.shape, F32), vec,
        jax.ShapeDtypeStruct(node_w2.shape, F32), vec,
    ]

    def place_pieces(parts, spots, outs, buf, row, sems):
        copies = []
        for i, (part, spot) in enumerate(zip(parts, spots)):
            buf[i * piece : (i + 1) * piece, :] = part[...].astype(F32)
            for j, (start, high, out) in enumerate(zip(starts, heights, outs[::2])):
                copies.append(
                    pltpu.make_async_copy(
                        buf.at[pl.ds(i * piece + start, high), :],
                        out.at[pl.ds(pl.multiple_of(spot * high, 8), high), :],
                        sems.at[i, j],
                    )
                )
                copies[-1].start()
        for i, spot in enumerate(spots):

            @pl.when(spot == 0)
            def _():
                for j, out in enumerate(outs[1::2]):
                    row[j][...] = buf[i * piece + at_bias + j, :]
                    pltpu.make_async_copy(row[j], out, sems.at[len(parts), j]).start()
                for j, out in enumerate(outs[1::2]):
                    pltpu.make_async_copy(row[j], out, sems.at[len(parts), j]).wait()

        for copy in copies:
            copy.wait()

    def place_call(keys, held, name, node=None):
        count = len(keys)
        parts = [sources[which, k] for which, k in keys]
        extra = [] if node is None else node

        def kernel(*refs):
            part_refs, refs = refs[:count], refs[count:]
            node_refs, refs = refs[: len(extra)], refs[len(extra) + len(held) :]
            if extra:
                node_out, *refs = refs
                halo_ref, mine_ref, din_ref, gon_ref = node_refs
                at = pl.multiple_of(lax.axis_index("helper") * own, own)
                node_out[...] = (
                    halo_ref[...] + mine_ref[...] + din_ref[pl.ds(at, own), :]
                    + gon_ref[...].astype(F32)
                )
            outs, (buf, *row, sems) = refs[:8], refs[8:]
            core, me = groups.core_id(), groups.group_id()
            spots = [
                (groups.core - 1 - core if which else core) * group + (me ^ k) for which, k in keys
            ]
            place_pieces(part_refs, spots, outs, buf, row, sems)

        vmem, hbm = pl.BlockSpec(memory_space=pltpu.VMEM), pl.BlockSpec(memory_space=pl.ANY)
        node_out = [sds(own, feat, F32)] if extra else []
        return pl.pallas_call(
            kernel,
            out_shape=node_out + out_shape,
            in_specs=[vmem] * (count + len(extra)) + [hbm] * len(held),
            out_specs=[vmem] * len(node_out) + [hbm] * 8,
            scratch_shapes=[pltpu.VMEM((count * piece, feat), F32)]
            + [pltpu.VMEM((feat,), F32)] * 4
            + [pltpu.SemaphoreType.DMA((count + 1, 4))],
            input_output_aliases={count + len(extra) + i: i for i in range(len(held))},
            compiler_params=pltpu.CompilerParams(vmem_limit_bytes=VMEM_LIMIT),
            cost_estimate=pl.CostEstimate(
                flops=0, bytes_accessed=6 * count * piece * feat, transcendentals=0
            ),
            name=name,
        )(*parts, *extra, *held)

    sources = {(0, k): part for k, part in enumerate(gathered)}
    sources[1, 0] = groups.core_swap(piece_sum)
    grad_node, *weight_grads = place_call(
        [(0, 0), (1, 0)], [], "place_first", [halo_sums, own_grad, node_din, grad_out_node]
    )
    if group > 1:
        far_one = sources[0, group - 1]
        far_one, *weight_grads = lax.optimization_barrier((far_one, *weight_grads))
        sources[0, group - 1] = far_one
    for k in range(group - 1, 0, -1):
        sources[1, k] = groups.core_swap(sources[0, k])
    last = [(1, 1)] if group > 1 else []
    middle = [(0, k) for k in range(1, group)] + [(1, k) for k in range(2, group)]
    if middle:
        weight_grads = place_call(middle, weight_grads, "place_middle")
    if last:
        weight_grads = place_call(last, weight_grads, "place_last")
    return (grad_node, grad_edge, *weight_grads)


def solution(mesh):
    rows = P(AXES, None)
    flat = P(AXES)
    in_specs = (
        rows, rows, rows, rows, flat, flat, P(), P("band", None), flat,
        P(), P(), P(), P(), P(), P(), P(), P(),
    )
    out_specs = (rows, rows) + (P(),) * 8
    return jax.shard_map(
        on_device, mesh=mesh, in_specs=in_specs, out_specs=out_specs, check_vma=False
    )
```

```python
import functools
import math

import jax
import jax.numpy as jnp
from jax import lax
from jax.experimental import pallas as pl
from jax.experimental.pallas import tpu as pltpu
from jax.sharding import PartitionSpec as P

EB = 128
LANES = 128
NORM_EPS = 1e-05
BF = jnp.bfloat16
F32 = jnp.float32
AXES = ("band", "helper")
VMEM_LIMIT = 24 * 1024 * 1024


def round_up(size, unit):
    return -(-size // unit) * unit


def dot(left, right):
    return jnp.dot(left, right, preferred_element_type=F32)


def dot_left_t(left, right):
    return lax.dot_general(left, right, (((0,), (0,)), ((), ())), preferred_element_type=F32)


def dot_right_t(left, right):
    return lax.dot_general(left, right, (((1,), (1,)), ((), ())), preferred_element_type=F32)


def normalise(pre):
    centre = pre - jnp.mean(pre, axis=-1, keepdims=True)
    inv = lax.rsqrt(jnp.mean(centre * centre, axis=-1, keepdims=True) + NORM_EPS)
    return centre * inv, inv


def norm_back(grad, normed, inv):
    return inv * (
        grad
        - jnp.mean(grad, axis=-1, keepdims=True)
        - normed * jnp.mean(grad * normed, axis=-1, keepdims=True)
    )


def ids_down_rows(ids_row):
    return jnp.broadcast_to(ids_row, (LANES, LANES)).T


def onehot_rows(ids_cols, width):
    rows = ids_cols[0].shape[0]
    lane = lax.broadcasted_iota(jnp.int32, (rows, LANES), 1)
    tiles = []
    for start in range(0, width, LANES):
        hit = ids_cols[0] == lane + start
        for more in ids_cols[1:]:
            hit = hit | (more == lane + start)
        tiles.append(jnp.where(hit, 1.0, 0.0).astype(BF))
    return jnp.concatenate(tiles, axis=1)


def onehot_cols(ids_rows, height):
    count = ids_rows[0].shape[1]
    down = lax.broadcasted_iota(jnp.int32, (height, count), 0)
    hit = ids_rows[0] == down
    for more in ids_rows[1:]:
        hit = hit | (more == down)
    return jnp.where(hit, 1.0, 0.0).astype(BF)


def call(kernel, out_shape, args, scratch=(), hbm_out=(), flops=0, name=None):
    in_specs = [pl.BlockSpec(memory_space=pltpu.VMEM)] * len(args)
    out_specs = [
        pl.BlockSpec(memory_space=pl.ANY if i in hbm_out else pltpu.VMEM)
        for i in range(len(out_shape))
    ]
    nbytes = sum(a.size * a.dtype.itemsize for a in args)
    nbytes += sum(math.prod(o.shape) * o.dtype.itemsize for o in out_shape)
    return pl.pallas_call(
        kernel,
        out_shape=out_shape,
        in_specs=in_specs,
        out_specs=out_specs,
        scratch_shapes=list(scratch),
        compiler_params=pltpu.CompilerParams(vmem_limit_bytes=VMEM_LIMIT),
        cost_estimate=pl.CostEstimate(flops=flops, bytes_accessed=nbytes, transcendentals=0),
        name=name,
    )(*args)


def sds(rows, cols, dtype):
    return jax.ShapeDtypeStruct((rows, cols), dtype)


class Groups:
    def __init__(self, bands, helpers):
        self.bands = bands
        self.helpers = helpers
        self.core = 2 if bands % 2 == 0 else 1
        rest = bands // self.core
        self.near = 2 if (helpers <= 2 and rest % 2 == 0) else 1
        self.group = self.near * helpers
        far = rest // self.near
        self.far_rounds = []
        stride = self.core * self.near
        while far > 1:
            size = 4 if far % 4 == 0 else 2
            self.far_rounds.append((stride, size))
            stride *= size
            far //= size

        self.crossed = (
            self.core == 2 and len(self.far_rounds) == 1 and self.far_rounds[0][1] == self.group
        )

    def permute(self, array, move):
        pairs = []
        for band in range(self.bands):
            for helper in range(self.helpers):
                to_band, to_helper = move(band, helper)
                pairs.append((band * self.helpers + helper, to_band * self.helpers + to_helper))
        return lax.ppermute(array, AXES, pairs)

    def core_swap(self, array):
        return self.permute(array, lambda b, h: (b ^ 1, h))

    def helper_swap(self, array, k):
        return self.permute(array, lambda b, h: (b, h ^ k))

    def near_move(self, band, helper, k):
        near, help_k = divmod(k, self.helpers)
        return band ^ (near * self.core), helper ^ help_k

    def first_swap(self, array, k):
        def move(band, helper):
            if self.crossed and band % 2:
                return band ^ (k * self.far_rounds[0][0]), helper
            return self.near_move(band, helper, k)

        return self.permute(array, move)

    def second_swap(self, array, stride, k):
        def move(band, helper):
            if self.crossed and band % 2:
                return self.near_move(band, helper, k)
            return band ^ (k * stride), helper

        return self.permute(array, move)

    def ring(self, array, by):
        return self.permute(array, lambda b, h: ((b + by) % self.bands, h))

    def core_id(self):
        return lax.rem(lax.axis_index("band"), self.core)

    def first_id(self, core):
        band = lax.axis_index("band")
        near = lax.rem(lax.div(band, self.core), self.near)
        near = near * self.helpers + lax.axis_index("helper")
        if not self.crossed:
            return near
        return jnp.where(core == 1, lax.div(band, self.core * self.near), near)


def tree_sum(parts):
    parts = list(parts)
    while len(parts) > 1:
        parts = [parts[i] + parts[i + 1] for i in range(0, len(parts), 2)]
    return parts[0]


def on_device(
    node_latent,
    edge_latent,
    grad_out_node,
    grad_out_edge,
    senders,
    receivers,
    band_edges,
    halo_list,
    sea_mask,
    edge_w1,
    edge_b1,
    edge_w2,
    edge_b2,
    node_w1,
    node_b1,
    node_w2,
    node_b2,
):
    helpers = lax.axis_size("helper")
    bands = lax.axis_size("band")
    groups = Groups(bands, helpers)
    own, feat = node_latent.shape
    band = own * helpers
    halo = halo_list.shape[1]
    edges = edge_latent.shape[0]
    slots = edges // EB
    look = band + 2 * halo
    width = round_up(look + band, LANES)
    chunk = 2 * EB if slots % 2 == 0 else EB
    per_chunk = chunk // EB
    edge_scale = 1.0 / math.sqrt(edges * helpers * bands)
    node_share = 1.0 / math.sqrt(own * helpers * bands) / helpers
    unit = edges * feat * feat * 2

    send_ids = senders.reshape(slots, EB)
    recv_ids = receivers.reshape(slots, EB)

    group = groups.group
    pieces = groups.core * group
    slices = [edge_w1.shape[0] // pieces, edge_w2.shape[0] // pieces, 8]
    n_slices = [node_w1.shape[0] // pieces, node_w2.shape[0] // pieces]
    e_piece, n_piece = sum(slices), sum(n_slices)
    piece = e_piece + n_piece
    half = piece * group
    starts = [0, slices[0], e_piece, e_piece + n_slices[0]]
    heights = [slices[0], slices[1], n_slices[0], n_slices[1]]
    at_bias = slices[0] + slices[1]

    def chunk_ids(ref, index):
        return jnp.concatenate(
            [
                ids_down_rows(ref[pl.ds(index * per_chunk + j, 1), :])
                for j in range(per_chunk)
            ],
            axis=0,
        )

    def chunk_row(ref, index):
        return jnp.concatenate(
            [ref[pl.ds(index * per_chunk + j, 1), :] for j in range(per_chunk)], axis=1
        )

    def chunk_live(ref, index):
        rows = [
            jnp.broadcast_to(ref[pl.ds(index * per_chunk + j, 1), :], (EB, feat))
            for j in range(per_chunk)
        ]
        return jnp.concatenate(rows, axis=0)

    b_width = round_up(2 * band, LANES)
    h_width = round_up(2 * halo, LANES)
    r_width = round_up(band, LANES)

    theirs = [groups.helper_swap(node_latent, k) for k in range(1, helpers)]

    def gather_kernel(halo_ref, *refs):
        parts, (band_ref, out_ref) = refs[:helpers], refs[helpers:]
        me = lax.axis_index("helper")
        for k in range(helpers):
            at = pl.multiple_of((me ^ k) * own, own)
            band_ref[pl.ds(at, own), :] = parts[k][...]
        pick = onehot_cols([halo_ref[...]], band)
        out_ref[...] = dot_left_t(pick, band_ref[...]).astype(BF)

    band_rows, outgoing = call(
        gather_kernel,
        [sds(band, feat, BF), sds(halo, feat, BF)],
        [halo_list, node_latent, *theirs],
        name="band_gather",
    )
    from_prev = groups.ring(outgoing, 1)
    from_next = groups.ring(outgoing, -1)

    def split_store(table, height, at, proj):
        high = proj.astype(BF)
        table[at : at + proj.shape[0], :] = high
        table[height + at : height + at + proj.shape[0], :] = (proj - high.astype(F32)).astype(BF)

    def local_kernel(
        send_ref, recv_ref, band_ref, e_ref, w1_ref, b1_ref, b2_ref, nb1_ref, nb2_ref, be_ref,
        sea_ref, pre_ref, place_ref, recv_pick_ref, halo_pick_ref, et_ref, bias_ref, live_ref,
        sea_diag_ref, table,
    ):
        for i, ref in enumerate((b1_ref, b2_ref, nb1_ref, nb2_ref)):
            bias_ref[i, :] = ref[...]
        counts = be_ref[...][None, :]
        mine = lax.broadcasted_iota(jnp.int32, counts.shape, 1) == lax.axis_index("band")
        count = jnp.sum(jnp.where(mine, counts, 0), axis=1, keepdims=True)
        slot = lax.broadcasted_iota(jnp.int32, (slots, feat), 0)
        live_ref[...] = jnp.where(
            slot * helpers + lax.axis_index("helper") < count, 1.0, 0.0
        )
        down = lax.broadcasted_iota(jnp.int32, (own, own), 0)
        across = lax.broadcasted_iota(jnp.int32, (own, own), 1)
        sea_diag_ref[...] = jnp.where(
            (down == across) & (sea_ref[...][None, :] != 0), 1.0, 0.0
        ).astype(BF)
        if b_width > 2 * band:
            table[...] = jnp.zeros_like(table)
        for at, rows in ((0, slice(0, feat)), (band, slice(feat, 2 * feat))):
            split_store(table, b_width, at, dot(band_ref[...], w1_ref[rows, :]))
        for i in range(edges // chunk):
            rows = pl.ds(i * chunk, chunk)
            send_cols = chunk_ids(send_ref, i)
            recv_cols = chunk_ids(recv_ref, i)
            halo_pick_ref[rows, :] = onehot_rows([send_cols - band], h_width)
            recv_pick_ref[rows, :] = onehot_rows([recv_cols], r_width)
            place_ref[:, rows] = onehot_cols(
                [chunk_row(send_ref, i), chunk_row(recv_ref, i) + look], look + band
            )
            send_cols = jnp.where(send_cols < band, send_cols, -1)
            pick = onehot_rows([send_cols, recv_cols + band], b_width)
            pre = dot(jnp.concatenate([pick, pick], axis=1), table[...])
            e_rows = e_ref[rows, :]
            pre_ref[rows, :] = pre + dot(e_rows, w1_ref[2 * feat :, :]) + b1_ref[...][None, :]
            et_ref[:, rows] = e_rows.T

    pre_local, place, recv_pick, halo_pick, edge_t, biases, live, sea_diag = call(
        local_kernel,
        [
            sds(edges, feat, F32), sds(look + band, edges, BF), sds(edges, r_width, BF),
            sds(edges, h_width, BF), sds(feat, edges, BF), sds(4, feat, F32),
            sds(slots, feat, F32), sds(own, own, BF),
        ],
        [send_ids, recv_ids, band_rows, edge_latent, edge_w1, edge_b1, edge_b2, node_b1, node_b2,
         band_edges, sea_mask],
        scratch=[pltpu.VMEM((2 * b_width, feat), BF)],
        flops=4 * unit,
        name="edge_local",
    )

    def forward_kernel(
        live_ref, pre_ref, place_ref, halo_pick_ref, prev_ref, next_ref, w1_ref, w2_ref, bias_ref,
        gon_ref, sea_ref, hid_ref, slope_ref, norm_ref, inv_ref, agg, swap_ref, table,
    ):
        if h_width > 2 * halo:
            table[...] = jnp.zeros_like(table)
        halo_rows = jnp.concatenate([prev_ref[...], next_ref[...]], axis=0)
        split_store(table, h_width, 0, dot(halo_rows, w1_ref[...]))
        for i in range(edges // chunk):
            rows = pl.ds(i * chunk, chunk)
            pick = halo_pick_ref[rows, :]
            pre = pre_ref[rows, :] + dot(jnp.concatenate([pick, pick], axis=1), table[...])
            sig = jax.nn.sigmoid(pre)
            hidden = (pre * sig).astype(BF)
            hid_ref[rows, :] = hidden
            slope_ref[rows, :] = sig * (1.0 + pre * (1.0 - sig))
            normed, inv = normalise(dot(hidden, w2_ref[...]) + bias_ref[1:2, :])
            norm_ref[rows, :] = normed
            inv_ref[rows, :] = inv
            message = (normed * chunk_live(live_ref, i)).astype(BF)
            part = dot(place_ref[look:, rows], message)
            if i == 0:
                agg[...] = part
            else:
                agg[...] += part
        swap_ref[:band, :] = agg[...].astype(BF)
        swap_ref[band:, :] = dot(sea_ref[...], gon_ref[...]).astype(BF)

    hidden, slope, normed, inv, agg_own, swap_own = call(
        forward_kernel,
        [sds(edges, feat, BF), sds(edges, feat, F32), sds(edges, feat, F32), sds(edges, 1, F32),
         sds(band, feat, F32), sds(band + own, feat, BF)],
        [live, pre_local, place, halo_pick, from_prev, from_next, edge_w1[:feat], edge_w2,
         biases, grad_out_node, sea_diag],
        scratch=[pltpu.VMEM((2 * h_width, feat), BF)],
        flops=3 * unit,
        name="edge_forward",
    )

    swaps = [swap_own] + [groups.helper_swap(swap_own, k) for k in range(1, helpers)]

    def backward_kernel(
        live_ref, place_ref, recv_pick_ref, band_ref, prev_ref, next_ref, et_ref, geo_ref,
        hid_ref, slope_ref, norm_ref, inv_ref, w1_ref, w2_ref, nw1_ref, nw2_ref, bias_ref,
        agg_ref, *refs,
    ):
        parts = refs[:helpers]
        edge_hbm, keep_ref, give_ref, lg_ref, din_ref, grads, sums, seed, edge_ref, sems = refs[helpers:]
        edge_copies = []
        band_v = band_ref[...]
        me = lax.axis_index("helper")
        for k in range(helpers):
            seed[pl.ds(pl.multiple_of((me ^ k) * own, own), own), :] = parts[k][band:, :]
        agg = tree_sum([agg_ref[...]] + [p[:band, :].astype(F32) for p in parts[1:]]).astype(BF)
        node_in = jnp.concatenate([band_v, agg], axis=1)
        n_pre = dot(node_in, nw1_ref[...]) + bias_ref[2:3, :]
        n_sig = jax.nn.sigmoid(n_pre)
        n_hidden = (n_pre * n_sig).astype(BF)
        n_normed, n_inv = normalise(dot(n_hidden, nw2_ref[...]) + bias_ref[3:4, :])
        n_dz = norm_back(seed[...].astype(F32), n_normed, n_inv)
        n_dzb = n_dz.astype(BF)
        n_dpre = dot_right_t(n_dzb, nw2_ref[...]) * (n_sig * (1.0 + n_pre * (1.0 - n_sig)))
        n_dpreb = n_dpre.astype(BF)
        din_ref[...] = dot_right_t(n_dpreb, nw1_ref[:feat, :])
        agg_grad = dot_right_t(n_dpreb, nw1_ref[feat:, :]).astype(BF)

        def put(which, first, value):
            high, row, count = heights[which], 0, value.shape[0]
            while row < count:
                spot, within = divmod(first + row, high)
                take = min(high - within, count - row)
                at = spot * piece + starts[which] + within
                grads[at : at + take, :] = value[row : row + take, :]
                row += take

        put(2, 0, dot_left_t(node_in, n_dpreb) * node_share)
        put(3, 0, dot_left_t(n_hidden, n_dzb) * node_share)
        gb_n1 = jnp.sum(n_dpre, axis=0, keepdims=True) * node_share
        gb_n2 = jnp.sum(n_dz, axis=0, keepdims=True) * node_share

        w1e = w1_ref[2 * feat :, :]
        gb_1 = jnp.zeros((1, feat), F32)
        gb_2 = jnp.zeros((1, feat), F32)
        gw_1 = jnp.zeros((feat, feat), F32)
        gw_2 = jnp.zeros((feat, feat), F32)
        for i in range(edges // chunk):
            rows = pl.ds(i * chunk, chunk)
            live = chunk_live(live_ref, i)
            geo = geo_ref[rows, :].astype(F32)
            at_recv = dot(recv_pick_ref[rows, :band], agg_grad)
            msg_grad = (geo + at_recv) * live
            dz = norm_back(msg_grad, norm_ref[rows, :], inv_ref[rows, :])
            gb_2 = gb_2 + jnp.sum(dz, axis=0, keepdims=True)
            dzb = dz.astype(BF)
            gw_2 = gw_2 + dot_left_t(hid_ref[rows, :], dzb)
            dpre = dot_right_t(dzb, w2_ref[...]) * slope_ref[rows, :]
            gb_1 = gb_1 + jnp.sum(dpre, axis=0, keepdims=True)
            dpreb = dpre.astype(BF)
            gw_1 = gw_1 + dot(et_ref[:, rows], dpreb)
            edge_ref[rows, :] = ((geo + dot_right_t(dpreb, w1e)) * live).astype(BF)
            edge_copies.append(
                pltpu.make_async_copy(edge_ref.at[rows, :], edge_hbm.at[rows, :], sems.at[i])
            )
            edge_copies[-1].start()
            part = dot(place_ref[:, rows], dpreb)
            if i == 0:
                sums[...] = part
            else:
                sums[...] += part
        at_send = sums[:look, :].astype(BF)
        at_recv = sums[look:, :].astype(BF)
        lookup = jnp.concatenate([band_v, prev_ref[...], next_ref[...]], axis=0)
        look_grad = dot_right_t(at_send, w1_ref[:feat, :])
        recv_grad = dot_right_t(at_recv, w1_ref[feat : 2 * feat, :])
        lg_ref[:band, :] = (look_grad[:band, :] + recv_grad).astype(BF)
        lg_ref[band:, :] = look_grad[band:, :].astype(BF)
        put(0, 0, dot_left_t(lookup, at_send) * edge_scale)
        put(0, feat, dot_left_t(band_v, at_recv) * edge_scale)
        put(0, 2 * feat, gw_1 * edge_scale)
        put(1, 0, gw_2 * edge_scale)
        bias = [gb_1 * edge_scale, gb_2 * edge_scale, gb_n1, gb_n2]
        grads[at_bias : at_bias + 8, :] = jnp.concatenate(bias + [jnp.zeros((4, feat), F32)], axis=0)
        for p in range(1, pieces):
            grads[p * piece + at_bias : p * piece + at_bias + 8, :] = jnp.zeros((8, feat), F32)
        core = groups.core_id()
        other = groups.core - 1 - core
        keep_ref[...] = grads[pl.ds(pl.multiple_of(core * half, 8), half), :]
        give_ref[...] = grads[pl.ds(pl.multiple_of(other * half, 8), half), :].astype(BF)
        for copy in edge_copies:
            copy.wait()

    grad_edge, keep, give, look_grad, node_din = call(
        backward_kernel,
        [sds(edges, feat, BF), sds(half, feat, F32), sds(half, feat, BF), sds(look, feat, BF),
         sds(band, feat, F32)],
        [live, place, recv_pick, band_rows, from_prev, from_next, edge_t, grad_out_edge,
         hidden, slope, normed, inv, edge_w1, edge_w2, node_w1, node_w2, biases, agg_own, *swaps],
        scratch=[pltpu.VMEM((half * groups.core, feat), F32), pltpu.VMEM((look + band, feat), F32),
                 pltpu.VMEM((band, feat), BF), pltpu.VMEM((edges, feat), BF),
                 pltpu.SemaphoreType.DMA((edges // chunk,))],
        hbm_out=(0,),
        flops=8 * unit,
        name="node_and_edge_backward",
    )

    got = groups.core_swap(give)
    look_grads = [look_grad] + [groups.helper_swap(look_grad, k) for k in range(1, helpers)]

    def split_kernel(keep_ref, got_ref, own_ref, *refs):
        outs, summed = refs[:-1], refs[-1]
        summed[...] = keep_ref[...] + got_ref[...].astype(F32)
        me = groups.first_id(groups.core_id())
        own_ref[...] = summed[pl.ds(pl.multiple_of(me * piece, 8), piece), :]
        for k in range(1, group):
            part = summed[pl.ds(pl.multiple_of((me ^ k) * piece, 8), piece), :]
            outs[k - 1][...] = part.astype(BF)

    own_part, *to_group = call(
        split_kernel,
        [sds(piece, feat, F32)] + [sds(piece, feat, BF)] * (group - 1),
        [keep, got],
        scratch=[pltpu.VMEM((half, feat), F32)],
        name="split_for_group",
    )
    from_group = [groups.first_swap(part, k) for k, part in enumerate(to_group, 1)]

    def join_kernel(own_ref, *refs):
        parts, looks = refs[: group - 1], refs[group - 1 : group - 1 + helpers]
        piece_ref, mine_ref, prev_ref, next_ref = refs[group - 1 + helpers :]
        summed = own_ref[...]
        for part in parts:
            summed = summed + part[...].astype(F32)
        piece_ref[...] = summed.astype(BF)
        at = pl.multiple_of(lax.axis_index("helper") * own, own)
        mine_ref[...] = tree_sum([g[pl.ds(at, own), :].astype(F32) for g in looks])
        halos = tree_sum([g[band:, :].astype(F32) for g in looks])
        prev_ref[...] = halos[:halo, :].astype(BF)
        next_ref[...] = halos[halo:, :].astype(BF)

    piece_sum, own_grad, prev_grad, next_grad = call(
        join_kernel,
        [sds(piece, feat, BF), sds(own, feat, F32), sds(halo, feat, BF), sds(halo, feat, BF)],
        [own_part, *from_group, *look_grads],
        name="join_group",
    )

    halo_back = groups.ring(prev_grad, -1)
    halo_forth = groups.ring(next_grad, 1)
    halo_sums = None
    for stride, size in groups.far_rounds:
        swapped = [piece_sum] + [groups.second_swap(piece_sum, stride, k) for k in range(1, size)]
        first = halo_sums is None

        def far_kernel(*refs):
            parts, rest = refs[:size], refs[size:]
            rest[-1][...] = tree_sum([r[...].astype(F32) for r in parts]).astype(BF)
            if first:
                halo_ref, back_ref, forth_ref, out_ref, _ = rest
                at = lax.axis_index("helper") * own
                place = onehot_cols([halo_ref[...] - at], own)
                out_ref[...] = dot(place, back_ref[...]) + dot(place, forth_ref[...])

        if first:
            halo_sums, piece_sum = call(
                far_kernel,
                [sds(own, feat, F32), sds(piece, feat, BF)],
                swapped + [halo_list, halo_back, halo_forth],
                name="join_far",
            )
        else:
            (piece_sum,) = call(far_kernel, [sds(piece, feat, BF)], swapped, name="join_far")

    gathered = [piece_sum] + [groups.first_swap(piece_sum, k) for k in range(1, group)]
    vec = jax.ShapeDtypeStruct((feat,), F32)
    out_shape = [
        jax.ShapeDtypeStruct(edge_w1.shape, F32), vec, jax.ShapeDtypeStruct(edge_w2.shape, F32),
        vec, jax.ShapeDtypeStruct(node_w1.shape, F32), vec,
        jax.ShapeDtypeStruct(node_w2.shape, F32), vec,
    ]

    def place_pieces(parts, spots, outs, buf, row, sems):
        copies = []
        for i, (part, spot) in enumerate(zip(parts, spots)):
            buf[i * piece : (i + 1) * piece, :] = part[...].astype(F32)
            for j, (start, high, out) in enumerate(zip(starts, heights, outs[::2])):
                copies.append(
                    pltpu.make_async_copy(
                        buf.at[pl.ds(i * piece + start, high), :],
                        out.at[pl.ds(pl.multiple_of(spot * high, 8), high), :],
                        sems.at[i, j],
                    )
                )
                copies[-1].start()
        for i, spot in enumerate(spots):

            @pl.when(spot == 0)
            def _():
                for j, out in enumerate(outs[1::2]):
                    row[j][...] = buf[i * piece + at_bias + j, :]
                    pltpu.make_async_copy(row[j], out, sems.at[len(parts), j]).start()
                for j, out in enumerate(outs[1::2]):
                    pltpu.make_async_copy(row[j], out, sems.at[len(parts), j]).wait()

        for copy in copies:
            copy.wait()

    def place_call(keys, held, name, node=None):
        count = len(keys)
        parts = [sources[which, k] for which, k in keys]
        extra = [] if node is None else node

        def kernel(*refs):
            part_refs, refs = refs[:count], refs[count:]
            node_refs, refs = refs[: len(extra)], refs[len(extra) + len(held) :]
            if extra:
                node_out, *refs = refs
                halo_ref, mine_ref, din_ref, gon_ref = node_refs
                at = pl.multiple_of(lax.axis_index("helper") * own, own)
                node_out[...] = (
                    halo_ref[...] + mine_ref[...] + din_ref[pl.ds(at, own), :]
                    + gon_ref[...].astype(F32)
                )
            outs, (buf, *row, sems) = refs[:8], refs[8:]
            spots = []
            for which, k in keys:
                core = groups.core - 1 - groups.core_id() if which else groups.core_id()
                spots.append(core * group + (groups.first_id(core) ^ k))
            place_pieces(part_refs, spots, outs, buf, row, sems)

        vmem, hbm = pl.BlockSpec(memory_space=pltpu.VMEM), pl.BlockSpec(memory_space=pl.ANY)
        node_out = [sds(own, feat, F32)] if extra else []
        return pl.pallas_call(
            kernel,
            out_shape=node_out + out_shape,
            in_specs=[vmem] * (count + len(extra)) + [hbm] * len(held),
            out_specs=[vmem] * len(node_out) + [hbm] * 8,
            scratch_shapes=[pltpu.VMEM((count * piece, feat), F32)]
            + [pltpu.VMEM((feat,), F32)] * 4
            + [pltpu.SemaphoreType.DMA((count + 1, 4))],
            input_output_aliases={count + len(extra) + i: i for i in range(len(held))},
            compiler_params=pltpu.CompilerParams(vmem_limit_bytes=VMEM_LIMIT),
            cost_estimate=pl.CostEstimate(
                flops=0, bytes_accessed=6 * count * piece * feat, transcendentals=0
            ),
            name=name,
        )(*parts, *extra, *held)

    sources = {(0, k): part for k, part in enumerate(gathered)}
    sources[1, 0] = groups.core_swap(piece_sum)
    grad_node, *weight_grads = place_call(
        [(0, 0), (1, 0)], [], "place_first", [halo_sums, own_grad, node_din, grad_out_node]
    )
    tops = range(group - 1, 0, -1)
    for i, k in enumerate(tops):
        if i < 2:
            sources[0, k], *weight_grads = lax.optimization_barrier(
                (sources[0, k], *weight_grads)
            )
        sources[1, k] = groups.core_swap(sources[0, k])
        if i == 0:
            weight_grads = place_call([(0, k)], weight_grads, "place_second")
    third = [(0, k) for k in tops[1:]] + [(1, k) for k in tops[:1]]
    weight_grads = place_call(third, weight_grads, "place_third")
    weight_grads = place_call([(1, k) for k in tops[1:]], weight_grads, "place_last")
    return (grad_node, grad_edge, *weight_grads)


def solution(mesh):
    rows = P(AXES, None)
    flat = P(AXES)
    in_specs = (
        rows, rows, rows, rows, flat, flat, P(), P("band", None), flat,
        P(), P(), P(), P(), P(), P(), P(), P(),
    )
    out_specs = (rows, rows) + (P(),) * 8
    return jax.shard_map(
        on_device, mesh=mesh, in_specs=in_specs, out_specs=out_specs, check_vma=False
    )
```

```python
import math

import jax
import jax.numpy as jnp
from jax import lax
from jax.experimental import pallas as pl
from jax.experimental.pallas import tpu as pltpu
from jax.sharding import PartitionSpec as P


EB = 128
LANES = 128
NORM_EPS = 1e-05
BF = jnp.bfloat16
F32 = jnp.float32
AXES = ("band", "helper")
VMEM_LIMIT = 24 * 1024 * 1024


def round_up(size, unit):
    return -(-size // unit) * unit


def dot(left, right):
    return jnp.dot(left, right, preferred_element_type=F32)


def dot_left_t(left, right):
    return lax.dot_general(left, right, (((0,), (0,)), ((), ())), preferred_element_type=F32)


def dot_right_t(left, right):
    return lax.dot_general(left, right, (((1,), (1,)), ((), ())), preferred_element_type=F32)


def normalise(pre):
    centre = pre - jnp.mean(pre, axis=-1, keepdims=True)
    inv = lax.rsqrt(jnp.mean(centre * centre, axis=-1, keepdims=True) + NORM_EPS)
    return centre * inv, inv


def norm_back(grad, normed, inv):
    return inv * (
        grad
        - jnp.mean(grad, axis=-1, keepdims=True)
        - normed * jnp.mean(grad * normed, axis=-1, keepdims=True)
    )


def ids_down_rows(ids_row):
    return jnp.broadcast_to(ids_row, (LANES, LANES)).T


def onehot_rows(ids_cols, width):
    rows = ids_cols[0].shape[0]
    lane = lax.broadcasted_iota(jnp.int32, (rows, LANES), 1)
    tiles = []
    for start in range(0, width, LANES):
        hit = ids_cols[0] == lane + start
        for more in ids_cols[1:]:
            hit = hit | (more == lane + start)
        tiles.append(jnp.where(hit, 1.0, 0.0).astype(BF))
    return jnp.concatenate(tiles, axis=1)


def onehot_cols(ids_rows, height):
    count = ids_rows[0].shape[1]
    down = lax.broadcasted_iota(jnp.int32, (height, count), 0)
    hit = ids_rows[0] == down
    for more in ids_rows[1:]:
        hit = hit | (more == down)
    return jnp.where(hit, 1.0, 0.0).astype(BF)


def call(kernel, out_shape, args, scratch=(), hbm_out=(), flops=0):
    in_specs = [pl.BlockSpec(memory_space=pltpu.VMEM)] * len(args)
    out_specs = [
        pl.BlockSpec(memory_space=pl.ANY if i in hbm_out else pltpu.VMEM)
        for i in range(len(out_shape))
    ]
    nbytes = sum(a.size * a.dtype.itemsize for a in args)
    nbytes += sum(math.prod(o.shape) * o.dtype.itemsize for o in out_shape)
    return pl.pallas_call(
        kernel,
        out_shape=out_shape,
        in_specs=in_specs,
        out_specs=out_specs,
        scratch_shapes=list(scratch),
        compiler_params=pltpu.CompilerParams(vmem_limit_bytes=VMEM_LIMIT),
        cost_estimate=pl.CostEstimate(flops=flops, bytes_accessed=nbytes, transcendentals=0),
    )(*args)


def sds(rows, cols, dtype):
    return jax.ShapeDtypeStruct((rows, cols), dtype)


class Groups:
    def __init__(self, bands, helpers):
        self.bands = bands
        self.helpers = helpers
        self.core = 2 if bands % 2 == 0 else 1
        rest = bands // self.core
        self.near = 2 if (helpers <= 2 and rest % 2 == 0) else 1
        self.group = self.near * helpers
        far = rest // self.near
        self.far_rounds = []
        stride = self.core * self.near
        while far > 1:
            size = 4 if far % 4 == 0 else 2
            self.far_rounds.append((stride, size))
            stride *= size
            far //= size

        self.crossed = (
            self.core == 2 and len(self.far_rounds) == 1 and self.far_rounds[0][1] == self.group
        )

    def permute(self, array, move):
        pairs = []
        for band in range(self.bands):
            for helper in range(self.helpers):
                to_band, to_helper = move(band, helper)
                pairs.append((band * self.helpers + helper, to_band * self.helpers + to_helper))
        return lax.ppermute(array, AXES, pairs)

    def core_swap(self, array):
        return self.permute(array, lambda b, h: (b ^ 1, h))

    def helper_swap(self, array, k):
        return self.permute(array, lambda b, h: (b, h ^ k))

    def near_move(self, band, helper, k):
        near, help_k = divmod(k, self.helpers)
        return band ^ (near * self.core), helper ^ help_k

    def first_swap(self, array, k):
        def move(band, helper):
            if self.crossed and band % 2:
                return band ^ (k * self.far_rounds[0][0]), helper
            return self.near_move(band, helper, k)

        return self.permute(array, move)

    def second_swap(self, array, stride, k):
        def move(band, helper):
            if self.crossed and band % 2:
                return self.near_move(band, helper, k)
            return band ^ (k * stride), helper

        return self.permute(array, move)

    def ring(self, array, by):
        return self.permute(array, lambda b, h: ((b + by) % self.bands, h))

    def core_id(self):
        return lax.rem(lax.axis_index("band"), self.core)

    def first_id(self, core):
        band = lax.axis_index("band")
        near = lax.rem(lax.div(band, self.core), self.near)
        near = near * self.helpers + lax.axis_index("helper")
        if not self.crossed:
            return near
        return jnp.where(core == 1, lax.div(band, self.core * self.near), near)


def tree_sum(parts):
    parts = list(parts)
    while len(parts) > 1:
        parts = [parts[i] + parts[i + 1] for i in range(0, len(parts), 2)]
    return parts[0]


def on_device(
    node_latent,
    edge_latent,
    grad_out_node,
    grad_out_edge,
    senders,
    receivers,
    band_edges,
    halo_list,
    sea_mask,
    edge_w1,
    edge_b1,
    edge_w2,
    edge_b2,
    node_w1,
    node_b1,
    node_w2,
    node_b2,
):
    helpers = lax.axis_size("helper")
    bands = lax.axis_size("band")
    groups = Groups(bands, helpers)
    own, feat = node_latent.shape
    band = own * helpers
    halo = halo_list.shape[1]
    edges = edge_latent.shape[0]
    slots = edges // EB
    look = band + 2 * halo
    chunk = 2 * EB if slots % 2 == 0 else EB
    per_chunk = chunk // EB
    edge_scale = 1.0 / math.sqrt(edges * helpers * bands)
    node_share = 1.0 / math.sqrt(own * helpers * bands) / helpers
    unit = edges * feat * feat * 2

    send_ids = senders.reshape(slots, EB)
    recv_ids = receivers.reshape(slots, EB)

    group = groups.group
    pieces = groups.core * group
    slices = [edge_w1.shape[0] // pieces, edge_w2.shape[0] // pieces, 8]
    n_slices = [node_w1.shape[0] // pieces, node_w2.shape[0] // pieces]
    e_piece, n_piece = sum(slices), sum(n_slices)
    piece = e_piece + n_piece
    half = piece * group
    starts = [0, slices[0], e_piece, e_piece + n_slices[0]]
    heights = [slices[0], slices[1], n_slices[0], n_slices[1]]
    at_bias = slices[0] + slices[1]

    def chunk_ids(ref, index):
        return jnp.concatenate(
            [
                ids_down_rows(ref[pl.ds(index * per_chunk + j, 1), :])
                for j in range(per_chunk)
            ],
            axis=0,
        )

    def chunk_row(ref, index):
        return jnp.concatenate(
            [ref[pl.ds(index * per_chunk + j, 1), :] for j in range(per_chunk)], axis=1
        )

    def chunk_live(ref, index):
        rows = [
            jnp.broadcast_to(ref[pl.ds(index * per_chunk + j, 1), :], (EB, feat))
            for j in range(per_chunk)
        ]
        return jnp.concatenate(rows, axis=0)

    b_width = round_up(2 * band, LANES)
    h_width = round_up(2 * halo, LANES)
    r_width = round_up(band, LANES)

    theirs = [groups.helper_swap(node_latent, k) for k in range(1, helpers)]

    def gather_kernel(halo_ref, *refs):
        parts, (band_ref, out_ref) = refs[:helpers], refs[helpers:]
        me = lax.axis_index("helper")
        for k in range(helpers):
            at = pl.multiple_of((me ^ k) * own, own)
            band_ref[pl.ds(at, own), :] = parts[k][...]
        pick = onehot_cols([halo_ref[...]], band)
        out_ref[...] = dot_left_t(pick, band_ref[...]).astype(BF)

    band_rows, outgoing = call(
        gather_kernel, [sds(band, feat, BF), sds(halo, feat, BF)], [halo_list, node_latent, *theirs]
    )
    from_prev = groups.ring(outgoing, 1)
    from_next = groups.ring(outgoing, -1)

    def split_store(table, height, at, proj):
        high = proj.astype(BF)
        table[at : at + proj.shape[0], :] = high
        table[height + at : height + at + proj.shape[0], :] = (proj - high.astype(F32)).astype(BF)

    def local_kernel(
        send_ref, recv_ref, band_ref, e_ref, w1_ref, b1_ref, b2_ref, nb1_ref, nb2_ref, be_ref,
        sea_ref, pre_ref, place_ref, recv_pick_ref, halo_pick_ref, et_ref, bias_ref, live_ref,
        sea_diag_ref, table,
    ):
        for i, ref in enumerate((b1_ref, b2_ref, nb1_ref, nb2_ref)):
            bias_ref[i, :] = ref[...]
        counts = be_ref[...][None, :]
        mine = lax.broadcasted_iota(jnp.int32, counts.shape, 1) == lax.axis_index("band")
        count = jnp.sum(jnp.where(mine, counts, 0), axis=1, keepdims=True)
        slot = lax.broadcasted_iota(jnp.int32, (slots, feat), 0)
        live_ref[...] = jnp.where(
            slot * helpers + lax.axis_index("helper") < count, 1.0, 0.0
        )
        down = lax.broadcasted_iota(jnp.int32, (own, own), 0)
        across = lax.broadcasted_iota(jnp.int32, (own, own), 1)
        sea_diag_ref[...] = jnp.where(
            (down == across) & (sea_ref[...][None, :] != 0), 1.0, 0.0
        ).astype(BF)
        if b_width > 2 * band:
            table[...] = jnp.zeros_like(table)
        for at, rows in ((0, slice(0, feat)), (band, slice(feat, 2 * feat))):
            split_store(table, b_width, at, dot(band_ref[...], w1_ref[rows, :]))
        for i in range(edges // chunk):
            rows = pl.ds(i * chunk, chunk)
            send_cols = chunk_ids(send_ref, i)
            recv_cols = chunk_ids(recv_ref, i)
            halo_pick_ref[rows, :] = onehot_rows([send_cols - band], h_width)
            recv_pick_ref[rows, :] = onehot_rows([recv_cols], r_width)
            place_ref[:, rows] = onehot_cols(
                [chunk_row(send_ref, i), chunk_row(recv_ref, i) + look], look + band
            )
            send_cols = jnp.where(send_cols < band, send_cols, -1)
            pick = onehot_rows([send_cols, recv_cols + band], b_width)
            pre = dot(jnp.concatenate([pick, pick], axis=1), table[...])
            e_rows = e_ref[rows, :]
            pre_ref[rows, :] = pre + dot(e_rows, w1_ref[2 * feat :, :]) + b1_ref[...][None, :]
            et_ref[:, rows] = e_rows.T

    pre_local, place, recv_pick, halo_pick, edge_t, biases, live, sea_diag = call(
        local_kernel,
        [
            sds(edges, feat, F32), sds(look + band, edges, BF), sds(edges, r_width, BF),
            sds(edges, h_width, BF), sds(feat, edges, BF), sds(4, feat, F32),
            sds(slots, feat, F32), sds(own, own, BF),
        ],
        [send_ids, recv_ids, band_rows, edge_latent, edge_w1, edge_b1, edge_b2, node_b1, node_b2,
         band_edges, sea_mask],
        scratch=[pltpu.VMEM((2 * b_width, feat), BF)],
        flops=4 * unit,
    )

    def forward_kernel(
        live_ref, pre_ref, place_ref, halo_pick_ref, prev_ref, next_ref, w1_ref, w2_ref, bias_ref,
        gon_ref, sea_ref, hid_ref, slope_ref, norm_ref, inv_ref, agg, swap_ref, table,
    ):
        if h_width > 2 * halo:
            table[...] = jnp.zeros_like(table)
        halo_rows = jnp.concatenate([prev_ref[...], next_ref[...]], axis=0)
        split_store(table, h_width, 0, dot(halo_rows, w1_ref[...]))
        for i in range(edges // chunk):
            rows = pl.ds(i * chunk, chunk)
            pick = halo_pick_ref[rows, :]
            pre = pre_ref[rows, :] + dot(jnp.concatenate([pick, pick], axis=1), table[...])
            sig = jax.nn.sigmoid(pre)
            hidden = (pre * sig).astype(BF)
            hid_ref[rows, :] = hidden
            slope_ref[rows, :] = sig * (1.0 + pre * (1.0 - sig))
            normed, inv = normalise(dot(hidden, w2_ref[...]) + bias_ref[1:2, :])
            norm_ref[rows, :] = normed
            inv_ref[rows, :] = inv
            message = (normed * chunk_live(live_ref, i)).astype(BF)
            part = dot(place_ref[look:, rows], message)
            if i == 0:
                agg[...] = part
            else:
                agg[...] += part
        swap_ref[:band, :] = agg[...].astype(BF)
        swap_ref[band:, :] = dot(sea_ref[...], gon_ref[...]).astype(BF)

    hidden, slope, normed, inv, agg_own, swap_own = call(
        forward_kernel,
        [sds(edges, feat, BF), sds(edges, feat, F32), sds(edges, feat, F32), sds(edges, 1, F32),
         sds(band, feat, F32), sds(band + own, feat, BF)],
        [live, pre_local, place, halo_pick, from_prev, from_next, edge_w1[:feat], edge_w2,
         biases, grad_out_node, sea_diag],
        scratch=[pltpu.VMEM((2 * h_width, feat), BF)],
        flops=3 * unit,
    )

    swaps = [swap_own] + [groups.helper_swap(swap_own, k) for k in range(1, helpers)]

    def backward_kernel(
        live_ref, place_ref, recv_pick_ref, band_ref, prev_ref, next_ref, et_ref, geo_ref,
        hid_ref, slope_ref, norm_ref, inv_ref, w1_ref, w2_ref, nw1_ref, nw2_ref, bias_ref,
        agg_ref, *refs,
    ):
        parts = refs[:helpers]
        edge_hbm, keep_ref, give_ref, lg_ref, din_ref, grads, sums, seed, edge_ref, sems = refs[helpers:]
        edge_copies = []
        band_v = band_ref[...]
        me = lax.axis_index("helper")
        for k in range(helpers):
            seed[pl.ds(pl.multiple_of((me ^ k) * own, own), own), :] = parts[k][band:, :]
        agg = tree_sum([agg_ref[...]] + [p[:band, :].astype(F32) for p in parts[1:]]).astype(BF)
        node_in = jnp.concatenate([band_v, agg], axis=1)
        n_pre = dot(node_in, nw1_ref[...]) + bias_ref[2:3, :]
        n_sig = jax.nn.sigmoid(n_pre)
        n_hidden = (n_pre * n_sig).astype(BF)
        n_normed, n_inv = normalise(dot(n_hidden, nw2_ref[...]) + bias_ref[3:4, :])
        n_dz = norm_back(seed[...].astype(F32), n_normed, n_inv)
        n_dzb = n_dz.astype(BF)
        n_dpre = dot_right_t(n_dzb, nw2_ref[...]) * (n_sig * (1.0 + n_pre * (1.0 - n_sig)))
        n_dpreb = n_dpre.astype(BF)
        din_ref[...] = dot_right_t(n_dpreb, nw1_ref[:feat, :])
        agg_grad = dot_right_t(n_dpreb, nw1_ref[feat:, :]).astype(BF)

        def put(which, first, value):
            high, row, count = heights[which], 0, value.shape[0]
            while row < count:
                spot, within = divmod(first + row, high)
                take = min(high - within, count - row)
                at = spot * piece + starts[which] + within
                grads[at : at + take, :] = value[row : row + take, :]
                row += take

        put(2, 0, dot_left_t(node_in, n_dpreb) * node_share)
        put(3, 0, dot_left_t(n_hidden, n_dzb) * node_share)
        gb_n1 = jnp.sum(n_dpre, axis=0, keepdims=True) * node_share
        gb_n2 = jnp.sum(n_dz, axis=0, keepdims=True) * node_share

        w1e = w1_ref[2 * feat :, :]
        gb_1 = jnp.zeros((1, feat), F32)
        gb_2 = jnp.zeros((1, feat), F32)
        gw_1 = jnp.zeros((feat, feat), F32)
        gw_2 = jnp.zeros((feat, feat), F32)
        for i in range(edges // chunk):
            rows = pl.ds(i * chunk, chunk)
            live = chunk_live(live_ref, i)
            geo = geo_ref[rows, :].astype(F32)
            at_recv = dot(recv_pick_ref[rows, :band], agg_grad)
            msg_grad = (geo + at_recv) * live
            dz = norm_back(msg_grad, norm_ref[rows, :], inv_ref[rows, :])
            gb_2 = gb_2 + jnp.sum(dz, axis=0, keepdims=True)
            dzb = dz.astype(BF)
            gw_2 = gw_2 + dot_left_t(hid_ref[rows, :], dzb)
            dpre = dot_right_t(dzb, w2_ref[...]) * slope_ref[rows, :]
            gb_1 = gb_1 + jnp.sum(dpre, axis=0, keepdims=True)
            dpreb = dpre.astype(BF)
            gw_1 = gw_1 + dot(et_ref[:, rows], dpreb)
            edge_ref[rows, :] = ((geo + dot_right_t(dpreb, w1e)) * live).astype(BF)
            edge_copies.append(
                pltpu.make_async_copy(edge_ref.at[rows, :], edge_hbm.at[rows, :], sems.at[i])
            )
            edge_copies[-1].start()
            part = dot(place_ref[:, rows], dpreb)
            if i == 0:
                sums[...] = part
            else:
                sums[...] += part
        at_send = sums[:look, :].astype(BF)
        at_recv = sums[look:, :].astype(BF)
        lookup = jnp.concatenate([band_v, prev_ref[...], next_ref[...]], axis=0)
        look_grad = dot_right_t(at_send, w1_ref[:feat, :])
        recv_grad = dot_right_t(at_recv, w1_ref[feat : 2 * feat, :])
        lg_ref[:band, :] = (look_grad[:band, :] + recv_grad).astype(BF)
        lg_ref[band:, :] = look_grad[band:, :].astype(BF)
        put(0, 0, dot_left_t(lookup, at_send) * edge_scale)
        put(0, feat, dot_left_t(band_v, at_recv) * edge_scale)
        put(0, 2 * feat, gw_1 * edge_scale)
        put(1, 0, gw_2 * edge_scale)
        bias = [gb_1 * edge_scale, gb_2 * edge_scale, gb_n1, gb_n2]
        grads[at_bias : at_bias + 8, :] = jnp.concatenate(bias + [jnp.zeros((4, feat), F32)], axis=0)
        for p in range(1, pieces):
            grads[p * piece + at_bias : p * piece + at_bias + 8, :] = jnp.zeros((8, feat), F32)
        core = groups.core_id()
        other = groups.core - 1 - core
        keep_ref[...] = grads[pl.ds(pl.multiple_of(core * half, 8), half), :]
        give_ref[...] = grads[pl.ds(pl.multiple_of(other * half, 8), half), :].astype(BF)
        for copy in edge_copies:
            copy.wait()

    grad_edge, keep, give, look_grad, node_din = call(
        backward_kernel,
        [sds(edges, feat, BF), sds(half, feat, F32), sds(half, feat, BF), sds(look, feat, BF),
         sds(band, feat, F32)],
        [live, place, recv_pick, band_rows, from_prev, from_next, edge_t, grad_out_edge,
         hidden, slope, normed, inv, edge_w1, edge_w2, node_w1, node_w2, biases, agg_own, *swaps],
        scratch=[pltpu.VMEM((half * groups.core, feat), F32), pltpu.VMEM((look + band, feat), F32),
                 pltpu.VMEM((band, feat), BF), pltpu.VMEM((edges, feat), BF),
                 pltpu.SemaphoreType.DMA((edges // chunk,))],
        hbm_out=(0,),
        flops=8 * unit,
    )

    got = groups.core_swap(give)
    looks = [look_grad] + [groups.helper_swap(look_grad, k) for k in range(1, helpers)]

    def split_kernel(keep_ref, got_ref, own_ref, *refs):
        outs, summed = refs[:-1], refs[-1]
        summed[...] = keep_ref[...] + got_ref[...].astype(F32)
        me = groups.first_id(groups.core_id())
        own_ref[...] = summed[pl.ds(pl.multiple_of(me * piece, 8), piece), :]
        for k in range(1, group):
            part = summed[pl.ds(pl.multiple_of((me ^ k) * piece, 8), piece), :]
            outs[k - 1][...] = part.astype(BF)

    own_part, *to_group = call(
        split_kernel,
        [sds(piece, feat, F32)] + [sds(piece, feat, BF)] * (group - 1),
        [keep, got],
        scratch=[pltpu.VMEM((half, feat), F32)],
    )
    from_group = [groups.first_swap(part, k) for k, part in enumerate(to_group, 1)]

    def look_kernel(*refs):
        parts, (mine_ref, prev_ref, next_ref) = refs[:helpers], refs[helpers:]
        at = pl.multiple_of(lax.axis_index("helper") * own, own)
        mine_ref[...] = tree_sum([g[pl.ds(at, own), :].astype(F32) for g in parts])
        halos = tree_sum([g[band:, :].astype(F32) for g in parts])
        prev_ref[...] = halos[:halo, :].astype(BF)
        next_ref[...] = halos[halo:, :].astype(BF)

    own_grad, prev_grad, next_grad = call(
        look_kernel, [sds(own, feat, F32), sds(halo, feat, BF), sds(halo, feat, BF)], looks
    )
    halo_back = groups.ring(prev_grad, -1)
    halo_forth = groups.ring(next_grad, 1)

    def join_kernel(own_ref, *refs):
        parts, piece_ref = refs[: group - 1], refs[group - 1]
        summed = own_ref[...]
        for part in parts:
            summed = summed + part[...].astype(F32)
        piece_ref[...] = summed.astype(BF)

    (piece_sum,) = call(join_kernel, [sds(piece, feat, BF)], [own_part, *from_group])

    halo_sums = None
    for stride, size in groups.far_rounds:
        swapped = [piece_sum] + [groups.second_swap(piece_sum, stride, k) for k in range(1, size)]
        first = halo_sums is None

        def far_kernel(*refs):
            parts, rest = refs[:size], refs[size:]
            rest[-1][...] = tree_sum([r[...].astype(F32) for r in parts]).astype(BF)
            if first:
                halo_ref, back_ref, forth_ref, out_ref, _ = rest
                at = lax.axis_index("helper") * own
                place = onehot_cols([halo_ref[...] - at], own)
                out_ref[...] = dot(place, back_ref[...]) + dot(place, forth_ref[...])

        if first:
            halo_sums, piece_sum = call(
                far_kernel,
                [sds(own, feat, F32), sds(piece, feat, BF)],
                swapped + [halo_list, halo_back, halo_forth],
            )
        else:
            (piece_sum,) = call(far_kernel, [sds(piece, feat, BF)], swapped)

    gathered = [piece_sum] + [groups.first_swap(piece_sum, k) for k in range(1, group)]
    vec = jax.ShapeDtypeStruct((feat,), F32)
    out_shape = [
        jax.ShapeDtypeStruct(edge_w1.shape, F32), vec, jax.ShapeDtypeStruct(edge_w2.shape, F32),
        vec, jax.ShapeDtypeStruct(node_w1.shape, F32), vec,
        jax.ShapeDtypeStruct(node_w2.shape, F32), vec,
    ]

    def place_pieces(parts, spots, outs, buf, row, sems):
        copies = []
        for i, (part, spot) in enumerate(zip(parts, spots)):
            buf[i * piece : (i + 1) * piece, :] = part[...].astype(F32)
            for j, (start, high, out) in enumerate(zip(starts, heights, outs[::2])):
                copies.append(
                    pltpu.make_async_copy(
                        buf.at[pl.ds(i * piece + start, high), :],
                        out.at[pl.ds(pl.multiple_of(spot * high, 8), high), :],
                        sems.at[i, j],
                    )
                )
                copies[-1].start()
        for i, spot in enumerate(spots):

            @pl.when(spot == 0)
            def _():
                for j, out in enumerate(outs[1::2]):
                    row[j][...] = buf[i * piece + at_bias + j, :]
                    pltpu.make_async_copy(row[j], out, sems.at[len(parts), j]).start()
                for j, out in enumerate(outs[1::2]):
                    pltpu.make_async_copy(row[j], out, sems.at[len(parts), j]).wait()

        for copy in copies:
            copy.wait()

    def place_call(keys, held, node=None):
        count = len(keys)
        parts = [sources[which, k] for which, k in keys]
        extra = [] if node is None else node

        def kernel(*refs):
            part_refs, refs = refs[:count], refs[count:]
            node_refs, refs = refs[: len(extra)], refs[len(extra) + len(held) :]
            if extra:
                node_out, *refs = refs
                halo_ref, mine_ref, din_ref, gon_ref = node_refs
                at = pl.multiple_of(lax.axis_index("helper") * own, own)
                node_out[...] = (
                    halo_ref[...] + mine_ref[...] + din_ref[pl.ds(at, own), :]
                    + gon_ref[...].astype(F32)
                )
            outs, (buf, *row, sems) = refs[:8], refs[8:]
            spots = []
            for which, k in keys:
                core = groups.core - 1 - groups.core_id() if which else groups.core_id()
                spots.append(core * group + (groups.first_id(core) ^ k))
            place_pieces(part_refs, spots, outs, buf, row, sems)

        vmem, hbm = pl.BlockSpec(memory_space=pltpu.VMEM), pl.BlockSpec(memory_space=pl.ANY)
        node_out = [sds(own, feat, F32)] if extra else []
        return pl.pallas_call(
            kernel,
            out_shape=node_out + out_shape,
            in_specs=[vmem] * (count + len(extra)) + [hbm] * len(held),
            out_specs=[vmem] * len(node_out) + [hbm] * 8,
            scratch_shapes=[pltpu.VMEM((count * piece, feat), F32)]
            + [pltpu.VMEM((feat,), F32)] * 4
            + [pltpu.SemaphoreType.DMA((count + 1, 4))],
            input_output_aliases={count + len(extra) + i: i for i in range(len(held))},
            compiler_params=pltpu.CompilerParams(vmem_limit_bytes=VMEM_LIMIT),
            cost_estimate=pl.CostEstimate(
                flops=0, bytes_accessed=6 * count * piece * feat, transcendentals=0
            ),
        )(*parts, *extra, *held)

    sources = {(0, k): part for k, part in enumerate(gathered)}
    sources[1, 0] = groups.core_swap(piece_sum)
    grad_node, *weight_grads = place_call(
        [(0, 0), (1, 0)], [], [halo_sums, own_grad, node_din, grad_out_node]
    )
    tops = range(group - 1, 0, -1)
    for i, k in enumerate(tops):
        if i < 2:
            sources[0, k], *weight_grads = lax.optimization_barrier(
                (sources[0, k], *weight_grads)
            )
        sources[1, k] = groups.core_swap(sources[0, k])
        if i == 0:
            weight_grads = place_call([(0, k)], weight_grads)
    third = [(0, k) for k in tops[1:]] + [(1, k) for k in tops[:1]]
    weight_grads = place_call(third, weight_grads)
    weight_grads = place_call([(1, k) for k in tops[1:]], weight_grads)
    return (grad_node, grad_edge, *weight_grads)


def solution(mesh):
    rows = P(AXES, None)
    flat = P(AXES)
    in_specs = (
        rows, rows, rows, rows, flat, flat, P(), P("band", None), flat,
        P(), P(), P(), P(), P(), P(), P(), P(),
    )
    out_specs = (rows, rows) + (P(),) * 8

    return jax.shard_map(
        on_device, mesh=mesh, in_specs=in_specs, out_specs=out_specs, check_vma=False
    )
```

```python
import math

import jax
import jax.numpy as jnp
from jax import lax
from jax.experimental import pallas as pl
from jax.experimental.pallas import tpu as pltpu
from jax.sharding import PartitionSpec as P


EB = 128
LANES = 128
NORM_EPS = 1e-05
BF = jnp.bfloat16
F32 = jnp.float32
AXES = ("band", "helper")
VMEM_LIMIT = 24 * 1024 * 1024


def round_up(size, unit):
    return -(-size // unit) * unit


def dot(left, right):
    return jnp.dot(left, right, preferred_element_type=F32)


def dot_left_t(left, right):
    return lax.dot_general(left, right, (((0,), (0,)), ((), ())), preferred_element_type=F32)


def dot_right_t(left, right):
    return lax.dot_general(left, right, (((1,), (1,)), ((), ())), preferred_element_type=F32)


def normalise(pre):
    centre = pre - jnp.mean(pre, axis=-1, keepdims=True)
    inv = lax.rsqrt(jnp.mean(centre * centre, axis=-1, keepdims=True) + NORM_EPS)
    return centre * inv, inv


def norm_back(grad, normed, inv):
    return inv * (
        grad
        - jnp.mean(grad, axis=-1, keepdims=True)
        - normed * jnp.mean(grad * normed, axis=-1, keepdims=True)
    )


def ids_down_rows(ids_row):
    return jnp.broadcast_to(ids_row, (LANES, LANES)).T


def onehot_rows(ids_cols, width):
    rows = ids_cols[0].shape[0]
    lane = lax.broadcasted_iota(jnp.int32, (rows, LANES), 1)
    tiles = []
    for start in range(0, width, LANES):
        hit = ids_cols[0] == lane + start
        for more in ids_cols[1:]:
            hit = hit | (more == lane + start)
        tiles.append(jnp.where(hit, 1.0, 0.0).astype(BF))
    return jnp.concatenate(tiles, axis=1)


def onehot_cols(ids_rows, height):
    count = ids_rows[0].shape[1]
    down = lax.broadcasted_iota(jnp.int32, (height, count), 0)
    hit = ids_rows[0] == down
    for more in ids_rows[1:]:
        hit = hit | (more == down)
    return jnp.where(hit, 1.0, 0.0).astype(BF)


def call(kernel, out_shape, args, scratch=(), hbm_out=(), flops=0):
    in_specs = [pl.BlockSpec(memory_space=pltpu.VMEM)] * len(args)
    out_specs = [
        pl.BlockSpec(memory_space=pl.ANY if i in hbm_out else pltpu.VMEM)
        for i in range(len(out_shape))
    ]
    nbytes = sum(a.size * a.dtype.itemsize for a in args)
    nbytes += sum(math.prod(o.shape) * o.dtype.itemsize for o in out_shape)
    return pl.pallas_call(
        kernel,
        out_shape=out_shape,
        in_specs=in_specs,
        out_specs=out_specs,
        scratch_shapes=list(scratch),
        compiler_params=pltpu.CompilerParams(vmem_limit_bytes=VMEM_LIMIT),
        cost_estimate=pl.CostEstimate(flops=flops, bytes_accessed=nbytes, transcendentals=0),
    )(*args)


def sds(rows, cols, dtype):
    return jax.ShapeDtypeStruct((rows, cols), dtype)


class Groups:
    def __init__(self, bands, helpers):
        self.bands = bands
        self.helpers = helpers
        self.core = 2 if bands % 2 == 0 else 1
        rest = bands // self.core
        self.near = 2 if (helpers <= 2 and rest % 2 == 0) else 1
        self.group = self.near * helpers
        far = rest // self.near
        self.far_rounds = []
        stride = self.core * self.near
        while far > 1:
            size = 4 if far % 4 == 0 else 2
            self.far_rounds.append((stride, size))
            stride *= size
            far //= size

        self.crossed = (
            self.core == 2 and len(self.far_rounds) == 1 and self.far_rounds[0][1] == self.group
        )

    def permute(self, array, move):
        pairs = []
        for band in range(self.bands):
            for helper in range(self.helpers):
                to_band, to_helper = move(band, helper)
                pairs.append((band * self.helpers + helper, to_band * self.helpers + to_helper))
        return lax.ppermute(array, AXES, pairs)

    def core_swap(self, array):
        return self.permute(array, lambda b, h: (b ^ 1, h))

    def helper_swap(self, array, k):
        return self.permute(array, lambda b, h: (b, h ^ k))

    def near_move(self, band, helper, k):
        near, help_k = divmod(k, self.helpers)
        return band ^ (near * self.core), helper ^ help_k

    def first_swap(self, array, k):
        def move(band, helper):
            if self.crossed and band % 2:
                return band ^ (k * self.far_rounds[0][0]), helper
            return self.near_move(band, helper, k)

        return self.permute(array, move)

    def second_swap(self, array, stride, k):
        def move(band, helper):
            if self.crossed and band % 2:
                return self.near_move(band, helper, k)
            return band ^ (k * stride), helper

        return self.permute(array, move)

    def ring_swap(self, array):
        return self.permute(
            array, lambda b, h: ((b + (1 if b % 2 else -1)) % self.bands, h)
        )

    def core_id(self):
        return lax.rem(lax.axis_index("band"), self.core)

    def first_id(self, core):
        band = lax.axis_index("band")
        near = lax.rem(lax.div(band, self.core), self.near)
        near = near * self.helpers + lax.axis_index("helper")
        if not self.crossed:
            return near
        return jnp.where(core == 1, lax.div(band, self.core * self.near), near)


def tree_sum(parts):
    parts = list(parts)
    while len(parts) > 1:
        parts = [parts[i] + parts[i + 1] for i in range(0, len(parts), 2)]
    return parts[0]


def on_device(
    node_latent,
    edge_latent,
    grad_out_node,
    grad_out_edge,
    senders,
    receivers,
    band_edges,
    halo_list,
    sea_mask,
    edge_w1,
    edge_b1,
    edge_w2,
    edge_b2,
    node_w1,
    node_b1,
    node_w2,
    node_b2,
):
    helpers = lax.axis_size("helper")
    bands = lax.axis_size("band")
    groups = Groups(bands, helpers)
    own, feat = node_latent.shape
    band = own * helpers
    halo = halo_list.shape[1]
    edges = edge_latent.shape[0]
    slots = edges // EB
    look = band + 2 * halo
    chunk = 2 * EB if slots % 2 == 0 else EB
    per_chunk = chunk // EB
    edge_scale = 1.0 / math.sqrt(edges * helpers * bands)
    node_share = 1.0 / math.sqrt(own * helpers * bands) / helpers
    unit = edges * feat * feat * 2

    send_ids = senders.reshape(slots, EB)
    recv_ids = receivers.reshape(slots, EB)

    group = groups.group
    pieces = groups.core * group
    slices = [edge_w1.shape[0] // pieces, edge_w2.shape[0] // pieces, 8]
    n_slices = [node_w1.shape[0] // pieces, node_w2.shape[0] // pieces]
    e_piece, n_piece = sum(slices), sum(n_slices)
    piece = e_piece + n_piece
    half = piece * group
    starts = [0, slices[0], e_piece, e_piece + n_slices[0]]
    heights = [slices[0], slices[1], n_slices[0], n_slices[1]]
    at_bias = slices[0] + slices[1]

    def chunk_ids(ref, index):
        return jnp.concatenate(
            [
                ids_down_rows(ref[pl.ds(index * per_chunk + j, 1), :])
                for j in range(per_chunk)
            ],
            axis=0,
        )

    def chunk_row(ref, index):
        return jnp.concatenate(
            [ref[pl.ds(index * per_chunk + j, 1), :] for j in range(per_chunk)], axis=1
        )

    def chunk_live(ref, index):
        rows = [
            jnp.broadcast_to(ref[pl.ds(index * per_chunk + j, 1), :], (EB, feat))
            for j in range(per_chunk)
        ]
        return jnp.concatenate(rows, axis=0)

    b_width = round_up(2 * band, LANES)
    h_width = round_up(2 * halo, LANES)
    r_width = round_up(band, LANES)

    theirs = [groups.helper_swap(node_latent, k) for k in range(1, helpers)]

    def gather_kernel(halo_ref, *refs):
        parts, (band_ref, out_ref) = refs[:helpers], refs[helpers:]
        me = lax.axis_index("helper")
        for k in range(helpers):
            at = pl.multiple_of((me ^ k) * own, own)
            band_ref[pl.ds(at, own), :] = parts[k][...]
        pick = onehot_cols([halo_ref[...]], band)
        out_ref[...] = dot_left_t(pick, band_ref[...]).astype(BF)

    band_rows, outgoing = call(
        gather_kernel, [sds(band, feat, BF), sds(halo, feat, BF)], [halo_list, node_latent, *theirs]
    )
    from_ring = groups.ring_swap(outgoing)
    from_core = groups.core_swap(outgoing)

    def split_store(table, height, at, proj):
        high = proj.astype(BF)
        table[at : at + proj.shape[0], :] = high
        table[height + at : height + at + proj.shape[0], :] = (proj - high.astype(F32)).astype(BF)

    def local_kernel(
        send_ref, recv_ref, band_ref, e_ref, w1_ref, b1_ref, b2_ref, nb1_ref, nb2_ref, be_ref,
        sea_ref, pre_ref, place_ref, recv_pick_ref, halo_pick_ref, et_ref, bias_ref, live_ref,
        sea_diag_ref, table,
    ):
        for i, ref in enumerate((b1_ref, b2_ref, nb1_ref, nb2_ref)):
            bias_ref[i, :] = ref[...]
        counts = be_ref[...][None, :]
        mine = lax.broadcasted_iota(jnp.int32, counts.shape, 1) == lax.axis_index("band")
        count = jnp.sum(jnp.where(mine, counts, 0), axis=1, keepdims=True)
        slot = lax.broadcasted_iota(jnp.int32, (slots, feat), 0)
        live_ref[...] = jnp.where(
            slot * helpers + lax.axis_index("helper") < count, 1.0, 0.0
        )
        down = lax.broadcasted_iota(jnp.int32, (own, own), 0)
        across = lax.broadcasted_iota(jnp.int32, (own, own), 1)
        sea_diag_ref[...] = jnp.where(
            (down == across) & (sea_ref[...][None, :] != 0), 1.0, 0.0
        ).astype(BF)
        if b_width > 2 * band:
            table[...] = jnp.zeros_like(table)
        for at, rows in ((0, slice(0, feat)), (band, slice(feat, 2 * feat))):
            split_store(table, b_width, at, dot(band_ref[...], w1_ref[rows, :]))
        for i in range(edges // chunk):
            rows = pl.ds(i * chunk, chunk)
            send_cols = chunk_ids(send_ref, i)
            recv_cols = chunk_ids(recv_ref, i)
            halo_pick_ref[rows, :] = onehot_rows([send_cols - band], h_width)
            recv_pick_ref[rows, :] = onehot_rows([recv_cols], r_width)
            place_ref[:, rows] = onehot_cols(
                [chunk_row(send_ref, i), chunk_row(recv_ref, i) + look], look + band
            )
            send_cols = jnp.where(send_cols < band, send_cols, -1)
            pick = onehot_rows([send_cols, recv_cols + band], b_width)
            pre = dot(jnp.concatenate([pick, pick], axis=1), table[...])
            e_rows = e_ref[rows, :]
            pre_ref[rows, :] = pre + dot(e_rows, w1_ref[2 * feat :, :]) + b1_ref[...][None, :]
            et_ref[:, rows] = e_rows.T

    pre_local, place, recv_pick, halo_pick, edge_t, biases, live, sea_diag = call(
        local_kernel,
        [
            sds(edges, feat, F32), sds(look + band, edges, BF), sds(edges, r_width, BF),
            sds(edges, h_width, BF), sds(feat, edges, BF), sds(4, feat, F32),
            sds(slots, feat, F32), sds(own, own, BF),
        ],
        [send_ids, recv_ids, band_rows, edge_latent, edge_w1, edge_b1, edge_b2, node_b1, node_b2,
         band_edges, sea_mask],
        scratch=[pltpu.VMEM((2 * b_width, feat), BF)],
        flops=4 * unit,
    )

    def forward_kernel(
        live_ref, pre_ref, place_ref, halo_pick_ref, ring_ref, core_ref, w1_ref, w2_ref, bias_ref,
        gon_ref, sea_ref, hid_ref, slope_ref, norm_ref, inv_ref, agg, swap_ref, halo_ref,
        table,
    ):
        if h_width > 2 * halo:
            table[...] = jnp.zeros_like(table)
        odd = lax.rem(lax.axis_index("band"), 2)
        halo_ref[pl.ds(pl.multiple_of(odd * halo, halo), halo), :] = ring_ref[...]
        halo_ref[pl.ds(pl.multiple_of((1 - odd) * halo, halo), halo), :] = core_ref[...]
        split_store(table, h_width, 0, dot(halo_ref[...], w1_ref[...]))
        for i in range(edges // chunk):
            rows = pl.ds(i * chunk, chunk)
            pick = halo_pick_ref[rows, :]
            pre = pre_ref[rows, :] + dot(jnp.concatenate([pick, pick], axis=1), table[...])
            sig = jax.nn.sigmoid(pre)
            hidden = (pre * sig).astype(BF)
            hid_ref[rows, :] = hidden
            slope_ref[rows, :] = sig * (1.0 + pre * (1.0 - sig))
            normed, inv = normalise(dot(hidden, w2_ref[...]) + bias_ref[1:2, :])
            norm_ref[rows, :] = normed
            inv_ref[rows, :] = inv
            message = (normed * chunk_live(live_ref, i)).astype(BF)
            part = dot(place_ref[look:, rows], message)
            if i == 0:
                agg[...] = part
            else:
                agg[...] += part
        swap_ref[:band, :] = agg[...].astype(BF)
        swap_ref[band:, :] = dot(sea_ref[...], gon_ref[...]).astype(BF)

    hidden, slope, normed, inv, agg_own, swap_own, halo_rows = call(
        forward_kernel,
        [sds(edges, feat, BF), sds(edges, feat, F32), sds(edges, feat, F32), sds(edges, 1, F32),
         sds(band, feat, F32), sds(band + own, feat, BF), sds(2 * halo, feat, BF)],
        [live, pre_local, place, halo_pick, from_ring, from_core, edge_w1[:feat], edge_w2,
         biases, grad_out_node, sea_diag],
        scratch=[pltpu.VMEM((2 * h_width, feat), BF)],
        flops=3 * unit,
    )

    swaps = [swap_own] + [groups.helper_swap(swap_own, k) for k in range(1, helpers)]

    def backward_kernel(
        live_ref, place_ref, recv_pick_ref, band_ref, halo_ref, et_ref, geo_ref,
        hid_ref, slope_ref, norm_ref, inv_ref, w1_ref, w2_ref, nw1_ref, nw2_ref, bias_ref,
        agg_ref, *refs,
    ):
        parts = refs[:helpers]
        edge_hbm, keep_ref, give_ref, lg_ref, din_ref, grads, sums, seed, edge_ref, sems = refs[helpers:]
        edge_copies = []
        band_v = band_ref[...]
        me = lax.axis_index("helper")
        for k in range(helpers):
            seed[pl.ds(pl.multiple_of((me ^ k) * own, own), own), :] = parts[k][band:, :]
        agg = tree_sum([agg_ref[...]] + [p[:band, :].astype(F32) for p in parts[1:]]).astype(BF)
        node_in = jnp.concatenate([band_v, agg], axis=1)
        n_pre = dot(node_in, nw1_ref[...]) + bias_ref[2:3, :]
        n_sig = jax.nn.sigmoid(n_pre)
        n_hidden = (n_pre * n_sig).astype(BF)
        n_normed, n_inv = normalise(dot(n_hidden, nw2_ref[...]) + bias_ref[3:4, :])
        n_dz = norm_back(seed[...].astype(F32), n_normed, n_inv)
        n_dzb = n_dz.astype(BF)
        n_dpre = dot_right_t(n_dzb, nw2_ref[...]) * (n_sig * (1.0 + n_pre * (1.0 - n_sig)))
        n_dpreb = n_dpre.astype(BF)
        din_ref[...] = dot_right_t(n_dpreb, nw1_ref[:feat, :])
        agg_grad = dot_right_t(n_dpreb, nw1_ref[feat:, :]).astype(BF)

        def put(which, first, value):
            high, row, count = heights[which], 0, value.shape[0]
            while row < count:
                spot, within = divmod(first + row, high)
                take = min(high - within, count - row)
                at = spot * piece + starts[which] + within
                grads[at : at + take, :] = value[row : row + take, :]
                row += take

        put(2, 0, dot_left_t(node_in, n_dpreb) * node_share)
        put(3, 0, dot_left_t(n_hidden, n_dzb) * node_share)
        gb_n1 = jnp.sum(n_dpre, axis=0, keepdims=True) * node_share
        gb_n2 = jnp.sum(n_dz, axis=0, keepdims=True) * node_share

        w1e = w1_ref[2 * feat :, :]
        gb_1 = jnp.zeros((1, feat), F32)
        gb_2 = jnp.zeros((1, feat), F32)
        gw_1 = jnp.zeros((feat, feat), F32)
        gw_2 = jnp.zeros((feat, feat), F32)
        for i in range(edges // chunk):
            rows = pl.ds(i * chunk, chunk)
            live = chunk_live(live_ref, i)
            geo = geo_ref[rows, :].astype(F32)
            at_recv = dot(recv_pick_ref[rows, :band], agg_grad)
            msg_grad = (geo + at_recv) * live
            dz = norm_back(msg_grad, norm_ref[rows, :], inv_ref[rows, :])
            gb_2 = gb_2 + jnp.sum(dz, axis=0, keepdims=True)
            dzb = dz.astype(BF)
            gw_2 = gw_2 + dot_left_t(hid_ref[rows, :], dzb)
            dpre = dot_right_t(dzb, w2_ref[...]) * slope_ref[rows, :]
            gb_1 = gb_1 + jnp.sum(dpre, axis=0, keepdims=True)
            dpreb = dpre.astype(BF)
            gw_1 = gw_1 + dot(et_ref[:, rows], dpreb)
            edge_ref[rows, :] = ((geo + dot_right_t(dpreb, w1e)) * live).astype(BF)
            edge_copies.append(
                pltpu.make_async_copy(edge_ref.at[rows, :], edge_hbm.at[rows, :], sems.at[i])
            )
            edge_copies[-1].start()
            part = dot(place_ref[:, rows], dpreb)
            if i == 0:
                sums[...] = part
            else:
                sums[...] += part
        at_send = sums[:look, :].astype(BF)
        at_recv = sums[look:, :].astype(BF)
        lookup = jnp.concatenate([band_v, halo_ref[...]], axis=0)
        look_grad = dot_right_t(at_send, w1_ref[:feat, :])
        recv_grad = dot_right_t(at_recv, w1_ref[feat : 2 * feat, :])
        lg_ref[:band, :] = (look_grad[:band, :] + recv_grad).astype(BF)
        lg_ref[band:, :] = look_grad[band:, :].astype(BF)
        put(0, 0, dot_left_t(lookup, at_send) * edge_scale)
        put(0, feat, dot_left_t(band_v, at_recv) * edge_scale)
        put(0, 2 * feat, gw_1 * edge_scale)
        put(1, 0, gw_2 * edge_scale)
        bias = [gb_1 * edge_scale, gb_2 * edge_scale, gb_n1, gb_n2]
        grads[at_bias : at_bias + 8, :] = jnp.concatenate(bias + [jnp.zeros((4, feat), F32)], axis=0)
        for p in range(1, pieces):
            grads[p * piece + at_bias : p * piece + at_bias + 8, :] = jnp.zeros((8, feat), F32)
        core = groups.core_id()
        other = groups.core - 1 - core
        keep_ref[...] = grads[pl.ds(pl.multiple_of(core * half, 8), half), :]
        give_ref[...] = grads[pl.ds(pl.multiple_of(other * half, 8), half), :].astype(BF)
        for copy in edge_copies:
            copy.wait()

    grad_edge, keep, give, look_grad, node_din = call(
        backward_kernel,
        [sds(edges, feat, BF), sds(half, feat, F32), sds(half, feat, BF), sds(look, feat, BF),
         sds(band, feat, F32)],
        [live, place, recv_pick, band_rows, halo_rows, edge_t, grad_out_edge,
         hidden, slope, normed, inv, edge_w1, edge_w2, node_w1, node_w2, biases, agg_own, *swaps],
        scratch=[pltpu.VMEM((half * groups.core, feat), F32), pltpu.VMEM((look + band, feat), F32),
                 pltpu.VMEM((band, feat), BF), pltpu.VMEM((edges, feat), BF),
                 pltpu.SemaphoreType.DMA((edges // chunk,))],
        hbm_out=(0,),
        flops=8 * unit,
    )

    got = groups.core_swap(give)
    looks = [look_grad] + [groups.helper_swap(look_grad, k) for k in range(1, helpers)]

    def split_kernel(keep_ref, got_ref, own_ref, *refs):
        outs, summed = refs[:-1], refs[-1]
        summed[...] = keep_ref[...] + got_ref[...].astype(F32)
        me = groups.first_id(groups.core_id())
        own_ref[...] = summed[pl.ds(pl.multiple_of(me * piece, 8), piece), :]
        for k in range(1, group):
            part = summed[pl.ds(pl.multiple_of((me ^ k) * piece, 8), piece), :]
            outs[k - 1][...] = part.astype(BF)

    own_part, *to_group = call(
        split_kernel,
        [sds(piece, feat, F32)] + [sds(piece, feat, BF)] * (group - 1),
        [keep, got],
        scratch=[pltpu.VMEM((half, feat), F32)],
    )
    from_group = [groups.first_swap(part, k) for k, part in enumerate(to_group, 1)]

    def look_kernel(*refs):
        parts, (mine_ref, ring_ref, core_ref, halos) = refs[:helpers], refs[helpers:]
        at = pl.multiple_of(lax.axis_index("helper") * own, own)
        mine_ref[...] = tree_sum([g[pl.ds(at, own), :].astype(F32) for g in parts])
        halos[...] = tree_sum([g[band:, :].astype(F32) for g in parts])
        odd = lax.rem(lax.axis_index("band"), 2)
        ring_ref[...] = halos[pl.ds(pl.multiple_of(odd * halo, halo), halo), :].astype(BF)
        core_ref[...] = halos[pl.ds(pl.multiple_of((1 - odd) * halo, halo), halo), :].astype(BF)

    own_grad, ring_grad, core_grad = call(
        look_kernel,
        [sds(own, feat, F32), sds(halo, feat, BF), sds(halo, feat, BF)],
        looks,
        scratch=[pltpu.VMEM((2 * halo, feat), F32)],
    )
    ring_back = groups.ring_swap(ring_grad)
    core_back = groups.core_swap(core_grad)

    def join_kernel(own_ref, *refs):
        parts, piece_ref = refs[: group - 1], refs[group - 1]
        summed = own_ref[...]
        for part in parts:
            summed = summed + part[...].astype(F32)
        piece_ref[...] = summed.astype(BF)

    (piece_sum,) = call(join_kernel, [sds(piece, feat, BF)], [own_part, *from_group])

    halo_sums = None
    for stride, size in groups.far_rounds:
        swapped = [piece_sum] + [groups.second_swap(piece_sum, stride, k) for k in range(1, size)]
        first = halo_sums is None

        def far_kernel(*refs):
            parts, rest = refs[:size], refs[size:]
            rest[-1][...] = tree_sum([r[...].astype(F32) for r in parts]).astype(BF)
            if first:
                halo_ref, back_ref, forth_ref, out_ref, _ = rest
                at = lax.axis_index("helper") * own
                place = onehot_cols([halo_ref[...] - at], own)
                out_ref[...] = dot(place, back_ref[...]) + dot(place, forth_ref[...])

        if first:
            halo_sums, piece_sum = call(
                far_kernel,
                [sds(own, feat, F32), sds(piece, feat, BF)],
                swapped + [halo_list, ring_back, core_back],
            )
        else:
            (piece_sum,) = call(far_kernel, [sds(piece, feat, BF)], swapped)

    gathered = [piece_sum] + [groups.first_swap(piece_sum, k) for k in range(1, group)]
    vec = jax.ShapeDtypeStruct((feat,), F32)
    out_shape = [
        jax.ShapeDtypeStruct(edge_w1.shape, F32), vec, jax.ShapeDtypeStruct(edge_w2.shape, F32),
        vec, jax.ShapeDtypeStruct(node_w1.shape, F32), vec,
        jax.ShapeDtypeStruct(node_w2.shape, F32), vec,
    ]

    def place_pieces(parts, spots, outs, buf, row, sems):
        copies = []
        for i, (part, spot) in enumerate(zip(parts, spots)):
            buf[i * piece : (i + 1) * piece, :] = part[...].astype(F32)
            for j, (start, high, out) in enumerate(zip(starts, heights, outs[::2])):
                copies.append(
                    pltpu.make_async_copy(
                        buf.at[pl.ds(i * piece + start, high), :],
                        out.at[pl.ds(pl.multiple_of(spot * high, 8), high), :],
                        sems.at[i, j],
                    )
                )
                copies[-1].start()
        for i, spot in enumerate(spots):

            @pl.when(spot == 0)
            def _():
                for j, out in enumerate(outs[1::2]):
                    row[j][...] = buf[i * piece + at_bias + j, :]
                    pltpu.make_async_copy(row[j], out, sems.at[len(parts), j]).start()
                for j, out in enumerate(outs[1::2]):
                    pltpu.make_async_copy(row[j], out, sems.at[len(parts), j]).wait()

        for copy in copies:
            copy.wait()

    def place_call(keys, held, node=None):
        count = len(keys)
        parts = [sources[which, k] for which, k in keys]
        extra = [] if node is None else node

        def kernel(*refs):
            part_refs, refs = refs[:count], refs[count:]
            node_refs, refs = refs[: len(extra)], refs[len(extra) + len(held) :]
            if extra:
                node_out, *refs = refs
                halo_ref, mine_ref, din_ref, gon_ref = node_refs
                at = pl.multiple_of(lax.axis_index("helper") * own, own)
                node_out[...] = (
                    halo_ref[...] + mine_ref[...] + din_ref[pl.ds(at, own), :]
                    + gon_ref[...].astype(F32)
                )
            outs, (buf, *row, sems) = refs[:8], refs[8:]
            spots = []
            for which, k in keys:
                core = groups.core - 1 - groups.core_id() if which else groups.core_id()
                spots.append(core * group + (groups.first_id(core) ^ k))
            place_pieces(part_refs, spots, outs, buf, row, sems)

        vmem, hbm = pl.BlockSpec(memory_space=pltpu.VMEM), pl.BlockSpec(memory_space=pl.ANY)
        node_out = [sds(own, feat, F32)] if extra else []
        return pl.pallas_call(
            kernel,
            out_shape=node_out + out_shape,
            in_specs=[vmem] * (count + len(extra)) + [hbm] * len(held),
            out_specs=[vmem] * len(node_out) + [hbm] * 8,
            scratch_shapes=[pltpu.VMEM((count * piece, feat), F32)]
            + [pltpu.VMEM((feat,), F32)] * 4
            + [pltpu.SemaphoreType.DMA((count + 1, 4))],
            input_output_aliases={count + len(extra) + i: i for i in range(len(held))},
            compiler_params=pltpu.CompilerParams(vmem_limit_bytes=VMEM_LIMIT),
            cost_estimate=pl.CostEstimate(
                flops=0, bytes_accessed=6 * count * piece * feat, transcendentals=0
            ),
        )(*parts, *extra, *held)

    sources = {(0, k): part for k, part in enumerate(gathered)}
    sources[1, 0] = groups.core_swap(piece_sum)
    grad_node, *weight_grads = place_call(
        [(0, 0), (1, 0)], [], [halo_sums, own_grad, node_din, grad_out_node]
    )
    tops = range(group - 1, 0, -1)
    for i, k in enumerate(tops):
        if i < 2:
            sources[0, k], *weight_grads = lax.optimization_barrier(
                (sources[0, k], *weight_grads)
            )
        sources[1, k] = groups.core_swap(sources[0, k])
        if i == 0:
            weight_grads = place_call([(0, k)], weight_grads)
    third = [(0, k) for k in tops[1:]] + [(1, k) for k in tops[:1]]
    weight_grads = place_call(third, weight_grads)
    weight_grads = place_call([(1, k) for k in tops[1:]], weight_grads)
    return (grad_node, grad_edge, *weight_grads)


def solution(mesh):
    rows = P(AXES, None)
    flat = P(AXES)
    in_specs = (
        rows, rows, rows, rows, flat, flat, P(), P("band", None), flat,
        P(), P(), P(), P(), P(), P(), P(), P(),
    )
    out_specs = (rows, rows) + (P(),) * 8

    return jax.shard_map(
        on_device, mesh=mesh, in_specs=in_specs, out_specs=out_specs, check_vma=False
    )
```

```python
import math

import jax
import jax.numpy as jnp
from jax import lax
from jax.experimental import pallas as pl
from jax.experimental.pallas import tpu as pltpu
from jax.sharding import PartitionSpec as P


EB = 128
LANES = 128
WIDE = 8
NORM_EPS = 1e-05
BF = jnp.bfloat16
F32 = jnp.float32
AXES = ("band", "helper")
VMEM_LIMIT = 24 * 1024 * 1024


def round_up(size, unit):
    return -(-size // unit) * unit


def dot(left, right):
    return jnp.dot(left, right, preferred_element_type=F32)


def dot_left_t(left, right):
    return lax.dot_general(left, right, (((0,), (0,)), ((), ())), preferred_element_type=F32)


def dot_right_t(left, right):
    return lax.dot_general(left, right, (((1,), (1,)), ((), ())), preferred_element_type=F32)


def normalise(pre):
    centre = pre - jnp.mean(pre, axis=-1, keepdims=True)
    inv = lax.rsqrt(jnp.mean(centre * centre, axis=-1, keepdims=True) + NORM_EPS)
    return centre * inv, inv


def norm_back(grad, normed, inv):
    return inv * (
        grad
        - jnp.mean(grad, axis=-1, keepdims=True)
        - normed * jnp.mean(grad * normed, axis=-1, keepdims=True)
    )


def ids_down_rows(ids_row):
    return jnp.broadcast_to(ids_row, (LANES, LANES)).T


def onehot_rows(ids_cols, width):
    rows = ids_cols[0].shape[0]
    lane = lax.broadcasted_iota(jnp.int32, (rows, LANES), 1)
    tiles = []
    for start in range(0, width, LANES):
        hit = ids_cols[0] == lane + start
        for more in ids_cols[1:]:
            hit = hit | (more == lane + start)
        tiles.append(jnp.where(hit, 1.0, 0.0).astype(BF))
    return jnp.concatenate(tiles, axis=1)


def onehot_cols(ids_rows, height):
    count = ids_rows[0].shape[1]
    down = lax.broadcasted_iota(jnp.int32, (height, count), 0)
    hit = ids_rows[0] == down
    for more in ids_rows[1:]:
        hit = hit | (more == down)
    return jnp.where(hit, 1.0, 0.0).astype(BF)


def call(kernel, out_shape, args, scratch=(), hbm_out=(), flops=0):
    in_specs = [pl.BlockSpec(memory_space=pltpu.VMEM)] * len(args)
    out_specs = [
        pl.BlockSpec(memory_space=pl.ANY if i in hbm_out else pltpu.VMEM)
        for i in range(len(out_shape))
    ]
    nbytes = sum(a.size * a.dtype.itemsize for a in args)
    nbytes += sum(math.prod(o.shape) * o.dtype.itemsize for o in out_shape)
    return pl.pallas_call(
        kernel,
        out_shape=out_shape,
        in_specs=in_specs,
        out_specs=out_specs,
        scratch_shapes=list(scratch),
        compiler_params=pltpu.CompilerParams(vmem_limit_bytes=VMEM_LIMIT),
        cost_estimate=pl.CostEstimate(flops=flops, bytes_accessed=nbytes, transcendentals=0),
    )(*args)


def sds(rows, cols, dtype):
    return jax.ShapeDtypeStruct((rows, cols), dtype)


class Groups:
    def __init__(self, bands, helpers):
        self.bands = bands
        self.helpers = helpers
        self.core = 2 if bands % 2 == 0 else 1
        rest = bands // self.core
        self.near = 2 if (helpers <= 2 and rest % 2 == 0) else 1
        self.group = self.near * helpers
        far = rest // self.near
        self.far_rounds = []
        stride = self.core * self.near
        while far > 1:
            size = 4 if far % 4 == 0 else 2
            self.far_rounds.append((stride, size))
            stride *= size
            far //= size

        self.crossed = (
            self.core == 2 and len(self.far_rounds) == 1 and self.far_rounds[0][1] == self.group
        )

    def permute(self, array, move):
        pairs = []
        for band in range(self.bands):
            for helper in range(self.helpers):
                to_band, to_helper = move(band, helper)
                pairs.append((band * self.helpers + helper, to_band * self.helpers + to_helper))
        return lax.ppermute(array, AXES, pairs)

    def core_swap(self, array):
        return self.permute(array, lambda b, h: (b ^ 1, h))

    def helper_swap(self, array, k):
        return self.permute(array, lambda b, h: (b, h ^ k))

    def near_move(self, band, helper, k):
        near, help_k = divmod(k, self.helpers)
        return band ^ (near * self.core), helper ^ help_k

    def first_swap(self, array, k):
        def move(band, helper):
            if self.crossed and band % 2:
                return band ^ (k * self.far_rounds[0][0]), helper
            return self.near_move(band, helper, k)

        return self.permute(array, move)

    def second_swap(self, array, stride, k):
        def move(band, helper):
            if self.crossed and band % 2:
                return self.near_move(band, helper, k)
            return band ^ (k * stride), helper

        return self.permute(array, move)

    def ring_swap(self, array):
        return self.permute(
            array, lambda b, h: ((b + (1 if b % 2 else -1)) % self.bands, h)
        )

    def core_id(self):
        return lax.rem(lax.axis_index("band"), self.core)

    def first_id(self, core):
        band = lax.axis_index("band")
        near = lax.rem(lax.div(band, self.core), self.near)
        near = near * self.helpers + lax.axis_index("helper")
        if not self.crossed:
            return near
        return jnp.where(core == 1, lax.div(band, self.core * self.near), near)


def tree_sum(parts):
    parts = list(parts)
    while len(parts) > 1:
        parts = [parts[i] + parts[i + 1] for i in range(0, len(parts), 2)]
    return parts[0]


def on_device(
    node_latent,
    edge_latent,
    grad_out_node,
    grad_out_edge,
    senders,
    receivers,
    band_edges,
    halo_list,
    sea_mask,
    edge_w1,
    edge_b1,
    edge_w2,
    edge_b2,
    node_w1,
    node_b1,
    node_w2,
    node_b2,
):
    helpers = lax.axis_size("helper")
    bands = lax.axis_size("band")
    groups = Groups(bands, helpers)
    own, feat = node_latent.shape
    band = own * helpers
    halo = halo_list.shape[1]
    edges = edge_latent.shape[0]
    slots = edges // EB
    look = band + 2 * halo
    chunk = 2 * EB if slots % 2 == 0 else EB
    per_chunk = chunk // EB
    edge_scale = 1.0 / math.sqrt(edges * helpers * bands)
    node_share = 1.0 / math.sqrt(own * helpers * bands) / helpers
    unit = edges * feat * feat * 2

    send_ids = senders.reshape(slots, EB)
    recv_ids = receivers.reshape(slots, EB)

    group = groups.group
    pieces = groups.core * group
    slices = [edge_w1.shape[0] // pieces, edge_w2.shape[0] // pieces, 8]
    n_slices = [node_w1.shape[0] // pieces, node_w2.shape[0] // pieces]
    e_piece, n_piece = sum(slices), sum(n_slices)
    piece = e_piece + n_piece
    half = piece * group
    starts = [0, slices[0], e_piece, e_piece + n_slices[0]]
    heights = [slices[0], slices[1], n_slices[0], n_slices[1]]
    at_bias = slices[0] + slices[1]

    def chunk_ids(ref, index):
        return jnp.concatenate(
            [
                ids_down_rows(ref[pl.ds(index * per_chunk + j, 1), :])
                for j in range(per_chunk)
            ],
            axis=0,
        )

    def chunk_row(ref, index):
        return jnp.concatenate(
            [ref[pl.ds(index * per_chunk + j, 1), :] for j in range(per_chunk)], axis=1
        )

    b_width = round_up(2 * band, LANES)
    h_width = round_up(2 * halo, LANES)
    r_width = round_up(band, LANES)
    wide = WIDE * EB if slots % WIDE == 0 else EB

    def wide_live(ref, index):
        rows = [
            jnp.broadcast_to(ref[pl.ds(index * (wide // EB) + j, 1), :], (EB, feat))
            for j in range(wide // EB)
        ]
        return jnp.concatenate(rows, axis=0)

    theirs = [groups.helper_swap(node_latent, k) for k in range(1, helpers)]

    def gather_kernel(halo_ref, *refs):
        parts, (band_ref, out_ref) = refs[:helpers], refs[helpers:]
        me = lax.axis_index("helper")
        for k in range(helpers):
            at = pl.multiple_of((me ^ k) * own, own)
            band_ref[pl.ds(at, own), :] = parts[k][...]
        pick = onehot_cols([halo_ref[...]], band)
        out_ref[...] = dot_left_t(pick, band_ref[...]).astype(BF)

    band_rows, outgoing = call(
        gather_kernel, [sds(band, feat, BF), sds(halo, feat, BF)], [halo_list, node_latent, *theirs]
    )
    from_ring = groups.ring_swap(outgoing)
    from_core = groups.core_swap(outgoing)

    def split_store(table, height, at, proj):
        high = proj.astype(BF)
        table[at : at + proj.shape[0], :] = high
        table[height + at : height + at + proj.shape[0], :] = (proj - high.astype(F32)).astype(BF)

    def local_kernel(
        send_ref, recv_ref, band_ref, e_ref, w1_ref, b1_ref, b2_ref, nb1_ref, nb2_ref, be_ref,
        sea_ref, pre_ref, place_ref, recv_pick_ref, halo_pick_ref, et_ref, bias_ref, live_ref,
        sea_diag_ref, table,
    ):
        for i, ref in enumerate((b1_ref, b2_ref, nb1_ref, nb2_ref)):
            bias_ref[i, :] = ref[...]
        counts = be_ref[...][None, :]
        mine = lax.broadcasted_iota(jnp.int32, counts.shape, 1) == lax.axis_index("band")
        count = jnp.sum(jnp.where(mine, counts, 0), axis=1, keepdims=True)
        slot = lax.broadcasted_iota(jnp.int32, (slots, feat), 0)
        live_ref[...] = jnp.where(
            slot * helpers + lax.axis_index("helper") < count, 1.0, 0.0
        )
        down = lax.broadcasted_iota(jnp.int32, (own, own), 0)
        across = lax.broadcasted_iota(jnp.int32, (own, own), 1)
        sea_diag_ref[...] = jnp.where(
            (down == across) & (sea_ref[...][None, :] != 0), 1.0, 0.0
        ).astype(BF)
        if b_width > 2 * band:
            table[...] = jnp.zeros_like(table)
        for at, rows in ((0, slice(0, feat)), (band, slice(feat, 2 * feat))):
            split_store(table, b_width, at, dot(band_ref[...], w1_ref[rows, :]))
        for i in range(edges // chunk):
            rows = pl.ds(i * chunk, chunk)
            send_cols = chunk_ids(send_ref, i)
            recv_cols = chunk_ids(recv_ref, i)
            halo_pick_ref[rows, :] = onehot_rows([send_cols - band], h_width)
            recv_pick_ref[rows, :] = onehot_rows([recv_cols], r_width)
            place_ref[:, rows] = onehot_cols(
                [chunk_row(send_ref, i), chunk_row(recv_ref, i) + look], look + band
            )
            send_cols = jnp.where(send_cols < band, send_cols, -1)
            pick = onehot_rows([send_cols, recv_cols + band], b_width)
            pre = dot(jnp.concatenate([pick, pick], axis=1), table[...])
            e_rows = e_ref[rows, :]
            pre_ref[rows, :] = pre + dot(e_rows, w1_ref[2 * feat :, :]) + b1_ref[...][None, :]
            et_ref[:, rows] = e_rows.T

    pre_local, place, recv_pick, halo_pick, edge_t, biases, live, sea_diag = call(
        local_kernel,
        [
            sds(edges, feat, F32), sds(look + band, edges, BF), sds(edges, r_width, BF),
            sds(edges, h_width, BF), sds(feat, edges, BF), sds(4, feat, F32),
            sds(slots, feat, F32), sds(own, own, BF),
        ],
        [send_ids, recv_ids, band_rows, edge_latent, edge_w1, edge_b1, edge_b2, node_b1, node_b2,
         band_edges, sea_mask],
        scratch=[pltpu.VMEM((2 * b_width, feat), BF)],
        flops=4 * unit,
    )

    def forward_kernel(
        live_ref, pre_ref, place_ref, halo_pick_ref, ring_ref, core_ref, w1_ref, w2_ref, bias_ref,
        gon_ref, sea_ref, hid_ref, slope_ref, norm_ref, inv_ref, agg, swap_ref, halo_ref,
        table,
    ):
        if h_width > 2 * halo:
            table[...] = jnp.zeros_like(table)
        odd = lax.rem(lax.axis_index("band"), 2)
        halo_ref[pl.ds(pl.multiple_of(odd * halo, halo), halo), :] = ring_ref[...]
        halo_ref[pl.ds(pl.multiple_of((1 - odd) * halo, halo), halo), :] = core_ref[...]
        split_store(table, h_width, 0, dot(halo_ref[...], w1_ref[...]))
        for i in range(edges // wide):
            rows = pl.ds(i * wide, wide)
            pick = halo_pick_ref[rows, :]
            pre = pre_ref[rows, :] + dot(jnp.concatenate([pick, pick], axis=1), table[...])
            sig = jax.nn.sigmoid(pre)
            hidden = (pre * sig).astype(BF)
            hid_ref[rows, :] = hidden
            slope_ref[rows, :] = sig * (1.0 + pre * (1.0 - sig))
            normed, inv = normalise(dot(hidden, w2_ref[...]) + bias_ref[1:2, :])
            norm_ref[rows, :] = normed
            inv_ref[rows, :] = inv
            message = (normed * wide_live(live_ref, i)).astype(BF)
            part = dot(place_ref[look:, rows], message)
            if i == 0:
                agg[...] = part
            else:
                agg[...] += part
        swap_ref[:band, :] = agg[...].astype(BF)
        swap_ref[band:, :] = dot(sea_ref[...], gon_ref[...]).astype(BF)

    hidden, slope, normed, inv, agg_own, swap_own, halo_rows = call(
        forward_kernel,
        [sds(edges, feat, BF), sds(edges, feat, F32), sds(edges, feat, F32), sds(edges, 1, F32),
         sds(band, feat, F32), sds(band + own, feat, BF), sds(2 * halo, feat, BF)],
        [live, pre_local, place, halo_pick, from_ring, from_core, edge_w1[:feat], edge_w2,
         biases, grad_out_node, sea_diag],
        scratch=[pltpu.VMEM((2 * h_width, feat), BF)],
        flops=3 * unit,
    )

    swaps = [swap_own] + [groups.helper_swap(swap_own, k) for k in range(1, helpers)]

    def backward_kernel(
        live_ref, place_ref, recv_pick_ref, band_ref, halo_ref, et_ref, geo_ref,
        hid_ref, slope_ref, norm_ref, inv_ref, w1_ref, w2_ref, nw1_ref, nw2_ref, bias_ref,
        agg_ref, *refs,
    ):
        parts = refs[:helpers]
        edge_hbm, keep_ref, give_ref, lg_ref, din_ref, grads, sums, seed, edge_ref, sems = refs[helpers:]
        edge_copies = []
        band_v = band_ref[...]
        me = lax.axis_index("helper")
        for k in range(helpers):
            seed[pl.ds(pl.multiple_of((me ^ k) * own, own), own), :] = parts[k][band:, :]
        agg = tree_sum([agg_ref[...]] + [p[:band, :].astype(F32) for p in parts[1:]]).astype(BF)
        node_in = jnp.concatenate([band_v, agg], axis=1)
        n_pre = dot(node_in, nw1_ref[...]) + bias_ref[2:3, :]
        n_sig = jax.nn.sigmoid(n_pre)
        n_hidden = (n_pre * n_sig).astype(BF)
        n_normed, n_inv = normalise(dot(n_hidden, nw2_ref[...]) + bias_ref[3:4, :])
        n_dz = norm_back(seed[...].astype(F32), n_normed, n_inv)
        n_dzb = n_dz.astype(BF)
        n_dpre = dot_right_t(n_dzb, nw2_ref[...]) * (n_sig * (1.0 + n_pre * (1.0 - n_sig)))
        n_dpreb = n_dpre.astype(BF)
        din_ref[...] = dot_right_t(n_dpreb, nw1_ref[:feat, :])
        agg_grad = dot_right_t(n_dpreb, nw1_ref[feat:, :]).astype(BF)

        def put(which, first, value):
            high, row, count = heights[which], 0, value.shape[0]
            while row < count:
                spot, within = divmod(first + row, high)
                take = min(high - within, count - row)
                at = spot * piece + starts[which] + within
                grads[at : at + take, :] = value[row : row + take, :]
                row += take

        put(2, 0, dot_left_t(node_in, n_dpreb) * node_share)
        put(3, 0, dot_left_t(n_hidden, n_dzb) * node_share)
        gb_n1 = jnp.sum(n_dpre, axis=0, keepdims=True) * node_share
        gb_n2 = jnp.sum(n_dz, axis=0, keepdims=True) * node_share

        w1e = w1_ref[2 * feat :, :]
        gb_1 = jnp.zeros((1, feat), F32)
        gb_2 = jnp.zeros((1, feat), F32)
        gw_1 = jnp.zeros((feat, feat), F32)
        gw_2 = jnp.zeros((feat, feat), F32)
        for i in range(edges // wide):
            rows = pl.ds(i * wide, wide)
            live = wide_live(live_ref, i)
            geo = geo_ref[rows, :].astype(F32)
            at_recv = dot(recv_pick_ref[rows, :band], agg_grad)
            msg_grad = (geo + at_recv) * live
            dz = norm_back(msg_grad, norm_ref[rows, :], inv_ref[rows, :])
            gb_2 = gb_2 + jnp.sum(dz, axis=0, keepdims=True)
            dzb = dz.astype(BF)
            gw_2 = gw_2 + dot_left_t(hid_ref[rows, :], dzb)
            dpre = dot_right_t(dzb, w2_ref[...]) * slope_ref[rows, :]
            gb_1 = gb_1 + jnp.sum(dpre, axis=0, keepdims=True)
            dpreb = dpre.astype(BF)
            gw_1 = gw_1 + dot(et_ref[:, rows], dpreb)
            edge_ref[rows, :] = ((geo + dot_right_t(dpreb, w1e)) * live).astype(BF)
            edge_copies.append(
                pltpu.make_async_copy(edge_ref.at[rows, :], edge_hbm.at[rows, :], sems.at[i])
            )
            edge_copies[-1].start()
            part = dot(place_ref[:, rows], dpreb)
            if i == 0:
                sums[...] = part
            else:
                sums[...] += part
        at_send = sums[:look, :].astype(BF)
        at_recv = sums[look:, :].astype(BF)
        lookup = jnp.concatenate([band_v, halo_ref[...]], axis=0)
        look_grad = dot_right_t(at_send, w1_ref[:feat, :])
        recv_grad = dot_right_t(at_recv, w1_ref[feat : 2 * feat, :])
        lg_ref[:band, :] = (look_grad[:band, :] + recv_grad).astype(BF)
        lg_ref[band:, :] = look_grad[band:, :].astype(BF)
        put(0, 0, dot_left_t(lookup, at_send) * edge_scale)
        put(0, feat, dot_left_t(band_v, at_recv) * edge_scale)
        put(0, 2 * feat, gw_1 * edge_scale)
        put(1, 0, gw_2 * edge_scale)
        bias = [gb_1 * edge_scale, gb_2 * edge_scale, gb_n1, gb_n2]
        grads[at_bias : at_bias + 8, :] = jnp.concatenate(bias + [jnp.zeros((4, feat), F32)], axis=0)
        for p in range(1, pieces):
            grads[p * piece + at_bias : p * piece + at_bias + 8, :] = jnp.zeros((8, feat), F32)
        core = groups.core_id()
        other = groups.core - 1 - core
        keep_ref[...] = grads[pl.ds(pl.multiple_of(core * half, 8), half), :]
        give_ref[...] = grads[pl.ds(pl.multiple_of(other * half, 8), half), :].astype(BF)
        for copy in edge_copies:
            copy.wait()

    grad_edge, keep, give, look_grad, node_din = call(
        backward_kernel,
        [sds(edges, feat, BF), sds(half, feat, F32), sds(half, feat, BF), sds(look, feat, BF),
         sds(band, feat, F32)],
        [live, place, recv_pick, band_rows, halo_rows, edge_t, grad_out_edge,
         hidden, slope, normed, inv, edge_w1, edge_w2, node_w1, node_w2, biases, agg_own, *swaps],
        scratch=[pltpu.VMEM((half * groups.core, feat), F32), pltpu.VMEM((look + band, feat), F32),
                 pltpu.VMEM((band, feat), BF), pltpu.VMEM((edges, feat), BF),
                 pltpu.SemaphoreType.DMA((edges // wide,))],
        hbm_out=(0,),
        flops=8 * unit,
    )

    got = groups.core_swap(give)
    looks = [look_grad] + [groups.helper_swap(look_grad, k) for k in range(1, helpers)]

    def split_kernel(keep_ref, got_ref, own_ref, *refs):
        outs, summed = refs[:-1], refs[-1]
        summed[...] = keep_ref[...] + got_ref[...].astype(F32)
        me = groups.first_id(groups.core_id())
        own_ref[...] = summed[pl.ds(pl.multiple_of(me * piece, 8), piece), :]
        for k in range(1, group):
            part = summed[pl.ds(pl.multiple_of((me ^ k) * piece, 8), piece), :]
            outs[k - 1][...] = part.astype(BF)

    own_part, *to_group = call(
        split_kernel,
        [sds(piece, feat, F32)] + [sds(piece, feat, BF)] * (group - 1),
        [keep, got],
        scratch=[pltpu.VMEM((half, feat), F32)],
    )
    from_group = [groups.first_swap(part, k) for k, part in enumerate(to_group, 1)]

    def look_kernel(*refs):
        parts, (mine_ref, ring_ref, core_ref, halos) = refs[:helpers], refs[helpers:]
        at = pl.multiple_of(lax.axis_index("helper") * own, own)
        mine_ref[...] = tree_sum([g[pl.ds(at, own), :].astype(F32) for g in parts])
        halos[...] = tree_sum([g[band:, :].astype(F32) for g in parts])
        odd = lax.rem(lax.axis_index("band"), 2)
        ring_ref[...] = halos[pl.ds(pl.multiple_of(odd * halo, halo), halo), :].astype(BF)
        core_ref[...] = halos[pl.ds(pl.multiple_of((1 - odd) * halo, halo), halo), :].astype(BF)

    own_grad, ring_grad, core_grad = call(
        look_kernel,
        [sds(own, feat, F32), sds(halo, feat, BF), sds(halo, feat, BF)],
        looks,
        scratch=[pltpu.VMEM((2 * halo, feat), F32)],
    )
    ring_back = groups.ring_swap(ring_grad)
    core_back = groups.core_swap(core_grad)

    def join_kernel(own_ref, *refs):
        parts, piece_ref = refs[: group - 1], refs[group - 1]
        summed = own_ref[...]
        for part in parts:
            summed = summed + part[...].astype(F32)
        piece_ref[...] = summed.astype(BF)

    (piece_sum,) = call(join_kernel, [sds(piece, feat, BF)], [own_part, *from_group])

    halo_sums = None
    for stride, size in groups.far_rounds:
        swapped = [piece_sum] + [groups.second_swap(piece_sum, stride, k) for k in range(1, size)]
        first = halo_sums is None

        def far_kernel(*refs):
            parts, rest = refs[:size], refs[size:]
            rest[-1][...] = tree_sum([r[...].astype(F32) for r in parts]).astype(BF)
            if first:
                halo_ref, back_ref, forth_ref, out_ref, _ = rest
                at = lax.axis_index("helper") * own
                place = onehot_cols([halo_ref[...] - at], own)
                out_ref[...] = dot(place, back_ref[...]) + dot(place, forth_ref[...])

        if first:
            halo_sums, piece_sum = call(
                far_kernel,
                [sds(own, feat, F32), sds(piece, feat, BF)],
                swapped + [halo_list, ring_back, core_back],
            )
        else:
            (piece_sum,) = call(far_kernel, [sds(piece, feat, BF)], swapped)

    gathered = [piece_sum] + [groups.first_swap(piece_sum, k) for k in range(1, group)]
    vec = jax.ShapeDtypeStruct((feat,), F32)
    out_shape = [
        jax.ShapeDtypeStruct(edge_w1.shape, F32), vec, jax.ShapeDtypeStruct(edge_w2.shape, F32),
        vec, jax.ShapeDtypeStruct(node_w1.shape, F32), vec,
        jax.ShapeDtypeStruct(node_w2.shape, F32), vec,
    ]

    def place_pieces(parts, spots, outs, buf, row, sems):
        copies = []
        for i, (part, spot) in enumerate(zip(parts, spots)):
            buf[i * piece : (i + 1) * piece, :] = part[...].astype(F32)
            for j, (start, high, out) in enumerate(zip(starts, heights, outs[::2])):
                copies.append(
                    pltpu.make_async_copy(
                        buf.at[pl.ds(i * piece + start, high), :],
                        out.at[pl.ds(pl.multiple_of(spot * high, 8), high), :],
                        sems.at[i, j],
                    )
                )
                copies[-1].start()
        for i, spot in enumerate(spots):

            @pl.when(spot == 0)
            def _():
                for j, out in enumerate(outs[1::2]):
                    row[j][...] = buf[i * piece + at_bias + j, :]
                    pltpu.make_async_copy(row[j], out, sems.at[len(parts), j]).start()
                for j, out in enumerate(outs[1::2]):
                    pltpu.make_async_copy(row[j], out, sems.at[len(parts), j]).wait()

        for copy in copies:
            copy.wait()

    def place_call(keys, held, node=None):
        count = len(keys)
        parts = [sources[which, k] for which, k in keys]
        extra = [] if node is None else node

        def kernel(*refs):
            part_refs, refs = refs[:count], refs[count:]
            node_refs, refs = refs[: len(extra)], refs[len(extra) + len(held) :]
            if extra:
                node_out, *refs = refs
                halo_ref, mine_ref, din_ref, gon_ref = node_refs
                at = pl.multiple_of(lax.axis_index("helper") * own, own)
                node_out[...] = (
                    halo_ref[...] + mine_ref[...] + din_ref[pl.ds(at, own), :]
                    + gon_ref[...].astype(F32)
                )
            outs, (buf, *row, sems) = refs[:8], refs[8:]
            spots = []
            for which, k in keys:
                core = groups.core - 1 - groups.core_id() if which else groups.core_id()
                spots.append(core * group + (groups.first_id(core) ^ k))
            place_pieces(part_refs, spots, outs, buf, row, sems)

        vmem, hbm = pl.BlockSpec(memory_space=pltpu.VMEM), pl.BlockSpec(memory_space=pl.ANY)
        node_out = [sds(own, feat, F32)] if extra else []
        return pl.pallas_call(
            kernel,
            out_shape=node_out + out_shape,
            in_specs=[vmem] * (count + len(extra)) + [hbm] * len(held),
            out_specs=[vmem] * len(node_out) + [hbm] * 8,
            scratch_shapes=[pltpu.VMEM((count * piece, feat), F32)]
            + [pltpu.VMEM((feat,), F32)] * 4
            + [pltpu.SemaphoreType.DMA((count + 1, 4))],
            input_output_aliases={count + len(extra) + i: i for i in range(len(held))},
            compiler_params=pltpu.CompilerParams(vmem_limit_bytes=VMEM_LIMIT),
            cost_estimate=pl.CostEstimate(
                flops=0, bytes_accessed=6 * count * piece * feat, transcendentals=0
            ),
        )(*parts, *extra, *held)

    sources = {(0, k): part for k, part in enumerate(gathered)}
    sources[1, 0] = groups.core_swap(piece_sum)
    grad_node, *weight_grads = place_call(
        [(0, 0), (1, 0)], [], [halo_sums, own_grad, node_din, grad_out_node]
    )
    tops = range(group - 1, 0, -1)
    for i, k in enumerate(tops):
        if i < 2:
            sources[0, k], *weight_grads = lax.optimization_barrier(
                (sources[0, k], *weight_grads)
            )
        sources[1, k] = groups.core_swap(sources[0, k])
        if i == 0:
            weight_grads = place_call([(0, k)], weight_grads)
    third = [(0, k) for k in tops[1:]] + [(1, k) for k in tops[:1]]
    weight_grads = place_call(third, weight_grads)
    weight_grads = place_call([(1, k) for k in tops[1:]], weight_grads)
    return (grad_node, grad_edge, *weight_grads)


def solution(mesh):
    rows = P(AXES, None)
    flat = P(AXES)
    in_specs = (
        rows, rows, rows, rows, flat, flat, P(), P("band", None), flat,
        P(), P(), P(), P(), P(), P(), P(), P(),
    )
    out_specs = (rows, rows) + (P(),) * 8

    return jax.shard_map(
        on_device, mesh=mesh, in_specs=in_specs, out_specs=out_specs, check_vma=False
    )
```

```python
import math

import jax
import jax.numpy as jnp
from jax import lax
from jax.experimental import pallas as pl
from jax.experimental.pallas import tpu as pltpu
from jax.sharding import PartitionSpec as P


EB = 128
LANES = 128
WIDE = 8
NORM_EPS = 1e-05
BF = jnp.bfloat16
F32 = jnp.float32
AXES = ("band", "helper")
VMEM_LIMIT = 24 * 1024 * 1024


def round_up(size, unit):
    return -(-size // unit) * unit


def dot(left, right):
    return jnp.dot(left, right, preferred_element_type=F32)


def dot_left_t(left, right):
    return lax.dot_general(left, right, (((0,), (0,)), ((), ())), preferred_element_type=F32)


def dot_right_t(left, right):
    return lax.dot_general(left, right, (((1,), (1,)), ((), ())), preferred_element_type=F32)


def normalise(pre):
    centre = pre - jnp.mean(pre, axis=-1, keepdims=True)
    inv = lax.rsqrt(jnp.mean(centre * centre, axis=-1, keepdims=True) + NORM_EPS)
    return centre * inv, inv


def norm_back(grad, normed, inv):
    return inv * (
        grad
        - jnp.mean(grad, axis=-1, keepdims=True)
        - normed * jnp.mean(grad * normed, axis=-1, keepdims=True)
    )


def ids_down_rows(ids_row):
    return jnp.broadcast_to(ids_row, (LANES, LANES)).T


def onehot_rows(ids_cols, width):
    rows = ids_cols[0].shape[0]
    lane = lax.broadcasted_iota(jnp.int32, (rows, LANES), 1)
    tiles = []
    for start in range(0, width, LANES):
        hit = ids_cols[0] == lane + start
        for more in ids_cols[1:]:
            hit = hit | (more == lane + start)
        tiles.append(jnp.where(hit, 1.0, 0.0).astype(BF))
    return jnp.concatenate(tiles, axis=1)


def onehot_cols(ids_rows, height):
    count = ids_rows[0].shape[1]
    down = lax.broadcasted_iota(jnp.int32, (height, count), 0)
    hit = ids_rows[0] == down
    for more in ids_rows[1:]:
        hit = hit | (more == down)
    return jnp.where(hit, 1.0, 0.0).astype(BF)


def call(kernel, out_shape, args, scratch=(), hbm_out=(), flops=0):
    in_specs = [pl.BlockSpec(memory_space=pltpu.VMEM)] * len(args)
    out_specs = [
        pl.BlockSpec(memory_space=pl.ANY if i in hbm_out else pltpu.VMEM)
        for i in range(len(out_shape))
    ]
    nbytes = sum(a.size * a.dtype.itemsize for a in args)
    nbytes += sum(math.prod(o.shape) * o.dtype.itemsize for o in out_shape)
    return pl.pallas_call(
        kernel,
        out_shape=out_shape,
        in_specs=in_specs,
        out_specs=out_specs,
        scratch_shapes=list(scratch),
        compiler_params=pltpu.CompilerParams(vmem_limit_bytes=VMEM_LIMIT),
        cost_estimate=pl.CostEstimate(flops=flops, bytes_accessed=nbytes, transcendentals=0),
    )(*args)


def sds(rows, cols, dtype):
    return jax.ShapeDtypeStruct((rows, cols), dtype)


class Groups:
    def __init__(self, bands, helpers):
        self.bands = bands
        self.helpers = helpers
        self.core = 2 if bands % 2 == 0 else 1
        rest = bands // self.core
        self.near = 2 if (helpers <= 2 and rest % 2 == 0) else 1
        self.group = self.near * helpers
        far = rest // self.near
        self.far_rounds = []
        stride = self.core * self.near
        while far > 1:
            size = 4 if far % 4 == 0 else 2
            self.far_rounds.append((stride, size))
            stride *= size
            far //= size

        self.crossed = (
            self.core == 2 and len(self.far_rounds) == 1 and self.far_rounds[0][1] == self.group
        )

    def permute(self, array, move):
        pairs = []
        for band in range(self.bands):
            for helper in range(self.helpers):
                to_band, to_helper = move(band, helper)
                pairs.append((band * self.helpers + helper, to_band * self.helpers + to_helper))
        return lax.ppermute(array, AXES, pairs)

    def core_swap(self, array):
        return self.permute(array, lambda b, h: (b ^ 1, h))

    def helper_swap(self, array, k):
        return self.permute(array, lambda b, h: (b, h ^ k))

    def near_move(self, band, helper, k):
        near, help_k = divmod(k, self.helpers)
        return band ^ (near * self.core), helper ^ help_k

    def first_swap(self, array, k):
        def move(band, helper):
            if self.crossed and band % 2:
                return band ^ (k * self.far_rounds[0][0]), helper
            return self.near_move(band, helper, k)

        return self.permute(array, move)

    def second_swap(self, array, stride, k):
        def move(band, helper):
            if self.crossed and band % 2:
                return self.near_move(band, helper, k)
            return band ^ (k * stride), helper

        return self.permute(array, move)

    def ring_swap(self, array):
        return self.permute(
            array, lambda b, h: ((b + (1 if b % 2 else -1)) % self.bands, h)
        )

    def core_id(self):
        return lax.rem(lax.axis_index("band"), self.core)

    def first_id(self, core):
        band = lax.axis_index("band")
        near = lax.rem(lax.div(band, self.core), self.near)
        near = near * self.helpers + lax.axis_index("helper")
        if not self.crossed:
            return near
        return jnp.where(core == 1, lax.div(band, self.core * self.near), near)


def tree_sum(parts):
    parts = list(parts)
    while len(parts) > 1:
        parts = [parts[i] + parts[i + 1] for i in range(0, len(parts), 2)]
    return parts[0]


def on_device(
    node_latent,
    edge_latent,
    grad_out_node,
    grad_out_edge,
    senders,
    receivers,
    band_edges,
    halo_list,
    sea_mask,
    edge_w1,
    edge_b1,
    edge_w2,
    edge_b2,
    node_w1,
    node_b1,
    node_w2,
    node_b2,
):
    helpers = lax.axis_size("helper")
    bands = lax.axis_size("band")
    groups = Groups(bands, helpers)
    own, feat = node_latent.shape
    band = own * helpers
    halo = halo_list.shape[1]
    edges = edge_latent.shape[0]
    slots = edges // EB
    look = band + 2 * halo
    chunk = 2 * EB if slots % 2 == 0 else EB
    per_chunk = chunk // EB
    edge_scale = 1.0 / math.sqrt(edges * helpers * bands)
    node_share = 1.0 / math.sqrt(own * helpers * bands) / helpers
    unit = edges * feat * feat * 2

    send_ids = senders.reshape(slots, EB)
    recv_ids = receivers.reshape(slots, EB)

    group = groups.group
    pieces = groups.core * group
    slices = [edge_w1.shape[0] // pieces, edge_w2.shape[0] // pieces, 8]
    n_slices = [node_w1.shape[0] // pieces, node_w2.shape[0] // pieces]
    e_piece, n_piece = sum(slices), sum(n_slices)
    piece = e_piece + n_piece
    half = piece * group
    starts = [0, slices[0], e_piece, e_piece + n_slices[0]]
    heights = [slices[0], slices[1], n_slices[0], n_slices[1]]
    at_bias = slices[0] + slices[1]

    def chunk_ids(ref, index):
        return jnp.concatenate(
            [
                ids_down_rows(ref[pl.ds(index * per_chunk + j, 1), :])
                for j in range(per_chunk)
            ],
            axis=0,
        )

    def chunk_row(ref, index):
        return jnp.concatenate(
            [ref[pl.ds(index * per_chunk + j, 1), :] for j in range(per_chunk)], axis=1
        )

    b_width = round_up(2 * band, LANES)
    h_width = round_up(2 * halo, LANES)
    r_width = round_up(band, LANES)
    wide = WIDE * EB if slots % WIDE == 0 else EB

    def wide_live(ref, index):
        rows = [
            jnp.broadcast_to(ref[pl.ds(index * (wide // EB) + j, 1), :], (EB, feat))
            for j in range(wide // EB)
        ]
        return jnp.concatenate(rows, axis=0)

    theirs = [groups.helper_swap(node_latent, k) for k in range(1, helpers)]
    w1_send, w1_rest = edge_w1[:feat], edge_w1[feat:]

    def gather_kernel(halo_ref, *refs):
        parts, (band_ref, out_ref) = refs[:helpers], refs[helpers:]
        me = lax.axis_index("helper")
        for k in range(helpers):
            at = pl.multiple_of((me ^ k) * own, own)
            band_ref[pl.ds(at, own), :] = parts[k][...]
        pick = onehot_cols([halo_ref[...]], band)
        out_ref[...] = dot_left_t(pick, band_ref[...]).astype(BF)

    band_rows, outgoing = call(
        gather_kernel, [sds(band, feat, BF), sds(halo, feat, BF)], [halo_list, node_latent, *theirs]
    )
    from_ring = groups.ring_swap(outgoing)
    from_core = groups.core_swap(outgoing)

    def split_store(table, height, at, proj):
        high = proj.astype(BF)
        table[at : at + proj.shape[0], :] = high
        table[height + at : height + at + proj.shape[0], :] = (proj - high.astype(F32)).astype(BF)

    def local_kernel(
        send_ref, recv_ref, band_ref, e_ref, ws_ref, wr_ref, b1_ref, b2_ref, nb1_ref, nb2_ref,
        be_ref, sea_ref, pre_ref, place_ref, recv_pick_ref, halo_pick_ref, et_ref, bias_ref, live_ref,
        sea_diag_ref, table,
    ):
        for i, ref in enumerate((b1_ref, b2_ref, nb1_ref, nb2_ref)):
            bias_ref[i, :] = ref[...]
        counts = be_ref[...][None, :]
        mine = lax.broadcasted_iota(jnp.int32, counts.shape, 1) == lax.axis_index("band")
        count = jnp.sum(jnp.where(mine, counts, 0), axis=1, keepdims=True)
        slot = lax.broadcasted_iota(jnp.int32, (slots, feat), 0)
        live_ref[...] = jnp.where(
            slot * helpers + lax.axis_index("helper") < count, 1.0, 0.0
        )
        down = lax.broadcasted_iota(jnp.int32, (own, own), 0)
        across = lax.broadcasted_iota(jnp.int32, (own, own), 1)
        sea_diag_ref[...] = jnp.where(
            (down == across) & (sea_ref[...][None, :] != 0), 1.0, 0.0
        ).astype(BF)
        if b_width > 2 * band:
            table[...] = jnp.zeros_like(table)
        for at, weights in ((0, ws_ref[...]), (band, wr_ref[:feat, :])):
            split_store(table, b_width, at, dot(band_ref[...], weights))
        for i in range(edges // chunk):
            rows = pl.ds(i * chunk, chunk)
            send_cols = chunk_ids(send_ref, i)
            recv_cols = chunk_ids(recv_ref, i)
            halo_pick_ref[rows, :] = onehot_rows([send_cols - band], h_width)
            recv_pick_ref[rows, :] = onehot_rows([recv_cols], r_width)
            place_ref[:, rows] = onehot_cols(
                [chunk_row(send_ref, i), chunk_row(recv_ref, i) + look], look + band
            )
            send_cols = jnp.where(send_cols < band, send_cols, -1)
            pick = onehot_rows([send_cols, recv_cols + band], b_width)
            pre = dot(jnp.concatenate([pick, pick], axis=1), table[...])
            e_rows = e_ref[rows, :]
            pre_ref[rows, :] = pre + dot(e_rows, wr_ref[feat:, :]) + b1_ref[...][None, :]
            et_ref[:, rows] = e_rows.T

    pre_local, place, recv_pick, halo_pick, edge_t, biases, live, sea_diag = call(
        local_kernel,
        [
            sds(edges, feat, F32), sds(look + band, edges, BF), sds(edges, r_width, BF),
            sds(edges, h_width, BF), sds(feat, edges, BF), sds(4, feat, F32),
            sds(slots, feat, F32), sds(own, own, BF),
        ],
        [send_ids, recv_ids, band_rows, edge_latent, w1_send, w1_rest, edge_b1, edge_b2, node_b1, node_b2,
         band_edges, sea_mask],
        scratch=[pltpu.VMEM((2 * b_width, feat), BF)],
        flops=4 * unit,
    )

    def forward_kernel(
        live_ref, pre_ref, place_ref, halo_pick_ref, ring_ref, core_ref, w1_ref, w2_ref, bias_ref,
        gon_ref, sea_ref, hid_ref, slope_ref, norm_ref, inv_ref, agg, swap_ref, halo_ref,
        table,
    ):
        if h_width > 2 * halo:
            table[...] = jnp.zeros_like(table)
        odd = lax.rem(lax.axis_index("band"), 2)
        halo_ref[pl.ds(pl.multiple_of(odd * halo, halo), halo), :] = ring_ref[...]
        halo_ref[pl.ds(pl.multiple_of((1 - odd) * halo, halo), halo), :] = core_ref[...]
        split_store(table, h_width, 0, dot(halo_ref[...], w1_ref[...]))
        for i in range(edges // wide):
            rows = pl.ds(i * wide, wide)
            pick = halo_pick_ref[rows, :]
            pre = pre_ref[rows, :] + dot(jnp.concatenate([pick, pick], axis=1), table[...])
            sig = jax.nn.sigmoid(pre)
            hidden = (pre * sig).astype(BF)
            hid_ref[rows, :] = hidden
            slope_ref[rows, :] = sig * (1.0 + pre * (1.0 - sig))
            normed, inv = normalise(dot(hidden, w2_ref[...]) + bias_ref[1:2, :])
            norm_ref[rows, :] = normed
            inv_ref[rows, :] = inv
            message = (normed * wide_live(live_ref, i)).astype(BF)
            part = dot(place_ref[look:, rows], message)
            if i == 0:
                agg[...] = part
            else:
                agg[...] += part
        swap_ref[:band, :] = agg[...].astype(BF)
        swap_ref[band:, :] = dot(sea_ref[...], gon_ref[...]).astype(BF)

    hidden, slope, normed, inv, agg_own, swap_own, halo_rows = call(
        forward_kernel,
        [sds(edges, feat, BF), sds(edges, feat, F32), sds(edges, feat, F32), sds(edges, 1, F32),
         sds(band, feat, F32), sds(band + own, feat, BF), sds(2 * halo, feat, BF)],
        [live, pre_local, place, halo_pick, from_ring, from_core, w1_send, edge_w2,
         biases, grad_out_node, sea_diag],
        scratch=[pltpu.VMEM((2 * h_width, feat), BF)],
        flops=3 * unit,
    )

    swaps = [swap_own] + [groups.helper_swap(swap_own, k) for k in range(1, helpers)]

    def backward_kernel(
        live_ref, place_ref, recv_pick_ref, band_ref, halo_ref, et_ref, geo_ref,
        hid_ref, slope_ref, norm_ref, inv_ref, ws_ref, wr_ref, w2_ref, nw1_ref, nw2_ref, bias_ref,
        agg_ref, *refs,
    ):
        parts = refs[:helpers]
        edge_hbm, keep_ref, give_ref, lg_ref, din_ref, grads, sums, seed, edge_ref, sems = refs[helpers:]
        edge_copies = []
        band_v = band_ref[...]
        me = lax.axis_index("helper")
        for k in range(helpers):
            seed[pl.ds(pl.multiple_of((me ^ k) * own, own), own), :] = parts[k][band:, :]
        agg = tree_sum([agg_ref[...]] + [p[:band, :].astype(F32) for p in parts[1:]]).astype(BF)
        node_in = jnp.concatenate([band_v, agg], axis=1)
        n_pre = dot(node_in, nw1_ref[...]) + bias_ref[2:3, :]
        n_sig = jax.nn.sigmoid(n_pre)
        n_hidden = (n_pre * n_sig).astype(BF)
        n_normed, n_inv = normalise(dot(n_hidden, nw2_ref[...]) + bias_ref[3:4, :])
        n_dz = norm_back(seed[...].astype(F32), n_normed, n_inv)
        n_dzb = n_dz.astype(BF)
        n_dpre = dot_right_t(n_dzb, nw2_ref[...]) * (n_sig * (1.0 + n_pre * (1.0 - n_sig)))
        n_dpreb = n_dpre.astype(BF)
        din_ref[...] = dot_right_t(n_dpreb, nw1_ref[:feat, :])
        agg_grad = dot_right_t(n_dpreb, nw1_ref[feat:, :]).astype(BF)

        def put(which, first, value):
            high, row, count = heights[which], 0, value.shape[0]
            while row < count:
                spot, within = divmod(first + row, high)
                take = min(high - within, count - row)
                at = spot * piece + starts[which] + within
                grads[at : at + take, :] = value[row : row + take, :]
                row += take

        put(2, 0, dot_left_t(node_in, n_dpreb) * node_share)
        put(3, 0, dot_left_t(n_hidden, n_dzb) * node_share)
        gb_n1 = jnp.sum(n_dpre, axis=0, keepdims=True) * node_share
        gb_n2 = jnp.sum(n_dz, axis=0, keepdims=True) * node_share

        w1e = wr_ref[feat:, :]
        gb_1 = jnp.zeros((1, feat), F32)
        gb_2 = jnp.zeros((1, feat), F32)
        gw_1 = jnp.zeros((feat, feat), F32)
        gw_2 = jnp.zeros((feat, feat), F32)
        for i in range(edges // wide):
            rows = pl.ds(i * wide, wide)
            live = wide_live(live_ref, i)
            geo = geo_ref[rows, :].astype(F32)
            at_recv = dot(recv_pick_ref[rows, :band], agg_grad)
            msg_grad = (geo + at_recv) * live
            dz = norm_back(msg_grad, norm_ref[rows, :], inv_ref[rows, :])
            gb_2 = gb_2 + jnp.sum(dz, axis=0, keepdims=True)
            dzb = dz.astype(BF)
            gw_2 = gw_2 + dot_left_t(hid_ref[rows, :], dzb)
            dpre = dot_right_t(dzb, w2_ref[...]) * slope_ref[rows, :]
            gb_1 = gb_1 + jnp.sum(dpre, axis=0, keepdims=True)
            dpreb = dpre.astype(BF)
            gw_1 = gw_1 + dot(et_ref[:, rows], dpreb)
            edge_ref[rows, :] = ((geo + dot_right_t(dpreb, w1e)) * live).astype(BF)
            edge_copies.append(
                pltpu.make_async_copy(edge_ref.at[rows, :], edge_hbm.at[rows, :], sems.at[i])
            )
            edge_copies[-1].start()
            part = dot(place_ref[:, rows], dpreb)
            if i == 0:
                sums[...] = part
            else:
                sums[...] += part
        at_send = sums[:look, :].astype(BF)
        at_recv = sums[look:, :].astype(BF)
        lookup = jnp.concatenate([band_v, halo_ref[...]], axis=0)
        look_grad = dot_right_t(at_send, ws_ref[...])
        recv_grad = dot_right_t(at_recv, wr_ref[:feat, :])
        lg_ref[:band, :] = (look_grad[:band, :] + recv_grad).astype(BF)
        lg_ref[band:, :] = look_grad[band:, :].astype(BF)
        put(0, 0, dot_left_t(lookup, at_send) * edge_scale)
        put(0, feat, dot_left_t(band_v, at_recv) * edge_scale)
        put(0, 2 * feat, gw_1 * edge_scale)
        put(1, 0, gw_2 * edge_scale)
        bias = [gb_1 * edge_scale, gb_2 * edge_scale, gb_n1, gb_n2]
        grads[at_bias : at_bias + 8, :] = jnp.concatenate(bias + [jnp.zeros((4, feat), F32)], axis=0)
        for p in range(1, pieces):
            grads[p * piece + at_bias : p * piece + at_bias + 8, :] = jnp.zeros((8, feat), F32)
        core = groups.core_id()
        other = groups.core - 1 - core
        keep_ref[...] = grads[pl.ds(pl.multiple_of(core * half, 8), half), :]
        give_ref[...] = grads[pl.ds(pl.multiple_of(other * half, 8), half), :].astype(BF)
        for copy in edge_copies:
            copy.wait()

    grad_edge, keep, give, look_grad, node_din = call(
        backward_kernel,
        [sds(edges, feat, BF), sds(half, feat, F32), sds(half, feat, BF), sds(look, feat, BF),
         sds(band, feat, F32)],
        [live, place, recv_pick, band_rows, halo_rows, edge_t, grad_out_edge,
         hidden, slope, normed, inv, w1_send, w1_rest, edge_w2, node_w1, node_w2, biases, agg_own, *swaps],
        scratch=[pltpu.VMEM((half * groups.core, feat), F32), pltpu.VMEM((look + band, feat), F32),
                 pltpu.VMEM((band, feat), BF), pltpu.VMEM((edges, feat), BF),
                 pltpu.SemaphoreType.DMA((edges // wide,))],
        hbm_out=(0,),
        flops=8 * unit,
    )

    got = groups.core_swap(give)
    looks = [look_grad] + [groups.helper_swap(look_grad, k) for k in range(1, helpers)]

    def split_kernel(keep_ref, got_ref, own_ref, *refs):
        outs, summed = refs[:-1], refs[-1]
        summed[...] = keep_ref[...] + got_ref[...].astype(F32)
        me = groups.first_id(groups.core_id())
        own_ref[...] = summed[pl.ds(pl.multiple_of(me * piece, 8), piece), :]
        for k in range(1, group):
            part = summed[pl.ds(pl.multiple_of((me ^ k) * piece, 8), piece), :]
            outs[k - 1][...] = part.astype(BF)

    own_part, *to_group = call(
        split_kernel,
        [sds(piece, feat, F32)] + [sds(piece, feat, BF)] * (group - 1),
        [keep, got],
        scratch=[pltpu.VMEM((half, feat), F32)],
    )
    from_group = [groups.first_swap(part, k) for k, part in enumerate(to_group, 1)]

    def look_kernel(*refs):
        parts, (mine_ref, ring_ref, core_ref, halos) = refs[:helpers], refs[helpers:]
        at = pl.multiple_of(lax.axis_index("helper") * own, own)
        mine_ref[...] = tree_sum([g[pl.ds(at, own), :].astype(F32) for g in parts])
        halos[...] = tree_sum([g[band:, :].astype(F32) for g in parts])
        odd = lax.rem(lax.axis_index("band"), 2)
        ring_ref[...] = halos[pl.ds(pl.multiple_of(odd * halo, halo), halo), :].astype(BF)
        core_ref[...] = halos[pl.ds(pl.multiple_of((1 - odd) * halo, halo), halo), :].astype(BF)

    own_grad, ring_grad, core_grad = call(
        look_kernel,
        [sds(own, feat, F32), sds(halo, feat, BF), sds(halo, feat, BF)],
        looks,
        scratch=[pltpu.VMEM((2 * halo, feat), F32)],
    )
    ring_back = groups.ring_swap(ring_grad)
    core_back = groups.core_swap(core_grad)

    def join_kernel(own_ref, *refs):
        parts, piece_ref = refs[: group - 1], refs[group - 1]
        summed = own_ref[...]
        for part in parts:
            summed = summed + part[...].astype(F32)
        piece_ref[...] = summed.astype(BF)

    (piece_sum,) = call(join_kernel, [sds(piece, feat, BF)], [own_part, *from_group])

    halo_sums = None
    for stride, size in groups.far_rounds:
        swapped = [piece_sum] + [groups.second_swap(piece_sum, stride, k) for k in range(1, size)]
        first = halo_sums is None

        def far_kernel(*refs):
            parts, rest = refs[:size], refs[size:]
            rest[-1][...] = tree_sum([r[...].astype(F32) for r in parts]).astype(BF)
            if first:
                halo_ref, back_ref, forth_ref, out_ref, _ = rest
                at = lax.axis_index("helper") * own
                place = onehot_cols([halo_ref[...] - at], own)
                out_ref[...] = dot(place, back_ref[...]) + dot(place, forth_ref[...])

        if first:
            halo_sums, piece_sum = call(
                far_kernel,
                [sds(own, feat, F32), sds(piece, feat, BF)],
                swapped + [halo_list, ring_back, core_back],
            )
        else:
            (piece_sum,) = call(far_kernel, [sds(piece, feat, BF)], swapped)

    gathered = [piece_sum] + [groups.first_swap(piece_sum, k) for k in range(1, group)]
    vec = jax.ShapeDtypeStruct((feat,), F32)
    out_shape = [
        jax.ShapeDtypeStruct(edge_w1.shape, F32), vec, jax.ShapeDtypeStruct(edge_w2.shape, F32),
        vec, jax.ShapeDtypeStruct(node_w1.shape, F32), vec,
        jax.ShapeDtypeStruct(node_w2.shape, F32), vec,
    ]

    def place_pieces(parts, spots, outs, buf, row, sems):
        copies = []
        for i, (part, spot) in enumerate(zip(parts, spots)):
            buf[i * piece : (i + 1) * piece, :] = part[...].astype(F32)
            for j, (start, high, out) in enumerate(zip(starts, heights, outs[::2])):
                copies.append(
                    pltpu.make_async_copy(
                        buf.at[pl.ds(i * piece + start, high), :],
                        out.at[pl.ds(pl.multiple_of(spot * high, 8), high), :],
                        sems.at[i, j],
                    )
                )
                copies[-1].start()
        for i, spot in enumerate(spots):

            @pl.when(spot == 0)
            def _():
                for j, out in enumerate(outs[1::2]):
                    row[j][...] = buf[i * piece + at_bias + j, :]
                    pltpu.make_async_copy(row[j], out, sems.at[len(parts), j]).start()
                for j, out in enumerate(outs[1::2]):
                    pltpu.make_async_copy(row[j], out, sems.at[len(parts), j]).wait()

        for copy in copies:
            copy.wait()

    def place_call(keys, held, node=None):
        count = len(keys)
        parts = [sources[which, k] for which, k in keys]
        extra = [] if node is None else node

        def kernel(*refs):
            part_refs, refs = refs[:count], refs[count:]
            node_refs, refs = refs[: len(extra)], refs[len(extra) + len(held) :]
            if extra:
                node_out, *refs = refs
                halo_ref, mine_ref, din_ref, gon_ref = node_refs
                at = pl.multiple_of(lax.axis_index("helper") * own, own)
                node_out[...] = (
                    halo_ref[...] + mine_ref[...] + din_ref[pl.ds(at, own), :]
                    + gon_ref[...].astype(F32)
                )
            outs, (buf, *row, sems) = refs[:8], refs[8:]
            spots = []
            for which, k in keys:
                core = groups.core - 1 - groups.core_id() if which else groups.core_id()
                spots.append(core * group + (groups.first_id(core) ^ k))
            place_pieces(part_refs, spots, outs, buf, row, sems)

        vmem, hbm = pl.BlockSpec(memory_space=pltpu.VMEM), pl.BlockSpec(memory_space=pl.ANY)
        node_out = [sds(own, feat, F32)] if extra else []
        return pl.pallas_call(
            kernel,
            out_shape=node_out + out_shape,
            in_specs=[vmem] * (count + len(extra)) + [hbm] * len(held),
            out_specs=[vmem] * len(node_out) + [hbm] * 8,
            scratch_shapes=[pltpu.VMEM((count * piece, feat), F32)]
            + [pltpu.VMEM((feat,), F32)] * 4
            + [pltpu.SemaphoreType.DMA((count + 1, 4))],
            input_output_aliases={count + len(extra) + i: i for i in range(len(held))},
            compiler_params=pltpu.CompilerParams(vmem_limit_bytes=VMEM_LIMIT),
            cost_estimate=pl.CostEstimate(
                flops=0, bytes_accessed=6 * count * piece * feat, transcendentals=0
            ),
        )(*parts, *extra, *held)

    sources = {(0, k): part for k, part in enumerate(gathered)}
    sources[1, 0] = groups.core_swap(piece_sum)
    grad_node, *weight_grads = place_call(
        [(0, 0), (1, 0)], [], [halo_sums, own_grad, node_din, grad_out_node]
    )
    tops = range(group - 1, 0, -1)
    for i, k in enumerate(tops):
        if i < 2:
            sources[0, k], *weight_grads = lax.optimization_barrier(
                (sources[0, k], *weight_grads)
            )
        sources[1, k] = groups.core_swap(sources[0, k])
        if i == 0:
            weight_grads = place_call([(0, k)], weight_grads)
    third = [(0, k) for k in tops[1:]] + [(1, k) for k in tops[:1]]
    weight_grads = place_call(third, weight_grads)
    weight_grads = place_call([(1, k) for k in tops[1:]], weight_grads)
    return (grad_node, grad_edge, *weight_grads)


def solution(mesh):
    rows = P(AXES, None)
    flat = P(AXES)
    in_specs = (
        rows, rows, rows, rows, flat, flat, P(), P("band", None), flat,
        P(), P(), P(), P(), P(), P(), P(), P(),
    )
    out_specs = (rows, rows) + (P(),) * 8

    return jax.shard_map(
        on_device, mesh=mesh, in_specs=in_specs, out_specs=out_specs, check_vma=False
    )
```
